32 devices in a mesh: grp: 8 (over z, core), seq: 4 (over y, x).
Axes of the slice: x: 2, y: 2, z: 4, core: 2. Of those that a mesh axis runs over, the one named last changes fastest.
Arguments:
- tokens: bfloat16 [4096, 1024], P(('grp', 'seq')), may hold values from -6 to 6
- cotangent: bfloat16 [4096, 1024], P(('grp', 'seq')), may hold values from -6 to 6
- slot_lengths: int32 [16], P('grp'), may hold values from 64 to 256, as said below
- w_qkv: bfloat16 [1024, 3072], P(('grp', 'seq')), may hold values from -0.1875 to 0.1875
- qv_bias: bfloat16 [2048], P(('grp', 'seq')), may hold values from -3 to 3
- w_out: bfloat16 [1024, 1024], P(('grp', 'seq')), may hold values from -1.5 to 1.5
- out_bias: bfloat16 [1024], P(('grp', 'seq')), may hold values from -3 to 3
- ln1_gain: bfloat16 [1024], P(('grp', 'seq')), may hold values from 0.099609375 to 1.8984375
- ln1_bias: bfloat16 [1024], P(('grp', 'seq')), may hold values from -3 to 3
- w_in: bfloat16 [1024, 4096], P(('grp', 'seq')), may hold values from -0.1875 to 0.1875
- in_bias: bfloat16 [4096], P(('grp', 'seq')), may hold values from -3 to 3
- w_back: bfloat16 [4096, 1024], P(('grp', 'seq')), may hold values from -0.09375 to 0.09375
- back_bias: bfloat16 [1024], P(('grp', 'seq')), may hold values from -3 to 3
- ln2_gain: bfloat16 [1024], P(('grp', 'seq')), may hold values from 0.099609375 to 1.8984375
- ln2_bias: bfloat16 [1024], P(('grp', 'seq')), may hold values from -3 to 3
Outputs:
- output: bfloat16 [4096, 1024], P(('grp', 'seq'))
- grad_tokens: float32 [4096, 1024], P(('grp', 'seq'))
- grad_w_qkv: float32 [1024, 3072], P(('grp', 'seq'))
- grad_qv_bias: float32 [2048], P(('grp', 'seq'))
- grad_w_out: float32 [1024, 1024], P(('grp', 'seq'))
- grad_out_bias: float32 [1024], P(('grp', 'seq'))
- grad_ln1_gain: float32 [1024], P(('grp', 'seq'))
- grad_ln1_bias: float32 [1024], P(('grp', 'seq'))
- grad_w_in: float32 [1024, 4096], P(('grp', 'seq'))
- grad_in_bias: float32 [4096], P(('grp', 'seq'))
- grad_w_back: float32 [4096, 1024], P(('grp', 'seq'))
- grad_back_bias: float32 [1024], P(('grp', 'seq'))
- grad_ln2_gain: float32 [1024], P(('grp', 'seq'))
- grad_ln2_bias: float32 [1024], P(('grp', 'seq'))
The draws below stay inside these ranges and needn't reach their ends.
Inputs may be any that keep to these rules, and one draw needn't show every extreme that they name: `slot_lengths`: valid tokens of each slot; in every draw some slot holds 256 valid tokens.
All inputs are finite; a program needn't handle non-finite values.
Results may differ from the reference program's by a relative error of at most 0.013.
Values may be sent and summed in bfloat16 or wider, within the bound.
A program may use at most 192 MiB of HBM per device.

```python
import math
import jax
import jax.numpy as jnp
from jax import lax

D = 1024
H = 16
HD = 64
FF = 4096
SLOT = 256
SLOTS_ALL = 16
TOKENS = 4096


def draw_slot_lengths(key, part):
    length_key, place_key = jax.random.split(key)
    lengths = jax.random.randint(length_key, (SLOTS_ALL,), SLOT // 4, SLOT + 1)
    chosen = jax.random.randint(place_key, (), 0, SLOTS_ALL)
    return jnp.where(jnp.arange(SLOTS_ALL) == chosen, SLOT, lengths).astype(jnp.int32)


def shard_levels(key, shape, cuts, least, largest):
    loudness = 1.0
    for position, blocks in cuts:
        steps = jax.random.uniform(jax.random.fold_in(jax.random.fold_in(key, 6), position), (blocks,), jnp.float32, least / len(cuts), largest / len(cuts))
        loudness = loudness * jnp.repeat(jnp.exp(steps), shape[position] // blocks).reshape((-1,) + (1,) * (len(shape) - 1 - position))
    return loudness


def centred(key, extent, scale, reach, cuts=(), dtype=jnp.bfloat16):
    loudness = shard_levels(key, extent, cuts, -0.22, 0.18) if cuts else 1.0
    values = jax.random.normal(key, extent, jnp.float32) * scale * loudness
    return jnp.minimum(jnp.maximum(values, -reach), reach).astype(dtype)


def setup_inputs(seed: int = 0) -> dict:
    arg_keys = jax.random.split(jax.random.key(seed), 16)
    return {
        "tokens": centred(arg_keys[0], (TOKENS, D), 1.0, 6.0, ((0, 32),)),
        "cotangent": centred(arg_keys[1], (TOKENS, D), 1.0, 6.0, ((0, 32),)),
        "slot_lengths": draw_slot_lengths(jax.random.fold_in(arg_keys[15], 71), 0),
        "w_qkv": centred(arg_keys[3], (D, 3 * D), D ** -0.5, 0.1875, ((0, 32),)),
        "qv_bias": centred(arg_keys[4], (2 * D,), 0.5, 3.0, ((0, 32),)),
        "w_out": centred(arg_keys[5], (D, D), (4 * D // SLOT) ** -0.5, 1.5, ((0, 32),)),
        "out_bias": centred(arg_keys[6], (D,), 0.5, 3.0, ((0, 32),)),
        "ln1_gain": jnp.clip(1.0 + 0.18 * jax.random.normal(arg_keys[7], (D,), jnp.float32), 0.099609375, 1.8984375).astype(jnp.bfloat16),
        "ln1_bias": centred(arg_keys[8], (D,), 0.5, 3.0, ((0, 32),)),
        "w_in": centred(arg_keys[9], (D, FF), D ** -0.5, 0.1875, ((0, 32),)),
        "in_bias": centred(arg_keys[10], (FF,), 0.5, 3.0, ((0, 32),)),
        "w_back": centred(arg_keys[11], (FF, D), FF ** -0.5, 0.09375, ((0, 32),)),
        "back_bias": centred(arg_keys[12], (D,), 0.5, 3.0, ((0, 32),)),
        "ln2_gain": jnp.clip(1.0 + 0.18 * jax.random.normal(arg_keys[13], (D,), jnp.float32), 0.099609375, 1.8984375).astype(jnp.bfloat16),
        "ln2_bias": centred(arg_keys[14], (D,), 0.5, 3.0, ((0, 32),)),
    }


NORM_EPS = 1e-06
PRECISE = lax.Precision.HIGHEST

@jax.custom_vjp
def low(v):
    return lax.optimization_barrier(v.astype(jnp.bfloat16)).astype(jnp.float32)

@jax.custom_vjp
def low_back(v):
    return v

def low_keep(v):
    return (low(v), None)

def low_pass(kept, grad):
    return (grad,)

def back_keep(v):
    return (v, None)

def back_low(kept, grad):
    return (low(grad),)
low.defvjp(low_keep, low_pass)
low_back.defvjp(back_keep, back_low)

def layer_norm(hidden, gain, shift):
    center = hidden - lax.optimization_barrier(jnp.mean(hidden, axis=-1, keepdims=True))
    spread = lax.optimization_barrier(jnp.mean(center * center, axis=-1, keepdims=True))
    return center * lax.rsqrt(spread + NORM_EPS) * gain + shift

def full_bias(pair_bias):
    pairs = pair_bias.reshape(H, 2, HD)
    return jnp.stack([pairs[:, 0], jnp.zeros_like(pairs[:, 0]), pairs[:, 1]], axis=1).reshape(3 * D)

def block_forward(params, rows, lengths):
    w_qkv, qv_bias, w_out, out_bias, ln1_gain, ln1_bias, w_in, in_bias, w_back, back_bias, ln2_gain, ln2_bias = params
    count = lengths.shape[0]
    factor = 1.0 / math.sqrt(HD)
    mixed = low(low_back(jnp.dot(rows, w_qkv, precision=PRECISE) + full_bias(qv_bias)))
    mixed = mixed.reshape(count, SLOT, H, 3, HD)
    queries = mixed[:, :, :, 0]
    key_rows = mixed[:, :, :, 1]
    value_rows = mixed[:, :, :, 2]
    scores = low_back(jnp.einsum('sqhd,skhd->shqk', queries, key_rows, precision=PRECISE)) * factor
    key_valid = jnp.arange(SLOT)[None, :] < lengths[:, None]
    scores = jnp.where(key_valid[:, None, None, :], scores, -1e+30)
    row_max = lax.optimization_barrier(jnp.max(scores, axis=-1, keepdims=True))
    expon = jnp.exp(scores - row_max)
    probs = expon / lax.optimization_barrier(jnp.sum(expon, axis=-1, keepdims=True))
    context = low(low_back(jnp.einsum('shqk,skhd->sqhd', low(probs), value_rows, precision=PRECISE)))
    context = context.reshape(count * SLOT, D)
    attended = low_back(jnp.dot(context, w_out, precision=PRECISE)) + out_bias
    normed = layer_norm(rows + attended, ln1_gain, ln1_bias)
    pre_act = low_back(jnp.dot(low(normed), w_in, precision=PRECISE)) + in_bias
    activated = low(jax.nn.gelu(pre_act, approximate=False))
    ffn_out = low_back(jnp.dot(activated, w_back, precision=PRECISE)) + back_bias
    return layer_norm(normed + ffn_out, ln2_gain, ln2_bias)

def reference(tokens, cotangent, slot_lengths, w_qkv, qv_bias, w_out, out_bias, ln1_gain, ln1_bias, w_in, in_bias, w_back, back_bias, ln2_gain, ln2_bias):
    params = tuple((item.astype(jnp.float32) for item in (w_qkv, qv_bias, w_out, out_bias, ln1_gain, ln1_bias, w_in, in_bias, w_back, back_bias, ln2_gain, ln2_bias)))
    per_block = math.gcd(SLOTS_ALL, max(1, 2048 // SLOT))
    blocks = SLOTS_ALL // per_block
    rows = tokens.astype(jnp.float32).reshape(blocks, per_block * SLOT, D)
    lengths = slot_lengths.reshape(blocks, per_block)

    def whole(params, rows):
        step_fn = jax.checkpoint(block_forward)

        def advance(carry, item):
            return (carry, step_fn(params, item[0], item[1]))
        final_carry, result = lax.scan(advance, jnp.zeros((), jnp.float32), (rows, lengths))
        return result
    result, pullback = jax.vjp(whole, params, rows)
    valid = (jnp.arange(SLOT)[None, :] < slot_lengths[:, None]).reshape(blocks, per_block * SLOT, 1)
    seed_grad = cotangent.astype(jnp.float32).reshape(rows.shape) * valid.astype(jnp.float32)
    grad_params, grad_rows = pullback(seed_grad)
    return (result.reshape(TOKENS, D).astype(jnp.bfloat16), grad_rows.reshape(TOKENS, D), grad_params[0], grad_params[1], grad_params[2], grad_params[3], grad_params[4], grad_params[5], grad_params[6], grad_params[7], grad_params[8], grad_params[9], grad_params[10], grad_params[11])
```

```python
from functools import partial
import math

import jax
import jax.numpy as jnp
from jax import lax
from jax.experimental import pallas as pl
from jax.experimental.pallas import tpu as pltpu
from jax.sharding import PartitionSpec as P

D = 1024
H = 16
HD = 64
SLOT_DEV = 64
SLOTS = 2


NORM_EPS = 1e-06


def layer_norm(hidden, gain, shift):
    center = hidden - jnp.mean(hidden, axis=-1, keepdims=True)
    spread = jnp.mean(center * center, axis=-1, keepdims=True)
    return center * lax.rsqrt(spread + NORM_EPS) * gain + shift


def exact_gelu(values):
    return jax.nn.gelu(values, approximate=False)


def full_bias(pair_bias):
    pairs = pair_bias.reshape(H, 2, HD)
    return jnp.stack([pairs[:, 0], jnp.zeros_like(pairs[:, 0]), pairs[:, 1]], axis=1).reshape(3 * D)


def contract_rows(left, right):
    return lax.dot_general(
        left, right, (((0,), (0,)), ((), ())), preferred_element_type=jnp.float32
    )


def contract_cols(left, right):
    return lax.dot_general(
        left, right, (((1,), (1,)), ((), ())), preferred_element_type=jnp.float32
    )


def slot_scores(mixed, length, factor):
    slot_width = mixed.shape[0]
    queries = mixed[:, :, 0]
    key_rows = mixed[:, :, 1]
    value_rows = mixed[:, :, 2]
    products = jnp.einsum("qhd,khd->hqk", queries, key_rows, preferred_element_type=jnp.float32)
    key_valid = (jnp.arange(slot_width) < length)[None, None, :]
    scores = jnp.where(key_valid, products * factor, -1e30)
    return (queries, key_rows, value_rows, scores)


def slot_forward(item, factor):
    mixed, length = item
    queries, key_rows, value_rows, scores = slot_scores(mixed, length, factor)
    row_max = jnp.max(scores, axis=-1, keepdims=True)
    expon = jnp.exp(scores - row_max)
    total = jnp.sum(expon, axis=-1, keepdims=True)
    probs = expon / total
    context = jnp.einsum(
        "hqk,khd->qhd", probs.astype(jnp.bfloat16), value_rows, preferred_element_type=jnp.float32
    )
    return (context.astype(jnp.bfloat16), row_max + jnp.log(total))


def slot_backward(item, factor):
    mixed, grad_context, log_total, length = item
    queries, key_rows, value_rows, scores = slot_scores(mixed, length, factor)
    probs = jnp.exp(scores - log_total)
    grad_probs = jnp.einsum(
        "qhd,khd->hqk", grad_context, value_rows, preferred_element_type=jnp.float32
    )
    inner = jnp.sum(probs * grad_probs, axis=-1, keepdims=True)
    grad_scores = (probs * (grad_probs - inner) * factor).astype(jnp.bfloat16)
    grad_queries = jnp.einsum(
        "hqk,khd->qhd", grad_scores, key_rows, preferred_element_type=jnp.float32
    )
    grad_keys = jnp.einsum("hqk,qhd->khd", grad_scores, queries, preferred_element_type=jnp.float32)
    grad_values = jnp.einsum(
        "hqk,qhd->khd", probs.astype(jnp.bfloat16), grad_context, preferred_element_type=jnp.float32
    )
    return jnp.stack([grad_queries, grad_keys, grad_values], axis=2).astype(jnp.bfloat16)


def shards(
    tokens,
    cotangent,
    slot_lengths,
    w_qkv,
    qv_bias,
    w_out,
    out_bias,
    ln1_gain,
    ln1_bias,
    w_in,
    in_bias,
    w_back,
    back_bias,
    ln2_gain,
    ln2_bias,
):
    seq_count = lax.axis_size("seq")
    local_rows = tokens.shape[0]
    slot_width = SLOT_DEV * seq_count
    heads_here = H // seq_count
    factor = 1.0 / math.sqrt(HD)
    full_qkv, full_qv, full_out, full_obias, gain_one, shift_one = (
        lax.all_gather(w_qkv, ("grp", "seq"), axis=0, tiled=True),
        lax.all_gather(qv_bias, ("grp", "seq"), axis=0, tiled=True),
        lax.all_gather(w_out, ("grp", "seq"), axis=0, tiled=True),
        lax.all_gather(out_bias, ("grp", "seq"), axis=0, tiled=True),
        lax.all_gather(ln1_gain, ("grp", "seq"), axis=0, tiled=True),
        lax.all_gather(ln1_bias, ("grp", "seq"), axis=0, tiled=True),
    )
    full_in, full_ibias, full_back, full_bbias, gain_two, shift_two = (
        lax.all_gather(w_in, ("grp", "seq"), axis=0, tiled=True),
        lax.all_gather(in_bias, ("grp", "seq"), axis=0, tiled=True),
        lax.all_gather(w_back, ("grp", "seq"), axis=0, tiled=True),
        lax.all_gather(back_bias, ("grp", "seq"), axis=0, tiled=True),
        lax.all_gather(ln2_gain, ("grp", "seq"), axis=0, tiled=True),
        lax.all_gather(ln2_bias, ("grp", "seq"), axis=0, tiled=True),
    )
    mixed = (
        jnp.dot(tokens, full_qkv, preferred_element_type=jnp.float32) + full_bias(full_qv)
    ).astype(jnp.bfloat16)
    gathered = lax.all_to_all(mixed, "seq", split_axis=1, concat_axis=0, tiled=True)
    per_slot = gathered.reshape(SLOTS, slot_width, heads_here, 3, HD)
    contexts, log_totals = lax.map(partial(slot_forward, factor=factor), (per_slot, slot_lengths))
    context_heads = contexts.reshape(SLOTS * slot_width, heads_here * HD)
    context = lax.all_to_all(context_heads, "seq", split_axis=0, concat_axis=1, tiled=True)
    attended = jnp.dot(context, full_out, preferred_element_type=jnp.float32) + full_obias
    first_in = tokens.astype(jnp.float32) + attended
    normed, norm_one_pull = jax.vjp(layer_norm, first_in, gain_one, shift_one)
    normed_low = normed.astype(jnp.bfloat16)
    pre_act = jnp.dot(normed_low, full_in, preferred_element_type=jnp.float32) + full_ibias
    activated, gelu_pull = jax.vjp(exact_gelu, pre_act)
    act_low = activated.astype(jnp.bfloat16)
    ffn_out = jnp.dot(act_low, full_back, preferred_element_type=jnp.float32) + full_bbias
    output, norm_two_pull = jax.vjp(layer_norm, normed + ffn_out, gain_two, shift_two)
    row_index = lax.axis_index("seq") * local_rows + jnp.arange(local_rows)
    slot_index = row_index // slot_width
    place = row_index % slot_width
    row_length = jnp.sum(
        jnp.where(slot_index[:, None] == jnp.arange(SLOTS)[None, :], slot_lengths[None, :], 0),
        axis=1,
    )
    row_valid = (place < row_length).astype(jnp.float32)
    seed_grad = cotangent.astype(jnp.float32) * row_valid[:, None]
    grad_second, grad_gain_two, grad_shift_two = norm_two_pull(seed_grad)
    grad_ffn_low = grad_second.astype(jnp.bfloat16)
    grad_back_w = contract_rows(act_low, grad_ffn_low)
    grad_back_b = jnp.sum(grad_second, axis=0)
    (grad_pre,) = gelu_pull(contract_cols(grad_ffn_low, full_back))
    grad_pre_low = grad_pre.astype(jnp.bfloat16)
    grad_in_w = contract_rows(normed_low, grad_pre_low)
    grad_in_b = jnp.sum(grad_pre, axis=0)
    grad_normed = grad_second + contract_cols(grad_pre_low, full_in)
    grad_first, grad_gain_one, grad_shift_one = norm_one_pull(grad_normed)
    grad_attn_low = grad_first.astype(jnp.bfloat16)
    grad_out_w = contract_rows(context, grad_attn_low)
    grad_out_b = jnp.sum(grad_first, axis=0)
    grad_context = contract_cols(grad_attn_low, full_out).astype(jnp.bfloat16)
    grad_heads = lax.all_to_all(grad_context, "seq", split_axis=1, concat_axis=0, tiled=True)
    grad_slots = grad_heads.reshape(SLOTS, slot_width, heads_here, HD)
    grad_mixed_heads = lax.map(
        partial(slot_backward, factor=factor), (per_slot, grad_slots, log_totals, slot_lengths)
    )
    grad_mixed = lax.all_to_all(
        grad_mixed_heads.reshape(SLOTS * slot_width, heads_here * 3 * HD),
        "seq",
        split_axis=0,
        concat_axis=1,
        tiled=True,
    )
    grad_qkv_w = contract_rows(tokens, grad_mixed)
    summed_bias = jnp.sum(grad_mixed.astype(jnp.float32), axis=0).reshape(H, 3, HD)
    grad_qv = jnp.stack([summed_bias[:, 0], summed_bias[:, 2]], axis=1).reshape(2 * D)
    input_grad = grad_first + contract_cols(grad_mixed, full_qkv)
    sums = (
        lax.psum_scatter(grad_qkv_w, ("grp", "seq"), scatter_dimension=0, tiled=True),
        lax.psum_scatter(grad_qv, ("grp", "seq"), scatter_dimension=0, tiled=True),
        lax.psum_scatter(grad_out_w, ("grp", "seq"), scatter_dimension=0, tiled=True),
        lax.psum_scatter(grad_out_b, ("grp", "seq"), scatter_dimension=0, tiled=True),
        lax.psum_scatter(
            grad_gain_one.astype(jnp.float32), ("grp", "seq"), scatter_dimension=0, tiled=True
        ),
        lax.psum_scatter(
            grad_shift_one.astype(jnp.float32), ("grp", "seq"), scatter_dimension=0, tiled=True
        ),
        lax.psum_scatter(grad_in_w, ("grp", "seq"), scatter_dimension=0, tiled=True),
        lax.psum_scatter(grad_in_b, ("grp", "seq"), scatter_dimension=0, tiled=True),
        lax.psum_scatter(grad_back_w, ("grp", "seq"), scatter_dimension=0, tiled=True),
        lax.psum_scatter(grad_back_b, ("grp", "seq"), scatter_dimension=0, tiled=True),
        lax.psum_scatter(
            grad_gain_two.astype(jnp.float32), ("grp", "seq"), scatter_dimension=0, tiled=True
        ),
        lax.psum_scatter(
            grad_shift_two.astype(jnp.float32), ("grp", "seq"), scatter_dimension=0, tiled=True
        ),
    )
    return (
        output.astype(jnp.bfloat16),
        input_grad,
        sums[0],
        sums[1],
        sums[2],
        sums[3],
        sums[4],
        sums[5],
        sums[6],
        sums[7],
        sums[8],
        sums[9],
        sums[10],
        sums[11],
    )


BF = jnp.bfloat16
F32 = jnp.float32
MESH = pl.DeviceIdType.MESH
PLANES = 4
RANKS = 4
(T_PACK, T_WQ, T_WI, T_TOK, T_WO, T_CTX, T_N, T_RSF, T_G, T_RSB, T_GC, T_GO, T_GT, T_GI, T_GQ, T_SV) = range(16)
(A_PACK, A_WO, A_WQ, A_WI, A_WB) = range(5)
(R_GB, R_GI, R_GO, R_GQ) = range(4)


def dot_nn(a, b):
    return jnp.dot(a, b, preferred_element_type=F32)


def dot_nt(a, b):
    return lax.dot_general(a, b, (((1,), (1,)), ((), ())), preferred_element_type=F32)


def dot_tn(a, b):
    return lax.dot_general(a, b, (((0,), (0,)), ((), ())), preferred_element_type=F32)


def layer_kernel(
    x_in, cot, wq_in, wo_in, wi_in, wb_in, pack, mask, valid,
    out_o, gtok_o, gq_o, go_o, gi_o, gb_o, sv_o,
    X, WQ, WI, WB, WO, PK, VEC, IB, BQ,
    MIX, PROB, CTX, CTXO, XH1, NF, RS1, N, DG, ACT, SB, RB, OWN,
    G, GS, GPB, SB2, RB2, GF, GFB, GCS, GC, GM, SB3, RB3,
    ACC,
    mB, csB, crB, zsB, zrB, rlB,
    mI, csI, crI, zsI, zrI, rlI,
    mQ, csQ, crQ, zsQ, zrQ, rlQ,
    csO, crO, mO, psO, prO, zO, zsO, zrO, rlO,
    siI, riI, siQ, riQ, resI, resQ,
    GV, GVC, RVC, TVZ, RVZ, PV, RVP,
    lsem, ps, pr, zs, zr, cs, cr, zs2, zr2, cs2, cr2, zs3, zr3,
):
    g = lax.axis_index("grp")
    s = lax.axis_index("seq")
    z = g // 2
    c = g % 2
    rank = {1: s + 1 - 2 * (s % 2), 2: (s + 2) % 4, 3: 3 - s}
    partner = (g + 1 - 2 * c, s)
    drains = []

    def peer(j):
        return (g, rank[j])

    def up(d):
        return (g + 2 * d, s)

    def has(d):
        return jnp.logical_and(z + d >= 0, z + d <= PLANES - 1)

    def rc(src, dst, ss, rs, dev):
        return pltpu.make_async_remote_copy(
            src_ref=src, dst_ref=dst, send_sem=ss, recv_sem=rs, device_id=dev, device_id_type=MESH
        )

    def send(src, dst, ss, rs, dev):
        rc(src, dst, ss, rs, dev).start()
        drains.append(lambda: rc(src, dst, ss, rs, dev).wait_send())

    def send_if(cond, src, dst, ss, rs, dev):
        @pl.when(cond)
        def _():
            rc(src, dst, ss, rs, dev).start()

        def drain():
            @pl.when(cond)
            def _():
                rc(src, dst, ss, rs, dev).wait_send()

        drains.append(drain)

    def got(dst, rs):
        rc(dst, dst, lsem.at[7], rs, partner).wait_recv()

    def rows(i, n):
        return pl.ds(pl.multiple_of(i * n, n), n)

    bar = pltpu.get_barrier_semaphore()
    for j in (1, 2, 3):
        pl.semaphore_signal(bar, inc=1, device_id=peer(j), device_id_type=MESH)
    for k in (1, 2, 3):
        pl.semaphore_signal(bar, inc=1, device_id=(2 * ((z + k) % 4) + c, s), device_id_type=MESH)
    pl.semaphore_signal(bar, inc=1, device_id=partner, device_id_type=MESH)
    local = [
        pltpu.make_async_copy(x_in, X.at[rows(s, 128)], lsem.at[0]),
        pltpu.make_async_copy(wq_in.at[:, rows(s, 768)], WQ.at[rows(4 * g + s, 32)], lsem.at[1]),
        pltpu.make_async_copy(wo_in, WO.at[z, c, s], lsem.at[2]),
        pltpu.make_async_copy(wb_in, WB.at[rows(g, 128)], lsem.at[3]),
        pltpu.make_async_copy(pack, PK.at[z, c, s], lsem.at[4]),
    ]
    wi_local = [
        pltpu.make_async_copy(
            wi_in.at[:, rows(4 * i + s, 128)], WI.at[rows(4 * g + s, 32), pl.ds(128 * i, 128)], lsem.at[5]
        )
        for i in range(8)
    ]
    for cp in local + wi_local:
        cp.start()
    pl.semaphore_wait(bar, 7)

    for j in (1, 2, 3):
        send(pack, PK.at[z, c, s], ps.at[T_PACK, j - 1], pr.at[T_PACK, j - 1], peer(j))
    for j in (1, 2, 3):
        send(
            wq_in.at[:, rows(rank[j], 768)], WQ.at[rows(4 * g + s, 32)],
            ps.at[T_WQ, j - 1], pr.at[T_WQ, j - 1], peer(j),
        )

    def zag_start(tag, own):
        for di, d in enumerate((1, -1, 2, -2)):
            send_if(has(d), own, own, zs.at[tag, di], zr.at[tag, z], up(d))

    def core_send(tag, o, ref):
        return rc(ref, ref, cs.at[tag, o], cr.at[tag, o], partner)

    def zag_mid(tag, chunk, core=True):
        for o in (0, 3, 1, 2):
            @pl.when(jnp.logical_and(z != o, jnp.logical_and(z - o <= 2, o - z <= 2)))
            def _():
                got(chunk(o, c), zr.at[tag, o])
                if core:
                    core_send(tag, o, chunk(o, c)).start()
            if o == 0:
                send_if(z == 2, chunk(0, c), chunk(0, c), zs.at[tag, 4], zr.at[tag, 0], up(1))
            if o == 3:
                send_if(z == 1, chunk(3, c), chunk(3, c), zs.at[tag, 4], zr.at[tag, 3], up(-1))

    def zag_far(tag, chunk, core=True):
        for o, at in ((0, 3), (3, 0)):
            @pl.when(z == at)
            def _():
                got(chunk(o, c), zr.at[tag, o])
                if core:
                    core_send(tag, o, chunk(o, c)).start()

    def zag_core(tag, chunk):
        for o in range(PLANES):
            got(chunk(o, 1 - c), cr.at[tag, o])

        def drain():
            for o in range(PLANES):
                core_send(tag, o, chunk(o, c)).wait_send()

        drains.append(drain)

    def ck_wo(o, cc):
        return WO.at[o, cc, s]

    def ck_pk(o, cc):
        return PK.at[o, cc]

    def ck(ref):
        return lambda o, cc: ref.at[rows(2 * o + cc, 128)]

    ck_wq, ck_wi, ck_wb = ck(WQ), ck(WI), ck(WB)

    for cp in local:
        cp.wait()
    zag_start(A_WO, WO.at[z, c, s])
    for j in (1, 2, 3):
        for i in range(8):
            send(
                wi_in.at[:, rows(4 * i + rank[j], 128)],
                WI.at[rows(4 * g + s, 32), pl.ds(128 * i, 128)],
                ps.at[T_WI, j - 1], pr.at[T_WI, j - 1], peer(j),
            )
            if i:
                drains.pop()
        drains.pop()

    def drain_wi():
        for j in (1, 2, 3):
            blk = WI.at[rows(4 * g + s, 32)]
            rc(blk, blk, ps.at[T_WI, j - 1], pr.at[T_WI, j - 1], peer(j)).wait_send()

    drains.append(drain_wi)
    for j in (1, 2, 3):
        send(x_in, X.at[rows(s, 128)], ps.at[T_TOK, j - 1], pr.at[T_TOK, j - 1], peer(j))
    for j in (1, 2, 3):
        got(PK.at[z, c, rank[j]], pr.at[T_PACK, j - 1])
    zag_start(A_PACK, PK.at[z, c])
    core_send(A_PACK, z, PK.at[z, c]).start()
    for j in (1, 2, 3):
        got(WQ.at[rows(4 * g + rank[j], 32)], pr.at[T_WQ, j - 1])
    zag_start(A_WQ, ck_wq(z, c))
    core_send(A_WQ, z, ck_wq(z, c)).start()
    for j in (1, 2, 3):
        got(WI.at[rows(4 * g + rank[j], 32)], pr.at[T_WI, j - 1])
    for cp in wi_local:
        cp.wait()
    zag_start(A_WI, ck_wi(z, c))
    core_send(A_WI, z, ck_wi(z, c)).start()
    zag_start(A_WB, ck_wb(z, c))
    core_send(A_WB, z, ck_wb(z, c)).start()

    zag_mid(A_WO, ck_wo, core=False)
    zag_mid(A_PACK, ck_pk)
    zag_far(A_WO, ck_wo, core=False)
    for j in (1, 2, 3):
        send(WO.at[:, c, s], WO.at[:, c, s], ps.at[T_WO, j - 1], pr.at[T_WO, j - 1], peer(j))
    zag_far(A_PACK, ck_pk)
    zag_mid(A_WQ, ck_wq)
    zag_far(A_WQ, ck_wq)
    zag_core(A_PACK, ck_pk)
    for gg in range(8):
        tot = PK[gg // 2, gg % 2, 0].astype(F32)
        for r in (1, 2, 3):
            tot = tot + PK[gg // 2, gg % 2, r].astype(F32)
        VEC[:, gg * 128 : (gg + 1) * 128] = tot
        IB[:, gg * 128 : (gg + 1) * 128] = PK[gg // 2, gg % 2, s].astype(F32)
    for cc in range(2):
        tot = PK[s, cc, 0].astype(F32)
        for r in (1, 2, 3):
            tot = tot + PK[s, cc, r].astype(F32)
        for k in range(3):
            BQ[0:1, (3 * cc + k) * 128 : (3 * cc + k + 1) * 128] = tot[k : k + 1, :]
    for j in (1, 2, 3):
        got(X.at[rows(rank[j], 128)], pr.at[T_TOK, j - 1])
    zag_core(A_WQ, ck_wq)

    def qkv(t, carry):
        cols = rows(t, 256)
        MIX[:, cols] = (dot_nn(X[...], WQ[:, cols]) + BQ[0:1, cols]).astype(BF)
        return carry

    lax.fori_loop(0, 3, qkv, 0)

    factor = 1.0 / math.sqrt(HD)

    def attend(n, carry):
        rr = rows(n, 256)
        ok = mask[rows(n, 8), :][0:1, :] > 0.5
        outs = []
        for i in range(4):
            q = MIX[rr, 192 * i : 192 * i + 64]
            k = MIX[rr, 192 * i + 64 : 192 * i + 128]
            v = MIX[rr, 192 * i + 128 : 192 * i + 192]
            sc = jnp.where(ok, dot_nt(q, k) * factor, -1e30)
            e = jnp.exp(sc - jnp.max(sc, axis=-1, keepdims=True))
            p = e * (1.0 / jnp.sum(e, axis=-1, keepdims=True))
            PROB[n, i] = p
            outs.append(dot_nn(p.astype(BF), v).astype(BF))
        CTX[rr, 0:128] = jnp.concatenate(outs[:2], axis=1)
        CTX[rr, 128:256] = jnp.concatenate(outs[2:], axis=1)
        return carry

    lax.fori_loop(0, 2, attend, 0)
    for j in (3, 1, 2):
        send(
            CTX.at[rows(rank[j], 128)], CTXO.at[:, rows(s, 256)],
            ps.at[T_CTX, j - 1], pr.at[T_CTX, j - 1], peer(j),
        )
    CTXO[:, rows(s, 256)] = CTX[rows(s, 128), :]
    for j in (1, 2, 3):
        got(WO.at[:, c, rank[j]], pr.at[T_WO, j - 1])
    wo_cp = rc(WO.at[:, c], WO.at[:, c], cs.at[A_WO, 0], cr.at[A_WO, 0], partner)
    wo_cp.start()
    drains.append(lambda: rc(WO.at[:, c], WO.at[:, c], cs.at[A_WO, 0], cr.at[A_WO, 0], partner).wait_send())
    zag_mid(A_WI, ck_wi)
    got(WO.at[:, 1 - c], cr.at[A_WO, 0])
    for j in (1, 2, 3):
        got(CTXO.at[:, rows(rank[j], 256)], pr.at[T_CTX, j - 1])

    def proj(t, carry):
        cols = rows(t, 256)
        w = WO[:, :, :, :, cols].reshape(1024, 256)
        XH1[:, cols] = x_in[:, cols].astype(F32) + (dot_nn(CTXO[...], w) + VEC[3:4, cols])
        return carry

    lax.fori_loop(0, 4, proj, 0)

    def norm_one(t, carry):
        rr = rows(t, 32)
        h = XH1[rr, :]
        ctr = h - jnp.mean(h, axis=-1, keepdims=True)
        rstd = lax.rsqrt(jnp.mean(ctr * ctr, axis=-1, keepdims=True) + NORM_EPS)
        xh = ctr * rstd
        nf = xh * VEC[4:5, :] + VEC[5:6, :]
        XH1[rr, :] = xh
        RS1[rr, :] = jnp.broadcast_to(rstd, (32, 128))
        NF[rr, :] = nf
        N[pl.ds(pl.multiple_of(s * 128 + t * 32, 32), 32), :] = nf.astype(BF)
        return carry

    lax.fori_loop(0, 4, norm_one, 0)
    me = rows(s, 128)
    for j in (3, 1, 2):
        send(N.at[me], N.at[me], ps.at[T_N, j - 1], pr.at[T_N, j - 1], peer(j))
    zag_far(A_WI, ck_wi)
    zag_core(A_WI, ck_wi)

    def ffn_in(rr):
        def body(t, carry):
            cols = rows(t, 256)
            pre = dot_nn(N[rr, :], WI[:, cols]) + IB[9:10, cols]
            cdf = 0.5 * (1.0 + lax.erf(pre * math.sqrt(0.5)))
            ACT[rr, cols] = (pre * cdf).astype(BF)
            DG[rr, cols] = cdf + pre * jnp.exp(-0.5 * (pre * pre)) * (1.0 / math.sqrt(2.0 * math.pi))
            return carry

        lax.fori_loop(0, 4, body, 0)

    def ffn_out(rr, j):
        def body(t, carry):
            cols = rows(t, 256)
            part = dot_nn(ACT[rr, :], WB[:, cols])
            if j == 0:
                OWN[:, cols] = part
            else:
                SB[j - 1, :, cols] = part.astype(BF)
            return carry

        lax.fori_loop(0, 4, body, 0)

    order = (1, 2, 3)
    ffn_in(me)
    zag_mid(A_WB, ck_wb)
    for j in order:
        rr = rows(rank[j], 128)
        got(N.at[rr], pr.at[T_N, j - 1])
        ffn_in(rr)
    zag_far(A_WB, ck_wb)
    zag_core(A_WB, ck_wb)
    for j in (3, 1, 2):
        ffn_out(rows(rank[j], 128), j)
        send(SB.at[j - 1], RB.at[j - 1], ps.at[T_RSF, j - 1], pr.at[T_RSF, j - 1], peer(j))
    ffn_out(me, 0)
    for j in (1, 2, 3):
        got(RB.at[j - 1], pr.at[T_RSF, j - 1])

    GV[...] = jnp.zeros_like(GV)

    def norm_two(t, carry):
        rr = rows(t, 32)
        h = OWN[rr, :] + RB[0, rr, :].astype(F32) + RB[1, rr, :].astype(F32) + RB[2, rr, :].astype(F32)
        h = NF[rr, :] + (h + VEC[6:7, :])
        ctr = h - jnp.mean(h, axis=-1, keepdims=True)
        rstd = lax.rsqrt(jnp.mean(ctr * ctr, axis=-1, keepdims=True) + NORM_EPS)
        xh = ctr * rstd
        out_o[rr, :] = (xh * VEC[7:8, :] + VEC[8:9, :]).astype(BF)
        seed = cot[rr, :].astype(F32) * valid[rr, 0:1]
        GV[7:8, :] += jnp.sum(seed * xh, axis=0, keepdims=True)
        GV[8:9, :] += jnp.sum(seed, axis=0, keepdims=True)
        u = seed * VEC[7:8, :]
        gs = rstd * (u - jnp.mean(u, axis=-1, keepdims=True) - xh * jnp.mean(u * xh, axis=-1, keepdims=True))
        GV[6:7, :] += jnp.sum(gs, axis=0, keepdims=True)
        GS[rr, :] = gs
        G[pl.ds(pl.multiple_of(s * 128 + t * 32, 32), 32), :] = gs.astype(BF)
        return carry

    lax.fori_loop(0, 4, norm_two, 0)
    for j in (3, 1, 2):
        send(G.at[me], G.at[me], ps.at[T_G, j - 1], pr.at[T_G, j - 1], peer(j))

    def bwd_act(rr):
        def body(t, carry):
            cols = rows(t, 256)
            gp = dot_nt(G[rr, :], WB[cols, :]) * DG[rr, cols]
            GV[9:10, cols] += jnp.sum(gp, axis=0, keepdims=True)
            GPB[rr, cols] = gp.astype(BF)
            return carry

        lax.fori_loop(0, 4, body, 0)

    def bwd_in(rr, j):
        def body(t, carry):
            cols = rows(t, 256)
            part = dot_nt(GPB[rr, :], WI[cols, :])
            if j == 0:
                OWN[:, cols] = part
            else:
                SB2[j - 1, :, cols] = part.astype(BF)
            return carry

        lax.fori_loop(0, 4, body, 0)

    bwd_act(me)
    bwd_in(me, 0)
    for j in order:
        rr = rows(rank[j], 128)
        got(G.at[rr], pr.at[T_G, j - 1])
        bwd_act(rr)
        bwd_in(rr, j)
        send(SB2.at[j - 1], RB2.at[j - 1], ps.at[T_RSB, j - 1], pr.at[T_RSB, j - 1], peer(j))

    def wgrad(lhs, rhs, mine, csend, cols):
        def body(t, carry):
            ACC[:, 0:cols] = dot_tn(lhs[:, rows(t, 256)], rhs[...])
            mine[t] = ACC[rows(c, 128), 0:cols]
            csend[t] = ACC[rows(1 - c, 128), 0:cols].astype(BF)
            return carry

        lax.fori_loop(0, 4, body, 0)

    def core_start(tag, csend, crecv):
        send(csend, crecv, cs2.at[tag], cr2.at[tag], partner)

    def core_sum(tag, mine, crecv, zsend):
        got(crecv, cr2.at[tag])

        def body(t, carry):
            v = mine[t] + crecv[t].astype(F32)
            mine[t] = v
            zsend[t] = v.astype(BF)
            return carry

        lax.fori_loop(0, 4, body, 0)

    def zrs_start(tag, zsend, zrecv, relay):
        send_if(z == 0, zsend.at[3], relay, zs2.at[tag, 4], zr2.at[tag, 4], up(1))
        send_if(z == 3, zsend.at[0], relay, zs2.at[tag, 4], zr2.at[tag, 4], up(-1))
        for di, d, late in ((2, 2, 1), (3, -2, 2), (0, 1, 9), (1, -1, 9)):
            send_if(
                jnp.logical_and(has(d), z != late),
                zsend.at[jnp.clip(z + d, 0, 3)], zrecv.at[z], zs2.at[tag, di], zr2.at[tag, z], up(d),
            )

    def zrs_relay(tag, mine, zsend, zrecv, relay):
        for at, far, di, d in ((1, 3, 2, 2), (2, 0, 3, -2)):
            @pl.when(z == at)
            def _():
                got(relay, zr2.at[tag, 4])
                zsend[far] = (mine[far] + relay[...].astype(F32)).astype(BF)

            send_if(z == at, zsend.at[far], zrecv.at[z], zs2.at[tag, di], zr2.at[tag, z], up(d))

    def zrs_end(tag, mine, zrecv, res):
        res[...] = mine[z]
        for o in range(PLANES):
            @pl.when(jnp.logical_and(z != o, jnp.logical_and(z - o <= 2, o - z <= 2)))
            def _():
                got(zrecv.at[o], zr2.at[tag, o])
                res[...] += zrecv[o].astype(F32)

    wgrad(ACT, G, mB, csB, 1024)
    core_start(R_GB, csB, crB)
    wgrad(N, GPB, mI, csI, 1024)
    core_start(R_GI, csI, crI)
    core_sum(R_GB, mB, crB, zsB)
    zrs_start(R_GB, zsB, zrB, rlB)
    for j in (1, 2, 3):
        got(RB2.at[j - 1], pr.at[T_RSB, j - 1])

    def norm_one_bwd(t, carry):
        rr = rows(t, 32)
        gn = OWN[rr, :] + RB2[0, rr, :].astype(F32) + RB2[1, rr, :].astype(F32) + RB2[2, rr, :].astype(F32)
        gn = GS[rr, :] + gn
        xh = XH1[rr, :]
        GV[4:5, :] += jnp.sum(gn * xh, axis=0, keepdims=True)
        GV[5:6, :] += jnp.sum(gn, axis=0, keepdims=True)
        u = gn * VEC[4:5, :]
        gf = RS1[rr, 0:1] * (
            u - jnp.mean(u, axis=-1, keepdims=True) - xh * jnp.mean(u * xh, axis=-1, keepdims=True)
        )
        GV[3:4, :] += jnp.sum(gf, axis=0, keepdims=True)
        GF[rr, :] = gf
        GFB[rr, :] = gf.astype(BF)
        return carry

    lax.fori_loop(0, 4, norm_one_bwd, 0)

    def gctx(t, carry):
        w = WO[t].reshape(256, 1024)
        GCS[t] = dot_nt(GFB[...], w).astype(BF)
        return carry

    lax.fori_loop(0, 4, gctx, 0)
    for j in (3, 1, 2):
        send(GCS.at[rank[j]], GC.at[me], ps.at[T_GC, j - 1], pr.at[T_GC, j - 1], peer(j))
    GC[me, :] = GCS[s]
    core_sum(R_GI, mI, crI, zsI)
    zrs_start(R_GI, zsI, zrI, rlI)
    wgrad(CTXO, GFB, mO, csO, 1024)
    core_start(R_GO, csO, crO)
    zrs_relay(R_GB, mB, zsB, zrB, rlB)
    for j in (1, 2, 3):
        got(GC.at[rows(rank[j], 128)], pr.at[T_GC, j - 1])

    got(crO, cr2.at[R_GO])

    def go_core(t, carry):
        v = mO[t] + crO[t].astype(F32)
        mO[t] = v
        for r in range(4):
            psO[r, t] = v[32 * r : 32 * r + 32, :].astype(BF)
        return carry

    lax.fori_loop(0, 4, go_core, 0)
    for j in (1, 2, 3):
        send(psO.at[rank[j]], prO.at[j - 1], ps.at[T_GO, j - 1], pr.at[T_GO, j - 1], peer(j))

    GQS = jnp.zeros((1, 768), F32)
    BQ[...] = jnp.zeros_like(BQ)

    def attend_bwd(n, carry):
        rr = rows(n, 256)
        for pair in range(2):
            parts = []
            for i in (2 * pair, 2 * pair + 1):
                q = MIX[rr, 192 * i : 192 * i + 64]
                k = MIX[rr, 192 * i + 64 : 192 * i + 128]
                v = MIX[rr, 192 * i + 128 : 192 * i + 192]
                gc = GC[rr, 64 * i : 64 * i + 64]
                p = PROB[n, i]
                gp = dot_nt(gc, v)
                inner = jnp.sum(p * gp, axis=-1, keepdims=True)
                gsc = (p * (gp - inner) * factor).astype(BF)
                parts += [dot_nn(gsc, k), dot_tn(gsc, q), dot_tn(p.astype(BF), gc)]
            both = jnp.concatenate([x.astype(BF) for x in parts], axis=1)
            GM[rr, 384 * pair : 384 * pair + 384] = both
            BQ[0:1, 384 * pair : 384 * pair + 384] += jnp.sum(both.astype(F32), axis=0, keepdims=True)
        return carry

    lax.fori_loop(0, 2, attend_bwd, 0)
    zrs_relay(R_GI, mI, zsI, zrI, rlI)
    wgrad(X, GM, mQ, csQ, 768)
    core_start(R_GQ, csQ, crQ)

    for j in (1, 2, 3):
        got(prO.at[j - 1], pr.at[T_GO, j - 1])

    def go_plane(t, carry):
        v = mO[t, rows(s, 32), :]
        for j in (1, 2, 3):
            v = v + prO[j - 1, t].astype(F32)
        zO[t] = v
        zsO[t] = v.astype(BF)
        return carry

    lax.fori_loop(0, 4, go_plane, 0)
    core_sum(R_GQ, mQ, crQ, zsQ)
    zrs_start(R_GQ, zsQ, zrQ, rlQ)
    zrs_start(R_GO, zsO, zrO, rlO)

    def gtok(rr, j):
        def body(t, carry):
            cols = rows(t, 256)
            part = dot_nt(GM[rr, :], WQ[cols, :])
            if j == 0:
                OWN[:, cols] = part
            else:
                SB3[j - 1, :, cols] = part.astype(BF)
            return carry

        lax.fori_loop(0, 4, body, 0)

    for j in (3, 1, 2):
        gtok(rows(rank[j], 128), j)
        send(SB3.at[j - 1], RB3.at[j - 1], ps.at[T_GT, j - 1], pr.at[T_GT, j - 1], peer(j))
    gtok(me, 0)

    for k in range(6):
        GV[k % 3 : k % 3 + 1, rows(2 * s + k // 3, 128)] = BQ[0:1, 128 * k : 128 * k + 128]
    for gg in range(8):
        GVC[gg % 2, gg // 2] = GV[:, 128 * gg : 128 * gg + 128]
    send(GVC.at[1 - c], RVC, cs2.at[4], cr2.at[4], partner)
    got(RVC, cr2.at[4])
    TVZ[...] = GVC[c] + RVC[...]
    for k in (1, 2, 3):
        t = (z + k) % 4
        send(TVZ.at[t], RVZ.at[k - 1], zs3.at[k - 1], zr3.at[k - 1], (2 * t + c, s))
    for k in (1, 2, 3):
        got(RVZ.at[k - 1], zr3.at[k - 1])
    PV[...] = TVZ[z] + RVZ[0] + RVZ[1] + RVZ[2]
    for j in (1, 2, 3):
        send(PV, RVP.at[j - 1], ps.at[T_SV, j - 1], pr.at[T_SV, j - 1], peer(j))

    zrs_relay(R_GQ, mQ, zsQ, zrQ, rlQ)
    zrs_relay(R_GO, zO, zsO, zrO, rlO)
    zrs_end(R_GB, mB, zrB, gb_o)
    zrs_end(R_GI, mI, zrI, resI)
    for j in (1, 2, 3):
        siI[j - 1] = resI[rows(rank[j], 32), :].astype(BF)
    for j in (1, 2, 3):
        send(siI.at[j - 1], riI.at[j - 1], ps.at[T_GI, j - 1], pr.at[T_GI, j - 1], peer(j))
    for j in (1, 2, 3):
        got(RB3.at[j - 1], pr.at[T_GT, j - 1])

    def gtok_sum(t, carry):
        rr = rows(t, 32)
        h = OWN[rr, :] + RB3[0, rr, :].astype(F32) + RB3[1, rr, :].astype(F32) + RB3[2, rr, :].astype(F32)
        gtok_o[rr, :] = GF[rr, :] + h
        return carry

    lax.fori_loop(0, 4, gtok_sum, 0)
    zrs_end(R_GQ, mQ, zrQ, resQ)
    for j in (1, 2, 3):
        siQ[j - 1] = resQ[rows(rank[j], 32), :].astype(BF)
    for j in (1, 2, 3):
        send(siQ.at[j - 1], riQ.at[j - 1], ps.at[T_GQ, j - 1], pr.at[T_GQ, j - 1], peer(j))
    zrs_end(R_GO, zO, zrO, go_o)
    for i in range(8):
        gi_o[:, rows(4 * i + s, 128)] = resI[rows(s, 32), 128 * i : 128 * i + 128]
    gq_o[:, rows(s, 768)] = resQ[rows(s, 32), :]
    for j in (1, 2, 3):
        got(riI.at[j - 1], pr.at[T_GI, j - 1])
        for i in range(8):
            gi_o[:, rows(4 * i + rank[j], 128)] = riI[j - 1, :, 128 * i : 128 * i + 128].astype(F32)
    for j in (1, 2, 3):
        got(RVP.at[j - 1], pr.at[T_SV, j - 1])
    tot = PV[...] + RVP[0] + RVP[1] + RVP[2]
    row = lax.broadcasted_iota(jnp.int32, (16, 128), 0)
    sv_o[...] = jnp.where(row == 9, PV[...], tot)
    for j in (1, 2, 3):
        got(riQ.at[j - 1], pr.at[T_GQ, j - 1])
        gq_o[:, rows(rank[j], 768)] = riQ[j - 1].astype(F32)
    for drain in drains:
        drain()


def fused_shards(
    tokens, cotangent, slot_lengths, w_qkv, qv_bias, w_out, out_bias, ln1_gain, ln1_bias,
    w_in, in_bias, w_back, back_bias, ln2_gain, ln2_bias,
):
    s = lax.axis_index("seq")
    lane = jnp.arange(128)

    def spread(v):
        return jnp.where(lane // 32 == s, jnp.tile(v, 4), 0).astype(BF)

    zero = jnp.zeros((128,), BF)
    both = jnp.where(lane // 64 == s // 2, jnp.tile(qv_bias, 2), 0).astype(BF)
    lines = [jnp.where((s + 1) // 2 == k, both, zero) for k in range(3)]
    lines += [spread(v) for v in (out_bias, ln1_gain, ln1_bias, back_bias, ln2_gain, ln2_bias)]
    lines += [in_bias]
    lines += [zero] * 6
    pack = jnp.stack(lines)
    mask = jnp.repeat((jnp.arange(256)[None, :] < slot_lengths[:, None]).astype(F32), 8, axis=0)
    place = (s % 2) * 128 + jnp.arange(128)
    length = jnp.where(s // 2 == 0, slot_lengths[0], slot_lengths[1])
    valid = jnp.broadcast_to((place < length).astype(F32)[:, None], (128, 128))

    vm = pltpu.VMEM
    dma = pltpu.SemaphoreType.DMA

    def item(n):
        return [
            vm((4, 128, n), F32), vm((4, 128, n), BF), vm((4, 128, n), BF),
            vm((4, 128, n), BF), vm((4, 128, n), BF), vm((128, n), BF),
        ]

    scratch = [
        vm((512, 1024), BF), vm((1024, 768), BF), vm((1024, 1024), BF), vm((1024, 1024), BF),
        vm((4, 2, 4, 32, 1024), BF), vm((4, 2, 4, 16, 128), BF), vm((16, 1024), F32), vm((16, 1024), F32),
        vm((8, 768), F32),
        vm((512, 768), BF), vm((2, 4, 256, 256), F32), vm((512, 256), BF), vm((128, 1024), BF),
        vm((128, 1024), F32), vm((128, 1024), F32), vm((128, 128), F32), vm((512, 1024), BF),
        vm((512, 1024), F32), vm((512, 1024), BF), vm((3, 128, 1024), BF), vm((3, 128, 1024), BF),
        vm((128, 1024), F32),
        vm((512, 1024), BF), vm((128, 1024), F32), vm((512, 1024), BF), vm((3, 128, 1024), BF),
        vm((3, 128, 1024), BF), vm((128, 1024), F32), vm((128, 1024), BF), vm((4, 128, 256), BF),
        vm((512, 256), BF), vm((512, 768), BF), vm((3, 128, 1024), BF), vm((3, 128, 1024), BF),
        vm((256, 1024), F32),
    ]
    scratch += item(1024) + item(1024) + item(768)
    scratch += [
        vm((4, 128, 1024), BF), vm((4, 128, 1024), BF), vm((4, 128, 1024), F32),
        vm((4, 4, 32, 1024), BF), vm((3, 4, 32, 1024), BF), vm((4, 32, 1024), F32),
        vm((4, 32, 1024), BF), vm((4, 32, 1024), BF), vm((32, 1024), BF),
        vm((3, 32, 1024), BF), vm((3, 32, 1024), BF), vm((3, 32, 768), BF), vm((3, 32, 768), BF),
        vm((128, 1024), F32), vm((128, 768), F32),
        vm((16, 1024), F32), vm((2, 4, 16, 128), F32), vm((4, 16, 128), F32), vm((4, 16, 128), F32),
        vm((3, 16, 128), F32), vm((16, 128), F32), vm((3, 16, 128), F32),
        dma((8,)), dma((16, 3)), dma((16, 3)), dma((5, 5)), dma((5, 4)), dma((5, 4)), dma((5, 4)),
        dma((4, 5)), dma((4, 5)), dma((5,)), dma((5,)), dma((3,)), dma((3,)),
    ]
    full = pl.BlockSpec(memory_space=pltpu.VMEM)
    shapes = [
        ((128, 1024), BF), ((128, 1024), F32), ((32, 3072), F32), ((32, 1024), F32),
        ((32, 4096), F32), ((128, 1024), F32), ((16, 128), F32),
    ]
    output, grad_tokens, grad_qkv, grad_wo, grad_wi, grad_wb, sums = pl.pallas_call(
        layer_kernel,
        out_shape=[jax.ShapeDtypeStruct(a, b) for a, b in shapes],
        in_specs=[full] * 9,
        out_specs=[full] * 7,
        scratch_shapes=scratch,
        compiler_params=pltpu.CompilerParams(
            collective_id=0, has_side_effects=True, vmem_limit_bytes=67_000_000
        ),
        name="encoder_layer",
    )(tokens, cotangent, w_qkv, w_out, w_in, w_back, pack, mask, valid)

    def own(k):
        return lax.dynamic_slice(sums[k], (s * 32,), (32,))

    qv = lax.dynamic_slice(sums, ((s + 1) // 2, (s // 2) * 64), (1, 64)).reshape(64)
    return (
        output, grad_tokens, grad_qkv, qv, grad_wo, own(3), own(4), own(5),
        grad_wi, sums[9], grad_wb, own(6), own(7), own(8),
    )


def solution(mesh):
    placed = (
        P(("grp", "seq"), None),
        P(("grp", "seq"), None),
        P("grp"),
        P(("grp", "seq"), None),
        P(("grp", "seq")),
        P(("grp", "seq"), None),
        P(("grp", "seq")),
        P(("grp", "seq")),
        P(("grp", "seq")),
        P(("grp", "seq"), None),
        P(("grp", "seq")),
        P(("grp", "seq"), None),
        P(("grp", "seq")),
        P(("grp", "seq")),
        P(("grp", "seq")),
    )
    fused = mesh.shape["grp"] == 2 * PLANES and mesh.shape["seq"] == RANKS
    return jax.shard_map(
        fused_shards if fused else shards,
        mesh=mesh,
        in_specs=placed,
        out_specs=(
            P(("grp", "seq"), None),
            P(("grp", "seq"), None),
            P(("grp", "seq"), None),
            P(("grp", "seq")),
            P(("grp", "seq"), None),
            P(("grp", "seq")),
            P(("grp", "seq")),
            P(("grp", "seq")),
            P(("grp", "seq"), None),
            P(("grp", "seq")),
            P(("grp", "seq"), None),
            P(("grp", "seq")),
            P(("grp", "seq")),
            P(("grp", "seq")),
        ),
        check_vma=False,
    )
```

```python
from functools import partial
import math

import jax
import jax.numpy as jnp
from jax import lax
from jax.experimental import pallas as pl
from jax.experimental.pallas import tpu as pltpu
from jax.sharding import PartitionSpec as P

D = 1024
H = 16
HD = 64
SLOT_DEV = 64
SLOTS = 2


NORM_EPS = 1e-06


def layer_norm(hidden, gain, shift):
    center = hidden - jnp.mean(hidden, axis=-1, keepdims=True)
    spread = jnp.mean(center * center, axis=-1, keepdims=True)
    return center * lax.rsqrt(spread + NORM_EPS) * gain + shift


def exact_gelu(values):
    return jax.nn.gelu(values, approximate=False)


def full_bias(pair_bias):
    pairs = pair_bias.reshape(H, 2, HD)
    return jnp.stack([pairs[:, 0], jnp.zeros_like(pairs[:, 0]), pairs[:, 1]], axis=1).reshape(3 * D)


def contract_rows(left, right):
    return lax.dot_general(
        left, right, (((0,), (0,)), ((), ())), preferred_element_type=jnp.float32
    )


def contract_cols(left, right):
    return lax.dot_general(
        left, right, (((1,), (1,)), ((), ())), preferred_element_type=jnp.float32
    )


def slot_scores(mixed, length, factor):
    slot_width = mixed.shape[0]
    queries = mixed[:, :, 0]
    key_rows = mixed[:, :, 1]
    value_rows = mixed[:, :, 2]
    products = jnp.einsum("qhd,khd->hqk", queries, key_rows, preferred_element_type=jnp.float32)
    key_valid = (jnp.arange(slot_width) < length)[None, None, :]
    scores = jnp.where(key_valid, products * factor, -1e30)
    return (queries, key_rows, value_rows, scores)


def slot_forward(item, factor):
    mixed, length = item
    queries, key_rows, value_rows, scores = slot_scores(mixed, length, factor)
    row_max = jnp.max(scores, axis=-1, keepdims=True)
    expon = jnp.exp(scores - row_max)
    total = jnp.sum(expon, axis=-1, keepdims=True)
    probs = expon / total
    context = jnp.einsum(
        "hqk,khd->qhd", probs.astype(jnp.bfloat16), value_rows, preferred_element_type=jnp.float32
    )
    return (context.astype(jnp.bfloat16), row_max + jnp.log(total))


def slot_backward(item, factor):
    mixed, grad_context, log_total, length = item
    queries, key_rows, value_rows, scores = slot_scores(mixed, length, factor)
    probs = jnp.exp(scores - log_total)
    grad_probs = jnp.einsum(
        "qhd,khd->hqk", grad_context, value_rows, preferred_element_type=jnp.float32
    )
    inner = jnp.sum(probs * grad_probs, axis=-1, keepdims=True)
    grad_scores = (probs * (grad_probs - inner) * factor).astype(jnp.bfloat16)
    grad_queries = jnp.einsum(
        "hqk,khd->qhd", grad_scores, key_rows, preferred_element_type=jnp.float32
    )
    grad_keys = jnp.einsum("hqk,qhd->khd", grad_scores, queries, preferred_element_type=jnp.float32)
    grad_values = jnp.einsum(
        "hqk,qhd->khd", probs.astype(jnp.bfloat16), grad_context, preferred_element_type=jnp.float32
    )
    return jnp.stack([grad_queries, grad_keys, grad_values], axis=2).astype(jnp.bfloat16)


def shards(
    tokens,
    cotangent,
    slot_lengths,
    w_qkv,
    qv_bias,
    w_out,
    out_bias,
    ln1_gain,
    ln1_bias,
    w_in,
    in_bias,
    w_back,
    back_bias,
    ln2_gain,
    ln2_bias,
):
    seq_count = lax.axis_size("seq")
    local_rows = tokens.shape[0]
    slot_width = SLOT_DEV * seq_count
    heads_here = H // seq_count
    factor = 1.0 / math.sqrt(HD)
    full_qkv, full_qv, full_out, full_obias, gain_one, shift_one = (
        lax.all_gather(w_qkv, ("grp", "seq"), axis=0, tiled=True),
        lax.all_gather(qv_bias, ("grp", "seq"), axis=0, tiled=True),
        lax.all_gather(w_out, ("grp", "seq"), axis=0, tiled=True),
        lax.all_gather(out_bias, ("grp", "seq"), axis=0, tiled=True),
        lax.all_gather(ln1_gain, ("grp", "seq"), axis=0, tiled=True),
        lax.all_gather(ln1_bias, ("grp", "seq"), axis=0, tiled=True),
    )
    full_in, full_ibias, full_back, full_bbias, gain_two, shift_two = (
        lax.all_gather(w_in, ("grp", "seq"), axis=0, tiled=True),
        lax.all_gather(in_bias, ("grp", "seq"), axis=0, tiled=True),
        lax.all_gather(w_back, ("grp", "seq"), axis=0, tiled=True),
        lax.all_gather(back_bias, ("grp", "seq"), axis=0, tiled=True),
        lax.all_gather(ln2_gain, ("grp", "seq"), axis=0, tiled=True),
        lax.all_gather(ln2_bias, ("grp", "seq"), axis=0, tiled=True),
    )
    mixed = (
        jnp.dot(tokens, full_qkv, preferred_element_type=jnp.float32) + full_bias(full_qv)
    ).astype(jnp.bfloat16)
    gathered = lax.all_to_all(mixed, "seq", split_axis=1, concat_axis=0, tiled=True)
    per_slot = gathered.reshape(SLOTS, slot_width, heads_here, 3, HD)
    contexts, log_totals = lax.map(partial(slot_forward, factor=factor), (per_slot, slot_lengths))
    context_heads = contexts.reshape(SLOTS * slot_width, heads_here * HD)
    context = lax.all_to_all(context_heads, "seq", split_axis=0, concat_axis=1, tiled=True)
    attended = jnp.dot(context, full_out, preferred_element_type=jnp.float32) + full_obias
    first_in = tokens.astype(jnp.float32) + attended
    normed, norm_one_pull = jax.vjp(layer_norm, first_in, gain_one, shift_one)
    normed_low = normed.astype(jnp.bfloat16)
    pre_act = jnp.dot(normed_low, full_in, preferred_element_type=jnp.float32) + full_ibias
    activated, gelu_pull = jax.vjp(exact_gelu, pre_act)
    act_low = activated.astype(jnp.bfloat16)
    ffn_out = jnp.dot(act_low, full_back, preferred_element_type=jnp.float32) + full_bbias
    output, norm_two_pull = jax.vjp(layer_norm, normed + ffn_out, gain_two, shift_two)
    row_index = lax.axis_index("seq") * local_rows + jnp.arange(local_rows)
    slot_index = row_index // slot_width
    place = row_index % slot_width
    row_length = jnp.sum(
        jnp.where(slot_index[:, None] == jnp.arange(SLOTS)[None, :], slot_lengths[None, :], 0),
        axis=1,
    )
    row_valid = (place < row_length).astype(jnp.float32)
    seed_grad = cotangent.astype(jnp.float32) * row_valid[:, None]
    grad_second, grad_gain_two, grad_shift_two = norm_two_pull(seed_grad)
    grad_ffn_low = grad_second.astype(jnp.bfloat16)
    grad_back_w = contract_rows(act_low, grad_ffn_low)
    grad_back_b = jnp.sum(grad_second, axis=0)
    (grad_pre,) = gelu_pull(contract_cols(grad_ffn_low, full_back))
    grad_pre_low = grad_pre.astype(jnp.bfloat16)
    grad_in_w = contract_rows(normed_low, grad_pre_low)
    grad_in_b = jnp.sum(grad_pre, axis=0)
    grad_normed = grad_second + contract_cols(grad_pre_low, full_in)
    grad_first, grad_gain_one, grad_shift_one = norm_one_pull(grad_normed)
    grad_attn_low = grad_first.astype(jnp.bfloat16)
    grad_out_w = contract_rows(context, grad_attn_low)
    grad_out_b = jnp.sum(grad_first, axis=0)
    grad_context = contract_cols(grad_attn_low, full_out).astype(jnp.bfloat16)
    grad_heads = lax.all_to_all(grad_context, "seq", split_axis=1, concat_axis=0, tiled=True)
    grad_slots = grad_heads.reshape(SLOTS, slot_width, heads_here, HD)
    grad_mixed_heads = lax.map(
        partial(slot_backward, factor=factor), (per_slot, grad_slots, log_totals, slot_lengths)
    )
    grad_mixed = lax.all_to_all(
        grad_mixed_heads.reshape(SLOTS * slot_width, heads_here * 3 * HD),
        "seq",
        split_axis=0,
        concat_axis=1,
        tiled=True,
    )
    grad_qkv_w = contract_rows(tokens, grad_mixed)
    summed_bias = jnp.sum(grad_mixed.astype(jnp.float32), axis=0).reshape(H, 3, HD)
    grad_qv = jnp.stack([summed_bias[:, 0], summed_bias[:, 2]], axis=1).reshape(2 * D)
    input_grad = grad_first + contract_cols(grad_mixed, full_qkv)
    sums = (
        lax.psum_scatter(grad_qkv_w, ("grp", "seq"), scatter_dimension=0, tiled=True),
        lax.psum_scatter(grad_qv, ("grp", "seq"), scatter_dimension=0, tiled=True),
        lax.psum_scatter(grad_out_w, ("grp", "seq"), scatter_dimension=0, tiled=True),
        lax.psum_scatter(grad_out_b, ("grp", "seq"), scatter_dimension=0, tiled=True),
        lax.psum_scatter(
            grad_gain_one.astype(jnp.float32), ("grp", "seq"), scatter_dimension=0, tiled=True
        ),
        lax.psum_scatter(
            grad_shift_one.astype(jnp.float32), ("grp", "seq"), scatter_dimension=0, tiled=True
        ),
        lax.psum_scatter(grad_in_w, ("grp", "seq"), scatter_dimension=0, tiled=True),
        lax.psum_scatter(grad_in_b, ("grp", "seq"), scatter_dimension=0, tiled=True),
        lax.psum_scatter(grad_back_w, ("grp", "seq"), scatter_dimension=0, tiled=True),
        lax.psum_scatter(grad_back_b, ("grp", "seq"), scatter_dimension=0, tiled=True),
        lax.psum_scatter(
            grad_gain_two.astype(jnp.float32), ("grp", "seq"), scatter_dimension=0, tiled=True
        ),
        lax.psum_scatter(
            grad_shift_two.astype(jnp.float32), ("grp", "seq"), scatter_dimension=0, tiled=True
        ),
    )
    return (
        output.astype(jnp.bfloat16),
        input_grad,
        sums[0],
        sums[1],
        sums[2],
        sums[3],
        sums[4],
        sums[5],
        sums[6],
        sums[7],
        sums[8],
        sums[9],
        sums[10],
        sums[11],
    )


BF = jnp.bfloat16
F32 = jnp.float32
MESH = pl.DeviceIdType.MESH
PLANES = 4
RANKS = 4
(T_PACK, T_WQ, T_WI, T_TOK, T_WO, T_CTX, T_N, T_RSF, T_G, T_RSB, T_GC, T_GO, T_GT, T_GI, T_GQ, T_SV) = range(16)
(A_PACK, A_WO, A_WQ, A_WI, A_WB) = range(5)
(R_GB, R_GI, R_GO, R_GQ) = range(4)


def dot_nn(a, b):
    return jnp.dot(a, b, preferred_element_type=F32)


def dot_nt(a, b):
    return lax.dot_general(a, b, (((1,), (1,)), ((), ())), preferred_element_type=F32)


def dot_tn(a, b):
    return lax.dot_general(a, b, (((0,), (0,)), ((), ())), preferred_element_type=F32)


def layer_kernel(
    x_in, cot, wq_in, wo_in, wi_in, wb_in, lens, qv_in, ob_in, g1_in, b1_in, ib_in, bb_in, g2_in, b2_in,
    out_o, gtok_o, gq_o, go_o, gi_o, gb_o, sv_o,
    pack, X, WQ, WI, WB, WO, PK, VEC, IB, BQ,
    MIX, PROB, CTX, CTXO, XH1, NF, RS1, N, DG, ACT, SB, RB, OWN,
    G, GS, GPB, SB2, RB2, GF, GFB, GCS, GC, GM, SB3, RB3,
    ACC,
    mB, csB, crB, zsB, zrB, rlB,
    mI, csI, crI, zsI, zrI, rlI,
    mQ, csQ, crQ, zsQ, zrQ, rlQ,
    csO, crO, mO, psO, prO, zO, zsO, zrO, rlO,
    siI, riI, siQ, riQ, resI, resQ,
    GV, GVC, RVC, TVZ, RVZ, PV, RVP,
    lsem, ps, pr, zs, zr, cs, cr, zs2, zr2, cs2, cr2, zs3, zr3,
):
    g = lax.axis_index("grp")
    s = lax.axis_index("seq")
    z = g // 2
    c = g % 2
    rank = {1: s + 1 - 2 * (s % 2), 2: (s + 2) % 4, 3: 3 - s}
    partner = (g + 1 - 2 * c, s)
    drains = []

    def peer(j):
        return (g, rank[j])

    def up(d):
        return (g + 2 * d, s)

    def has(d):
        return jnp.logical_and(z + d >= 0, z + d <= PLANES - 1)

    def rc(src, dst, ss, rs, dev):
        return pltpu.make_async_remote_copy(
            src_ref=src, dst_ref=dst, send_sem=ss, recv_sem=rs, device_id=dev, device_id_type=MESH
        )

    def send(src, dst, ss, rs, dev):
        rc(src, dst, ss, rs, dev).start()
        drains.append(lambda: rc(src, dst, ss, rs, dev).wait_send())

    def send_if(cond, src, dst, ss, rs, dev):
        @pl.when(cond)
        def _():
            rc(src, dst, ss, rs, dev).start()

        def drain():
            @pl.when(cond)
            def _():
                rc(src, dst, ss, rs, dev).wait_send()

        drains.append(drain)

    def got(dst, rs):
        rc(dst, dst, lsem.at[7], rs, partner).wait_recv()

    def rows(i, n):
        return pl.ds(pl.multiple_of(i * n, n), n)

    bar = pltpu.get_barrier_semaphore()
    for j in (1, 2, 3):
        pl.semaphore_signal(bar, inc=1, device_id=peer(j), device_id_type=MESH)
    for k in (1, 2, 3):
        pl.semaphore_signal(bar, inc=1, device_id=(2 * ((z + k) % 4) + c, s), device_id_type=MESH)
    pl.semaphore_signal(bar, inc=1, device_id=partner, device_id_type=MESH)
    lane = lax.broadcasted_iota(jnp.int32, (1, 128), 1)
    pack[...] = jnp.zeros_like(pack)
    two = jnp.concatenate([qv_in[...].astype(F32)] * 2, axis=1)
    for k in range(3):
        pack[k : k + 1, :] = jnp.where(lane // 64 + 4 * ((s + 1) // 2) == s // 2 + 4 * k, two, 0.0)
    for k, ref in ((3, ob_in), (4, g1_in), (5, b1_in), (6, bb_in), (7, g2_in), (8, b2_in)):
        four = jnp.concatenate([ref[...].astype(F32)] * 4, axis=1)
        pack[k : k + 1, :] = jnp.where(lane // 32 == s, four, 0.0)
    pack[9:10, :] = ib_in[...].astype(F32)
    local = [
        pltpu.make_async_copy(x_in, X.at[rows(s, 128)], lsem.at[0]),
        pltpu.make_async_copy(wq_in.at[:, rows(s, 768)], WQ.at[rows(4 * g + s, 32)], lsem.at[1]),
        pltpu.make_async_copy(wo_in, WO.at[z, c, s], lsem.at[2]),
        pltpu.make_async_copy(wb_in, WB.at[rows(g, 128)], lsem.at[3]),
        pltpu.make_async_copy(pack, PK.at[z, c, s], lsem.at[4]),
    ]
    wi_local = [
        pltpu.make_async_copy(
            wi_in.at[:, rows(4 * i + s, 128)], WI.at[rows(4 * g + s, 32), pl.ds(128 * i, 128)], lsem.at[5]
        )
        for i in range(8)
    ]
    for cp in local + wi_local:
        cp.start()
    pl.semaphore_wait(bar, 7)

    for j in (1, 2, 3):
        send(pack, PK.at[z, c, s], ps.at[T_PACK, j - 1], pr.at[T_PACK, j - 1], peer(j))
    for j in (1, 2, 3):
        send(
            wq_in.at[:, rows(rank[j], 768)], WQ.at[rows(4 * g + s, 32)],
            ps.at[T_WQ, j - 1], pr.at[T_WQ, j - 1], peer(j),
        )

    inner = jnp.logical_and(z >= 1, z <= 2)
    outer = jnp.logical_or(z == 0, z == 3)

    def both(p, q):
        return q if p is None else jnp.logical_and(p, q)

    def zag_start(tag, own, cond=None):
        for di, d in ((2, 2), (3, -2), (0, 1), (1, -1)):
            send_if(both(cond, has(d)), own, own, zs.at[tag, di], zr.at[tag, z], up(d))

    def core_send(tag, o, ref):
        return rc(ref, ref, cs.at[tag, o], cr.at[tag, o], partner)

    def take(tag, o, chunk, core):
        got(chunk(o, c), zr.at[tag, o])
        if core:
            core_send(tag, o, chunk(o, c)).start()

    def zag_relay(tag, chunk, core=True):
        for at, o, d in ((2, 0, 1), (1, 3, -1)):
            @pl.when(z == at)
            def _():
                got(chunk(o, c), zr.at[tag, o])

            send_if(z == at, chunk(o, c), chunk(o, c), zs.at[tag, 4], zr.at[tag, o], up(d))

            @pl.when(z == at)
            def _():
                if core:
                    core_send(tag, o, chunk(o, c)).start()

    def zag_near(tag, chunk, core=True):
        for d in (1, -1, 2, -2):
            for o in range(PLANES):
                at = o + d
                if 0 <= at < PLANES and (at, o) not in ((2, 0), (1, 3)):
                    @pl.when(z == at)
                    def _():
                        take(tag, o, chunk, core)

    def zag_far(tag, chunk, core=True):
        for o, at in ((0, 3), (3, 0)):
            @pl.when(z == at)
            def _():
                take(tag, o, chunk, core)

    def zag_core(tag, chunk):
        for o in range(PLANES):
            got(chunk(o, 1 - c), cr.at[tag, o])

        def drain():
            for o in range(PLANES):
                core_send(tag, o, chunk(o, c)).wait_send()

        drains.append(drain)

    def ck_wo(o, cc):
        return WO.at[o, cc, s]

    def ck_pk(o, cc):
        return PK.at[o, cc]

    def ck(ref):
        return lambda o, cc: ref.at[rows(2 * o + cc, 128)]

    ck_wq, ck_wi, ck_wb = ck(WQ), ck(WI), ck(WB)

    for cp in local:
        cp.wait()
    zag_start(A_WO, WO.at[z, c, s])
    for j in (1, 2, 3):
        for i in range(8):
            send(
                wi_in.at[:, rows(4 * i + rank[j], 128)],
                WI.at[rows(4 * g + s, 32), pl.ds(128 * i, 128)],
                ps.at[T_WI, j - 1], pr.at[T_WI, j - 1], peer(j),
            )
            drains.pop()

    def drain_wi():
        for j in (1, 2, 3):
            blk = WI.at[rows(4 * g + s, 32)]
            rc(blk, blk, ps.at[T_WI, j - 1], pr.at[T_WI, j - 1], peer(j)).wait_send()

    drains.append(drain_wi)
    for j in (1, 2, 3):
        send(x_in, X.at[rows(s, 128)], ps.at[T_TOK, j - 1], pr.at[T_TOK, j - 1], peer(j))
    for j in (1, 2, 3):
        got(WQ.at[rows(4 * g + rank[j], 32)], pr.at[T_WQ, j - 1])
    zag_start(A_WQ, ck_wq(z, c))
    core_send(A_WQ, z, ck_wq(z, c)).start()
    for j in (1, 2, 3):
        got(PK.at[z, c, rank[j]], pr.at[T_PACK, j - 1])
    zag_start(A_PACK, PK.at[z, c])
    core_send(A_PACK, z, PK.at[z, c]).start()
    for j in (1, 2, 3):
        got(WI.at[rows(4 * g + rank[j], 32)], pr.at[T_WI, j - 1])
    for cp in wi_local:
        cp.wait()
    core_send(A_WI, z, ck_wi(z, c)).start()
    core_send(A_WB, z, ck_wb(z, c)).start()
    zag_start(A_WI, ck_wi(z, c), outer)
    zag_start(A_WB, ck_wb(z, c), outer)
    zag_relay(A_WO, ck_wo, core=False)
    zag_relay(A_WQ, ck_wq)
    zag_relay(A_PACK, ck_pk)
    zag_start(A_WI, ck_wi(z, c), inner)
    zag_near(A_WO, ck_wo, core=False)
    zag_far(A_WO, ck_wo, core=False)
    for j in (1, 2, 3):
        send(WO.at[:, c, s], WO.at[:, c, s], ps.at[T_WO, j - 1], pr.at[T_WO, j - 1], peer(j))
    zag_near(A_WQ, ck_wq)
    zag_far(A_WQ, ck_wq)
    zag_near(A_PACK, ck_pk)
    zag_far(A_PACK, ck_pk)
    zag_core(A_PACK, ck_pk)
    for gg in range(8):
        tot = PK[gg // 2, gg % 2, 0]
        for r in (1, 2, 3):
            tot = tot + PK[gg // 2, gg % 2, r]
        VEC[:, gg * 128 : (gg + 1) * 128] = tot
        IB[:, gg * 128 : (gg + 1) * 128] = PK[gg // 2, gg % 2, s]
    for cc in range(2):
        tot = PK[s, cc, 0]
        for r in (1, 2, 3):
            tot = tot + PK[s, cc, r]
        for k in range(3):
            BQ[0:1, (3 * cc + k) * 128 : (3 * cc + k + 1) * 128] = tot[k : k + 1, :]
    for j in (1, 2, 3):
        got(X.at[rows(rank[j], 128)], pr.at[T_TOK, j - 1])
    zag_core(A_WQ, ck_wq)

    def qkv(t, carry):
        cols = rows(t, 256)
        MIX[:, cols] = (dot_nn(X[...], WQ[:, cols]) + BQ[0:1, cols]).astype(BF)
        return carry

    lax.fori_loop(0, 3, qkv, 0)

    factor = 1.0 / math.sqrt(HD)

    def attend(n, carry):
        rr = rows(n, 256)
        ok = lax.broadcasted_iota(jnp.int32, (1, 256), 1) < lens[n]
        outs = []
        for i in range(4):
            q = MIX[rr, 192 * i : 192 * i + 64]
            k = MIX[rr, 192 * i + 64 : 192 * i + 128]
            v = MIX[rr, 192 * i + 128 : 192 * i + 192]
            sc = jnp.where(ok, dot_nt(q, k) * factor, -1e30)
            e = jnp.exp(sc - jnp.max(sc, axis=-1, keepdims=True))
            p = e * (1.0 / jnp.sum(e, axis=-1, keepdims=True))
            PROB[n, i] = p
            outs.append(dot_nn(p.astype(BF), v).astype(BF))
        CTX[rr, 0:128] = jnp.concatenate(outs[:2], axis=1)
        CTX[rr, 128:256] = jnp.concatenate(outs[2:], axis=1)
        return carry

    lax.fori_loop(0, 1, attend, 0)
    zag_relay(A_WI, ck_wi)
    zag_start(A_WB, ck_wb(z, c), inner)
    lax.fori_loop(1, 2, attend, 0)
    for j in (3, 1, 2):
        send(
            CTX.at[rows(rank[j], 128)], CTXO.at[:, rows(s, 256)],
            ps.at[T_CTX, j - 1], pr.at[T_CTX, j - 1], peer(j),
        )
    CTXO[:, rows(s, 256)] = CTX[rows(s, 128), :]
    for j in (1, 2, 3):
        got(WO.at[:, c, rank[j]], pr.at[T_WO, j - 1])
    wo_cp = rc(WO.at[:, c], WO.at[:, c], cs.at[A_WO, 0], cr.at[A_WO, 0], partner)
    wo_cp.start()
    drains.append(lambda: rc(WO.at[:, c], WO.at[:, c], cs.at[A_WO, 0], cr.at[A_WO, 0], partner).wait_send())
    zag_near(A_WI, ck_wi)
    got(WO.at[:, 1 - c], cr.at[A_WO, 0])
    for j in (1, 2, 3):
        got(CTXO.at[:, rows(rank[j], 256)], pr.at[T_CTX, j - 1])

    def proj(t, carry):
        cols = rows(t, 256)
        w = WO[:, :, :, :, cols].reshape(1024, 256)
        XH1[:, cols] = x_in[:, cols].astype(F32) + (dot_nn(CTXO[...], w) + VEC[3:4, cols])
        return carry

    lax.fori_loop(0, 4, proj, 0)

    def norm_one(t, carry):
        rr = rows(t, 32)
        h = XH1[rr, :]
        ctr = h - jnp.mean(h, axis=-1, keepdims=True)
        rstd = lax.rsqrt(jnp.mean(ctr * ctr, axis=-1, keepdims=True) + NORM_EPS)
        xh = ctr * rstd
        nf = xh * VEC[4:5, :] + VEC[5:6, :]
        XH1[rr, :] = xh
        RS1[rr, :] = jnp.broadcast_to(rstd, (32, 128))
        NF[rr, :] = nf
        N[pl.ds(pl.multiple_of(s * 128 + t * 32, 32), 32), :] = nf.astype(BF)
        return carry

    lax.fori_loop(0, 4, norm_one, 0)
    me = rows(s, 128)
    for j in (3, 1, 2):
        send(N.at[me], N.at[me], ps.at[T_N, j - 1], pr.at[T_N, j - 1], peer(j))
    zag_far(A_WI, ck_wi)
    zag_core(A_WI, ck_wi)

    def ffn_in(rr):
        def body(t, carry):
            cols = rows(t, 256)
            pre = dot_nn(N[rr, :], WI[:, cols]) + IB[9:10, cols]
            cdf = 0.5 * (1.0 + lax.erf(pre * math.sqrt(0.5)))
            ACT[rr, cols] = (pre * cdf).astype(BF)
            DG[rr, cols] = cdf + pre * jnp.exp(-0.5 * (pre * pre)) * (1.0 / math.sqrt(2.0 * math.pi))
            return carry

        lax.fori_loop(0, 4, body, 0)

    def ffn_out(rr, j):
        def body(t, carry):
            cols = rows(t, 256)
            part = dot_nn(ACT[rr, :], WB[:, cols])
            if j == 0:
                OWN[:, cols] = part
            else:
                SB[j - 1, :, cols] = part.astype(BF)
            return carry

        lax.fori_loop(0, 4, body, 0)

    order = (1, 2, 3)
    ffn_in(me)
    zag_relay(A_WB, ck_wb)
    for j in order:
        rr = rows(rank[j], 128)
        got(N.at[rr], pr.at[T_N, j - 1])
        ffn_in(rr)
    zag_near(A_WB, ck_wb)
    zag_far(A_WB, ck_wb)
    zag_core(A_WB, ck_wb)
    for j in (3, 1, 2):
        ffn_out(rows(rank[j], 128), j)
        send(SB.at[j - 1], RB.at[j - 1], ps.at[T_RSF, j - 1], pr.at[T_RSF, j - 1], peer(j))
    ffn_out(me, 0)
    for j in (1, 2, 3):
        got(RB.at[j - 1], pr.at[T_RSF, j - 1])

    GV[...] = jnp.zeros_like(GV)

    def norm_two(t, carry):
        rr = rows(t, 32)
        h = OWN[rr, :] + RB[0, rr, :].astype(F32) + RB[1, rr, :].astype(F32) + RB[2, rr, :].astype(F32)
        h = NF[rr, :] + (h + VEC[6:7, :])
        ctr = h - jnp.mean(h, axis=-1, keepdims=True)
        rstd = lax.rsqrt(jnp.mean(ctr * ctr, axis=-1, keepdims=True) + NORM_EPS)
        xh = ctr * rstd
        out_o[rr, :] = (xh * VEC[7:8, :] + VEC[8:9, :]).astype(BF)
        place = (s % 2) * 128 + t * 32 + lax.broadcasted_iota(jnp.int32, (32, 1), 0)
        seed = jnp.where(place < lens[s // 2], cot[rr, :].astype(F32), 0.0)
        GV[7:8, :] += jnp.sum(seed * xh, axis=0, keepdims=True)
        GV[8:9, :] += jnp.sum(seed, axis=0, keepdims=True)
        u = seed * VEC[7:8, :]
        gs = rstd * (u - jnp.mean(u, axis=-1, keepdims=True) - xh * jnp.mean(u * xh, axis=-1, keepdims=True))
        GV[6:7, :] += jnp.sum(gs, axis=0, keepdims=True)
        GS[rr, :] = gs
        G[pl.ds(pl.multiple_of(s * 128 + t * 32, 32), 32), :] = gs.astype(BF)
        return carry

    lax.fori_loop(0, 4, norm_two, 0)
    for j in (3, 1, 2):
        send(G.at[me], G.at[me], ps.at[T_G, j - 1], pr.at[T_G, j - 1], peer(j))

    def bwd_act(rr):
        def body(t, carry):
            cols = rows(t, 256)
            gp = dot_nt(G[rr, :], WB[cols, :]) * DG[rr, cols]
            GV[9:10, cols] += jnp.sum(gp, axis=0, keepdims=True)
            GPB[rr, cols] = gp.astype(BF)
            return carry

        lax.fori_loop(0, 4, body, 0)

    def bwd_in(rr, j):
        def body(t, carry):
            cols = rows(t, 256)
            part = dot_nt(GPB[rr, :], WI[cols, :])
            if j == 0:
                OWN[:, cols] = part
            else:
                SB2[j - 1, :, cols] = part.astype(BF)
            return carry

        lax.fori_loop(0, 4, body, 0)

    bwd_act(me)
    bwd_in(me, 0)
    for j in order:
        rr = rows(rank[j], 128)
        got(G.at[rr], pr.at[T_G, j - 1])
        bwd_act(rr)
        bwd_in(rr, j)
        send(SB2.at[j - 1], RB2.at[j - 1], ps.at[T_RSB, j - 1], pr.at[T_RSB, j - 1], peer(j))

    def wgrad(lhs, rhs, mine, csend, cols):
        def body(t, carry):
            ACC[:, 0:cols] = dot_tn(lhs[:, rows(t, 256)], rhs[...])
            mine[t] = ACC[rows(c, 128), 0:cols]
            csend[t] = ACC[rows(1 - c, 128), 0:cols].astype(BF)
            return carry

        lax.fori_loop(0, 4, body, 0)

    def core_start(tag, csend, crecv):
        send(csend, crecv, cs2.at[tag], cr2.at[tag], partner)

    def core_sum(tag, mine, crecv, zsend):
        got(crecv, cr2.at[tag])

        def body(t, carry):
            v = mine[t] + crecv[t].astype(F32)
            mine[t] = v
            zsend[t] = v.astype(BF)
            return carry

        lax.fori_loop(0, 4, body, 0)

    def zrs_start(tag, zsend, zrecv, relay):
        send_if(z == 0, zsend.at[3], relay, zs2.at[tag, 4], zr2.at[tag, 4], up(1))
        send_if(z == 3, zsend.at[0], relay, zs2.at[tag, 4], zr2.at[tag, 4], up(-1))
        for di, d, late in ((2, 2, 1), (3, -2, 2), (0, 1, 9), (1, -1, 9)):
            send_if(
                jnp.logical_and(has(d), z != late),
                zsend.at[jnp.clip(z + d, 0, 3)], zrecv.at[z], zs2.at[tag, di], zr2.at[tag, z], up(d),
            )

    def zrs_relay(tag, mine, zsend, zrecv, relay):
        for at, far, di, d in ((1, 3, 2, 2), (2, 0, 3, -2)):
            @pl.when(z == at)
            def _():
                got(relay, zr2.at[tag, 4])
                zsend[far] = (mine[far] + relay[...].astype(F32)).astype(BF)

            send_if(z == at, zsend.at[far], zrecv.at[z], zs2.at[tag, di], zr2.at[tag, z], up(d))

    def zrs_end(tag, mine, zrecv, res):
        res[...] = mine[z]
        for o in range(PLANES):
            @pl.when(jnp.logical_and(z != o, jnp.logical_and(z - o <= 2, o - z <= 2)))
            def _():
                got(zrecv.at[o], zr2.at[tag, o])
                res[...] += zrecv[o].astype(F32)

    wgrad(ACT, G, mB, csB, 1024)
    core_start(R_GB, csB, crB)
    wgrad(N, GPB, mI, csI, 1024)
    core_start(R_GI, csI, crI)
    core_sum(R_GB, mB, crB, zsB)
    zrs_start(R_GB, zsB, zrB, rlB)
    for j in (1, 2, 3):
        got(RB2.at[j - 1], pr.at[T_RSB, j - 1])

    def norm_one_bwd(t, carry):
        rr = rows(t, 32)
        gn = OWN[rr, :] + RB2[0, rr, :].astype(F32) + RB2[1, rr, :].astype(F32) + RB2[2, rr, :].astype(F32)
        gn = GS[rr, :] + gn
        xh = XH1[rr, :]
        GV[4:5, :] += jnp.sum(gn * xh, axis=0, keepdims=True)
        GV[5:6, :] += jnp.sum(gn, axis=0, keepdims=True)
        u = gn * VEC[4:5, :]
        gf = RS1[rr, 0:1] * (
            u - jnp.mean(u, axis=-1, keepdims=True) - xh * jnp.mean(u * xh, axis=-1, keepdims=True)
        )
        GV[3:4, :] += jnp.sum(gf, axis=0, keepdims=True)
        GF[rr, :] = gf
        GFB[rr, :] = gf.astype(BF)
        return carry

    lax.fori_loop(0, 4, norm_one_bwd, 0)

    def gctx(t, carry):
        w = WO[t].reshape(256, 1024)
        GCS[t] = dot_nt(GFB[...], w).astype(BF)
        return carry

    lax.fori_loop(0, 4, gctx, 0)
    for j in (3, 1, 2):
        send(GCS.at[rank[j]], GC.at[me], ps.at[T_GC, j - 1], pr.at[T_GC, j - 1], peer(j))
    GC[me, :] = GCS[s]
    core_sum(R_GI, mI, crI, zsI)
    zrs_start(R_GI, zsI, zrI, rlI)
    wgrad(CTXO, GFB, mO, csO, 1024)
    core_start(R_GO, csO, crO)
    zrs_relay(R_GB, mB, zsB, zrB, rlB)
    for j in (1, 2, 3):
        got(GC.at[rows(rank[j], 128)], pr.at[T_GC, j - 1])

    got(crO, cr2.at[R_GO])

    def go_core(t, carry):
        v = mO[t] + crO[t].astype(F32)
        mO[t] = v
        for r in range(4):
            psO[r, t] = v[32 * r : 32 * r + 32, :].astype(BF)
        return carry

    lax.fori_loop(0, 4, go_core, 0)
    for j in (1, 2, 3):
        send(psO.at[rank[j]], prO.at[j - 1], ps.at[T_GO, j - 1], pr.at[T_GO, j - 1], peer(j))

    GQS = jnp.zeros((1, 768), F32)
    BQ[...] = jnp.zeros_like(BQ)

    def attend_bwd(n, carry):
        rr = rows(n, 256)
        for pair in range(2):
            parts = []
            for i in (2 * pair, 2 * pair + 1):
                q = MIX[rr, 192 * i : 192 * i + 64]
                k = MIX[rr, 192 * i + 64 : 192 * i + 128]
                v = MIX[rr, 192 * i + 128 : 192 * i + 192]
                gc = GC[rr, 64 * i : 64 * i + 64]
                p = PROB[n, i]
                gp = dot_nt(gc, v)
                inner = jnp.sum(p * gp, axis=-1, keepdims=True)
                gsc = (p * (gp - inner) * factor).astype(BF)
                parts += [dot_nn(gsc, k), dot_tn(gsc, q), dot_tn(p.astype(BF), gc)]
            both = jnp.concatenate([x.astype(BF) for x in parts], axis=1)
            GM[rr, 384 * pair : 384 * pair + 384] = both
            BQ[0:1, 384 * pair : 384 * pair + 384] += jnp.sum(both.astype(F32), axis=0, keepdims=True)
        return carry

    lax.fori_loop(0, 2, attend_bwd, 0)
    zrs_relay(R_GI, mI, zsI, zrI, rlI)
    for k in range(6):
        GV[k % 3 : k % 3 + 1, rows(2 * s + k // 3, 128)] = BQ[0:1, 128 * k : 128 * k + 128]
    for gg in range(8):
        GVC[gg % 2, gg // 2] = GV[:, 128 * gg : 128 * gg + 128]
    send(GVC.at[1 - c], RVC, cs2.at[4], cr2.at[4], partner)
    wgrad(X, GM, mQ, csQ, 768)
    core_start(R_GQ, csQ, crQ)
    got(RVC, cr2.at[4])
    TVZ[...] = GVC[c] + RVC[...]
    for k in (1, 2, 3):
        t = (z + k) % 4
        send(TVZ.at[t], RVZ.at[k - 1], zs3.at[k - 1], zr3.at[k - 1], (2 * t + c, s))

    for j in (1, 2, 3):
        got(prO.at[j - 1], pr.at[T_GO, j - 1])

    def go_plane(t, carry):
        v = mO[t, rows(s, 32), :]
        for j in (1, 2, 3):
            v = v + prO[j - 1, t].astype(F32)
        zO[t] = v
        zsO[t] = v.astype(BF)
        return carry

    lax.fori_loop(0, 4, go_plane, 0)
    core_sum(R_GQ, mQ, crQ, zsQ)
    zrs_start(R_GQ, zsQ, zrQ, rlQ)
    zrs_start(R_GO, zsO, zrO, rlO)

    def gtok(rr, j):
        def body(t, carry):
            cols = rows(t, 256)
            part = dot_nt(GM[rr, :], WQ[cols, :])
            if j == 0:
                OWN[:, cols] = part
            else:
                SB3[j - 1, :, cols] = part.astype(BF)
            return carry

        lax.fori_loop(0, 4, body, 0)

    for j in (3, 1, 2):
        gtok(rows(rank[j], 128), j)
        send(SB3.at[j - 1], RB3.at[j - 1], ps.at[T_GT, j - 1], pr.at[T_GT, j - 1], peer(j))
    gtok(me, 0)

    zrs_relay(R_GQ, mQ, zsQ, zrQ, rlQ)
    zrs_relay(R_GO, zO, zsO, zrO, rlO)
    zrs_end(R_GB, mB, zrB, gb_o)
    zrs_end(R_GI, mI, zrI, resI)
    for j in (1, 2, 3):
        siI[j - 1] = resI[rows(rank[j], 32), :].astype(BF)
    for j in (1, 2, 3):
        send(siI.at[j - 1], riI.at[j - 1], ps.at[T_GI, j - 1], pr.at[T_GI, j - 1], peer(j))
    for k in (1, 2, 3):
        got(RVZ.at[k - 1], zr3.at[k - 1])
    PV[...] = TVZ[z] + RVZ[0] + RVZ[1] + RVZ[2]
    for j in (1, 2, 3):
        send(PV, RVP.at[j - 1], ps.at[T_SV, j - 1], pr.at[T_SV, j - 1], peer(j))
    for j in (1, 2, 3):
        got(RB3.at[j - 1], pr.at[T_GT, j - 1])

    def gtok_sum(t, carry):
        rr = rows(t, 32)
        h = OWN[rr, :] + RB3[0, rr, :].astype(F32) + RB3[1, rr, :].astype(F32) + RB3[2, rr, :].astype(F32)
        gtok_o[rr, :] = GF[rr, :] + h
        return carry

    lax.fori_loop(0, 4, gtok_sum, 0)
    zrs_end(R_GQ, mQ, zrQ, resQ)
    for j in (1, 2, 3):
        siQ[j - 1] = resQ[rows(rank[j], 32), :].astype(BF)
    for j in (1, 2, 3):
        send(siQ.at[j - 1], riQ.at[j - 1], ps.at[T_GQ, j - 1], pr.at[T_GQ, j - 1], peer(j))
    zrs_end(R_GO, zO, zrO, go_o)
    for i in range(8):
        gi_o[:, rows(4 * i + s, 128)] = resI[rows(s, 32), 128 * i : 128 * i + 128]
    gq_o[:, rows(s, 768)] = resQ[rows(s, 32), :]
    for j in (1, 2, 3):
        got(riI.at[j - 1], pr.at[T_GI, j - 1])
        for i in range(8):
            gi_o[:, rows(4 * i + rank[j], 128)] = riI[j - 1, :, 128 * i : 128 * i + 128].astype(F32)
    for j in (1, 2, 3):
        got(RVP.at[j - 1], pr.at[T_SV, j - 1])
    tot = PV[...] + RVP[0] + RVP[1] + RVP[2]
    row = lax.broadcasted_iota(jnp.int32, (16, 128), 0)
    sv_o[...] = jnp.where(row == 9, PV[...], tot)
    for j in (1, 2, 3):
        got(riQ.at[j - 1], pr.at[T_GQ, j - 1])
        gq_o[:, rows(rank[j], 768)] = riQ[j - 1].astype(F32)
    for drain in drains:
        drain()


def hand_over(*refs):
    sources, sums, targets = refs[:6], refs[6], refs[7:]
    s = lax.axis_index("seq")
    for src, dst in zip(sources, targets[:6]):
        dst[...] = src[...]
    qv, ob, g1, b1, ib, bb, g2, b2 = targets[6:]
    turned = pltpu.roll(sums[...], (128 - 32 * s) % 128, 1)
    for k, ref in ((3, ob), (4, g1), (5, b1), (6, bb), (7, g2), (8, b2)):
        ref[...] = turned[k : k + 1, 0:32]
    ib[...] = sums[9:10, :]
    line = jnp.where(s == 0, sums[0:1, :], jnp.where(s == 3, sums[2:3, :], sums[1:2, :]))
    qv[...] = jnp.where(s // 2 == 0, line[:, 0:64], line[:, 64:128])


def fused_shards(
    tokens, cotangent, slot_lengths, w_qkv, qv_bias, w_out, out_bias, ln1_gain, ln1_bias,
    w_in, in_bias, w_back, back_bias, ln2_gain, ln2_bias,
):
    vm = pltpu.VMEM
    dma = pltpu.SemaphoreType.DMA

    def item(n):
        return [
            vm((4, 128, n), F32), vm((4, 128, n), BF), vm((4, 128, n), BF),
            vm((4, 128, n), BF), vm((4, 128, n), BF), vm((128, n), BF),
        ]

    scratch = [
        vm((16, 128), F32), vm((512, 1024), BF), vm((1024, 768), BF), vm((1024, 1024), BF), vm((1024, 1024), BF),
        vm((4, 2, 4, 32, 1024), BF), vm((4, 2, 4, 16, 128), F32), vm((16, 1024), F32), vm((16, 1024), F32),
        vm((8, 768), F32),
        vm((512, 768), BF), vm((2, 4, 256, 256), F32), vm((512, 256), BF), vm((128, 1024), BF),
        vm((128, 1024), F32), vm((128, 1024), F32), vm((128, 128), F32), vm((512, 1024), BF),
        vm((512, 1024), F32), vm((512, 1024), BF), vm((3, 128, 1024), BF), vm((3, 128, 1024), BF),
        vm((128, 1024), F32),
        vm((512, 1024), BF), vm((128, 1024), F32), vm((512, 1024), BF), vm((3, 128, 1024), BF),
        vm((3, 128, 1024), BF), vm((128, 1024), F32), vm((128, 1024), BF), vm((4, 128, 256), BF),
        vm((512, 256), BF), vm((512, 768), BF), vm((3, 128, 1024), BF), vm((3, 128, 1024), BF),
        vm((256, 1024), F32),
    ]
    scratch += item(1024) + item(1024) + item(768)
    scratch += [
        vm((4, 128, 1024), BF), vm((4, 128, 1024), BF), vm((4, 128, 1024), F32),
        vm((4, 4, 32, 1024), BF), vm((3, 4, 32, 1024), BF), vm((4, 32, 1024), F32),
        vm((4, 32, 1024), BF), vm((4, 32, 1024), BF), vm((32, 1024), BF),
        vm((3, 32, 1024), BF), vm((3, 32, 1024), BF), vm((3, 32, 768), BF), vm((3, 32, 768), BF),
        vm((128, 1024), F32), vm((128, 768), F32),
        vm((16, 1024), F32), vm((2, 4, 16, 128), F32), vm((4, 16, 128), F32), vm((4, 16, 128), F32),
        vm((3, 16, 128), F32), vm((16, 128), F32), vm((3, 16, 128), F32),
        dma((8,)), dma((16, 3)), dma((16, 3)), dma((5, 5)), dma((5, 4)), dma((5, 4)), dma((5, 4)),
        dma((4, 5)), dma((4, 5)), dma((5,)), dma((5,)), dma((3,)), dma((3,)),
    ]
    full = pl.BlockSpec(memory_space=pltpu.VMEM)
    shapes = [
        ((128, 1024), BF), ((128, 1024), F32), ((32, 3072), F32), ((32, 1024), F32),
        ((32, 4096), F32), ((128, 1024), F32), ((16, 128), F32),
    ]
    smem = pl.BlockSpec(memory_space=pltpu.SMEM)
    small = [v.reshape(1, -1) for v in (qv_bias, out_bias, ln1_gain, ln1_bias, in_bias, back_bias, ln2_gain, ln2_bias)]
    results = pl.pallas_call(
        layer_kernel,
        out_shape=[jax.ShapeDtypeStruct(a, b) for a, b in shapes],
        in_specs=[full] * 6 + [smem] + [full] * 8,
        out_specs=[full] * 7,
        scratch_shapes=scratch,
        compiler_params=pltpu.CompilerParams(
            collective_id=0, has_side_effects=True, vmem_limit_bytes=67_000_000
        ),
        name="encoder_layer",
    )(tokens, cotangent, w_qkv, w_out, w_in, w_back, slot_lengths, *small)
    lengths = (64, 32, 32, 32, 128, 32, 32, 32)
    final = pl.pallas_call(
        hand_over,
        out_shape=[jax.ShapeDtypeStruct(a, b) for a, b in shapes[:6]]
        + [jax.ShapeDtypeStruct((1, n), F32) for n in lengths],
        in_specs=[full] * 7,
        out_specs=[full] * 14,
        name="hand_over",
    )(*results)
    output, grad_tokens, grad_qkv, grad_wo, grad_wi, grad_wb = final[:6]
    qv, ob, g1, b1, ib, bb, g2, b2 = [v.reshape(-1) for v in final[6:]]
    return (output, grad_tokens, grad_qkv, qv, grad_wo, ob, g1, b1, grad_wi, ib, grad_wb, bb, g2, b2)


def solution(mesh):
    placed = (
        P(("grp", "seq"), None),
        P(("grp", "seq"), None),
        P("grp"),
        P(("grp", "seq"), None),
        P(("grp", "seq")),
        P(("grp", "seq"), None),
        P(("grp", "seq")),
        P(("grp", "seq")),
        P(("grp", "seq")),
        P(("grp", "seq"), None),
        P(("grp", "seq")),
        P(("grp", "seq"), None),
        P(("grp", "seq")),
        P(("grp", "seq")),
        P(("grp", "seq")),
    )
    fused = mesh.shape["grp"] == 2 * PLANES and mesh.shape["seq"] == RANKS
    return jax.shard_map(
        fused_shards if fused else shards,
        mesh=mesh,
        in_specs=placed,
        out_specs=(
            P(("grp", "seq"), None),
            P(("grp", "seq"), None),
            P(("grp", "seq"), None),
            P(("grp", "seq")),
            P(("grp", "seq"), None),
            P(("grp", "seq")),
            P(("grp", "seq")),
            P(("grp", "seq")),
            P(("grp", "seq"), None),
            P(("grp", "seq")),
            P(("grp", "seq"), None),
            P(("grp", "seq")),
            P(("grp", "seq")),
            P(("grp", "seq")),
        ),
        check_vma=False,
    )
```

```python
from functools import partial
import math

import jax
import jax.numpy as jnp
from jax import lax
from jax.experimental import pallas as pl
from jax.experimental.pallas import tpu as pltpu
from jax.sharding import PartitionSpec as P

D = 1024
H = 16
HD = 64
SLOT_DEV = 64
SLOTS = 2


NORM_EPS = 1e-06


def layer_norm(hidden, gain, shift):
    center = hidden - jnp.mean(hidden, axis=-1, keepdims=True)
    spread = jnp.mean(center * center, axis=-1, keepdims=True)
    return center * lax.rsqrt(spread + NORM_EPS) * gain + shift


def exact_gelu(values):
    return jax.nn.gelu(values, approximate=False)


def full_bias(pair_bias):
    pairs = pair_bias.reshape(H, 2, HD)
    return jnp.stack([pairs[:, 0], jnp.zeros_like(pairs[:, 0]), pairs[:, 1]], axis=1).reshape(3 * D)


def contract_rows(left, right):
    return lax.dot_general(
        left, right, (((0,), (0,)), ((), ())), preferred_element_type=jnp.float32
    )


def contract_cols(left, right):
    return lax.dot_general(
        left, right, (((1,), (1,)), ((), ())), preferred_element_type=jnp.float32
    )


def slot_scores(mixed, length, factor):
    slot_width = mixed.shape[0]
    queries = mixed[:, :, 0]
    key_rows = mixed[:, :, 1]
    value_rows = mixed[:, :, 2]
    products = jnp.einsum("qhd,khd->hqk", queries, key_rows, preferred_element_type=jnp.float32)
    key_valid = (jnp.arange(slot_width) < length)[None, None, :]
    scores = jnp.where(key_valid, products * factor, -1e30)
    return (queries, key_rows, value_rows, scores)


def slot_forward(item, factor):
    mixed, length = item
    queries, key_rows, value_rows, scores = slot_scores(mixed, length, factor)
    row_max = jnp.max(scores, axis=-1, keepdims=True)
    expon = jnp.exp(scores - row_max)
    total = jnp.sum(expon, axis=-1, keepdims=True)
    probs = expon / total
    context = jnp.einsum(
        "hqk,khd->qhd", probs.astype(jnp.bfloat16), value_rows, preferred_element_type=jnp.float32
    )
    return (context.astype(jnp.bfloat16), row_max + jnp.log(total))


def slot_backward(item, factor):
    mixed, grad_context, log_total, length = item
    queries, key_rows, value_rows, scores = slot_scores(mixed, length, factor)
    probs = jnp.exp(scores - log_total)
    grad_probs = jnp.einsum(
        "qhd,khd->hqk", grad_context, value_rows, preferred_element_type=jnp.float32
    )
    inner = jnp.sum(probs * grad_probs, axis=-1, keepdims=True)
    grad_scores = (probs * (grad_probs - inner) * factor).astype(jnp.bfloat16)
    grad_queries = jnp.einsum(
        "hqk,khd->qhd", grad_scores, key_rows, preferred_element_type=jnp.float32
    )
    grad_keys = jnp.einsum("hqk,qhd->khd", grad_scores, queries, preferred_element_type=jnp.float32)
    grad_values = jnp.einsum(
        "hqk,qhd->khd", probs.astype(jnp.bfloat16), grad_context, preferred_element_type=jnp.float32
    )
    return jnp.stack([grad_queries, grad_keys, grad_values], axis=2).astype(jnp.bfloat16)


def shards(
    tokens,
    cotangent,
    slot_lengths,
    w_qkv,
    qv_bias,
    w_out,
    out_bias,
    ln1_gain,
    ln1_bias,
    w_in,
    in_bias,
    w_back,
    back_bias,
    ln2_gain,
    ln2_bias,
):
    seq_count = lax.axis_size("seq")
    local_rows = tokens.shape[0]
    slot_width = SLOT_DEV * seq_count
    heads_here = H // seq_count
    factor = 1.0 / math.sqrt(HD)
    full_qkv, full_qv, full_out, full_obias, gain_one, shift_one = (
        lax.all_gather(w_qkv, ("grp", "seq"), axis=0, tiled=True),
        lax.all_gather(qv_bias, ("grp", "seq"), axis=0, tiled=True),
        lax.all_gather(w_out, ("grp", "seq"), axis=0, tiled=True),
        lax.all_gather(out_bias, ("grp", "seq"), axis=0, tiled=True),
        lax.all_gather(ln1_gain, ("grp", "seq"), axis=0, tiled=True),
        lax.all_gather(ln1_bias, ("grp", "seq"), axis=0, tiled=True),
    )
    full_in, full_ibias, full_back, full_bbias, gain_two, shift_two = (
        lax.all_gather(w_in, ("grp", "seq"), axis=0, tiled=True),
        lax.all_gather(in_bias, ("grp", "seq"), axis=0, tiled=True),
        lax.all_gather(w_back, ("grp", "seq"), axis=0, tiled=True),
        lax.all_gather(back_bias, ("grp", "seq"), axis=0, tiled=True),
        lax.all_gather(ln2_gain, ("grp", "seq"), axis=0, tiled=True),
        lax.all_gather(ln2_bias, ("grp", "seq"), axis=0, tiled=True),
    )
    mixed = (
        jnp.dot(tokens, full_qkv, preferred_element_type=jnp.float32) + full_bias(full_qv)
    ).astype(jnp.bfloat16)
    gathered = lax.all_to_all(mixed, "seq", split_axis=1, concat_axis=0, tiled=True)
    per_slot = gathered.reshape(SLOTS, slot_width, heads_here, 3, HD)
    contexts, log_totals = lax.map(partial(slot_forward, factor=factor), (per_slot, slot_lengths))
    context_heads = contexts.reshape(SLOTS * slot_width, heads_here * HD)
    context = lax.all_to_all(context_heads, "seq", split_axis=0, concat_axis=1, tiled=True)
    attended = jnp.dot(context, full_out, preferred_element_type=jnp.float32) + full_obias
    first_in = tokens.astype(jnp.float32) + attended
    normed, norm_one_pull = jax.vjp(layer_norm, first_in, gain_one, shift_one)
    normed_low = normed.astype(jnp.bfloat16)
    pre_act = jnp.dot(normed_low, full_in, preferred_element_type=jnp.float32) + full_ibias
    activated, gelu_pull = jax.vjp(exact_gelu, pre_act)
    act_low = activated.astype(jnp.bfloat16)
    ffn_out = jnp.dot(act_low, full_back, preferred_element_type=jnp.float32) + full_bbias
    output, norm_two_pull = jax.vjp(layer_norm, normed + ffn_out, gain_two, shift_two)
    row_index = lax.axis_index("seq") * local_rows + jnp.arange(local_rows)
    slot_index = row_index // slot_width
    place = row_index % slot_width
    row_length = jnp.sum(
        jnp.where(slot_index[:, None] == jnp.arange(SLOTS)[None, :], slot_lengths[None, :], 0),
        axis=1,
    )
    row_valid = (place < row_length).astype(jnp.float32)
    seed_grad = cotangent.astype(jnp.float32) * row_valid[:, None]
    grad_second, grad_gain_two, grad_shift_two = norm_two_pull(seed_grad)
    grad_ffn_low = grad_second.astype(jnp.bfloat16)
    grad_back_w = contract_rows(act_low, grad_ffn_low)
    grad_back_b = jnp.sum(grad_second, axis=0)
    (grad_pre,) = gelu_pull(contract_cols(grad_ffn_low, full_back))
    grad_pre_low = grad_pre.astype(jnp.bfloat16)
    grad_in_w = contract_rows(normed_low, grad_pre_low)
    grad_in_b = jnp.sum(grad_pre, axis=0)
    grad_normed = grad_second + contract_cols(grad_pre_low, full_in)
    grad_first, grad_gain_one, grad_shift_one = norm_one_pull(grad_normed)
    grad_attn_low = grad_first.astype(jnp.bfloat16)
    grad_out_w = contract_rows(context, grad_attn_low)
    grad_out_b = jnp.sum(grad_first, axis=0)
    grad_context = contract_cols(grad_attn_low, full_out).astype(jnp.bfloat16)
    grad_heads = lax.all_to_all(grad_context, "seq", split_axis=1, concat_axis=0, tiled=True)
    grad_slots = grad_heads.reshape(SLOTS, slot_width, heads_here, HD)
    grad_mixed_heads = lax.map(
        partial(slot_backward, factor=factor), (per_slot, grad_slots, log_totals, slot_lengths)
    )
    grad_mixed = lax.all_to_all(
        grad_mixed_heads.reshape(SLOTS * slot_width, heads_here * 3 * HD),
        "seq",
        split_axis=0,
        concat_axis=1,
        tiled=True,
    )
    grad_qkv_w = contract_rows(tokens, grad_mixed)
    summed_bias = jnp.sum(grad_mixed.astype(jnp.float32), axis=0).reshape(H, 3, HD)
    grad_qv = jnp.stack([summed_bias[:, 0], summed_bias[:, 2]], axis=1).reshape(2 * D)
    input_grad = grad_first + contract_cols(grad_mixed, full_qkv)
    sums = (
        lax.psum_scatter(grad_qkv_w, ("grp", "seq"), scatter_dimension=0, tiled=True),
        lax.psum_scatter(grad_qv, ("grp", "seq"), scatter_dimension=0, tiled=True),
        lax.psum_scatter(grad_out_w, ("grp", "seq"), scatter_dimension=0, tiled=True),
        lax.psum_scatter(grad_out_b, ("grp", "seq"), scatter_dimension=0, tiled=True),
        lax.psum_scatter(
            grad_gain_one.astype(jnp.float32), ("grp", "seq"), scatter_dimension=0, tiled=True
        ),
        lax.psum_scatter(
            grad_shift_one.astype(jnp.float32), ("grp", "seq"), scatter_dimension=0, tiled=True
        ),
        lax.psum_scatter(grad_in_w, ("grp", "seq"), scatter_dimension=0, tiled=True),
        lax.psum_scatter(grad_in_b, ("grp", "seq"), scatter_dimension=0, tiled=True),
        lax.psum_scatter(grad_back_w, ("grp", "seq"), scatter_dimension=0, tiled=True),
        lax.psum_scatter(grad_back_b, ("grp", "seq"), scatter_dimension=0, tiled=True),
        lax.psum_scatter(
            grad_gain_two.astype(jnp.float32), ("grp", "seq"), scatter_dimension=0, tiled=True
        ),
        lax.psum_scatter(
            grad_shift_two.astype(jnp.float32), ("grp", "seq"), scatter_dimension=0, tiled=True
        ),
    )
    return (
        output.astype(jnp.bfloat16),
        input_grad,
        sums[0],
        sums[1],
        sums[2],
        sums[3],
        sums[4],
        sums[5],
        sums[6],
        sums[7],
        sums[8],
        sums[9],
        sums[10],
        sums[11],
    )


BF = jnp.bfloat16
F32 = jnp.float32
MESH = pl.DeviceIdType.MESH
PLANES = 4
RANKS = 4
(
    T_PACK, T_WQ, T_WI, T_TOK, T_WO, T_CTX, T_N, T_N2, T_RSF, T_RSF2, T_G, T_G2, T_RSB, T_RSB2,
    T_GC, T_GO, T_GT, T_GI, T_GQ, T_SV,
) = range(20)
(A_PACK, A_WO, A_WQ, A_WI, A_WB) = range(5)
(R_GB, R_GBL, R_GI, R_GO, R_GQ, R_SV) = range(6)


def dot_nn(a, b):
    return jnp.dot(a, b, preferred_element_type=F32)


def dot_nt(a, b):
    return lax.dot_general(a, b, (((1,), (1,)), ((), ())), preferred_element_type=F32)


def dot_tn(a, b):
    return lax.dot_general(a, b, (((0,), (0,)), ((), ())), preferred_element_type=F32)


def layer_kernel(
    x_in, cot_in, wq_in, wo_in, wi_in, wb_in, lens, *refs
):
    (
        small_in, (out_o, gtok_o, gq_o, go_o, gi_o, gb_o, sv_o), small,
        (
            pack, packf, cot, X, WQ, WI, WB, WO, PK, VEC, IB, BQ,
            MIX, PROB, CTX, CTXO, XH1, NF, RS1, N, DG, ACT, SB, RB, OWN,
            G, GS, GPB, SB2, RB2, GF, GFB, GCS, GC, GM, SB3, RB3,
            ACC,
            mB, csB, crB, zsB, zrB, rlB,
            mI, csI, crI, zsI, zrI, rlI,
            mQ, csQ, crQ, zsQ, zrQ, rlQ,
            csO, crO, mO, psO, prO, zO, zsO, zrO, rlO,
            siI, riI, siQ, riQ, resI, resQ,
            GV, GVC, RVC, TVZ, RVZ, PV, RVP,
            OUT, GTS, GQF, GOF, GIF, GBF,
            osem, ps, pr, zs, zr, cs, cr, cs2, cr2, zs2, zr2,
        ),
    ) = refs[:8], refs[8:15], refs[15:23], refs[23:]
    g = lax.axis_index("grp")
    s = lax.axis_index("seq")
    z = g // 2
    c = g % 2
    rank = {1: s + 1 - 2 * (s % 2), 2: (s + 2) % 4, 3: 3 - s}
    partner = (g + 1 - 2 * c, s)
    inner = jnp.logical_and(z >= 1, z <= 2)
    outer = jnp.logical_or(z == 0, z == 3)
    two_off, inward, outward = (z + 2) % 4, 1 + z % 2, 3 * (z // 2)
    pair, across, far_end = z + 1 - 2 * (z % 2), 2 - z // 2, 3 * (1 - z // 2)
    is_outer = (z // 2 + z % 2 + 1) % 2
    drains = []

    def peer(j):
        return (g, rank[j])

    def plane(t):
        return (2 * t + c, s)

    def rc(src, dst, ss, rs, dev):
        return pltpu.make_async_remote_copy(
            src_ref=src, dst_ref=dst, send_sem=ss, recv_sem=rs, device_id=dev, device_id_type=MESH
        )

    def got(dst, rs):
        rc(dst, dst, osem.at[0], rs, partner).wait_recv()

    def sent(src, ss):
        rc(src, src, ss, pr.at[0], partner).wait_send()

    def send(src, dst, ss, rs, dev):
        rc(src, dst, ss, rs, dev).start()
        drains.append(lambda: sent(src, ss))

    def spread(tag, pieces, total):
        for j, src, dst in pieces:
            rc(src, dst, ps.at[tag], pr.at[tag], peer(j)).start()
        drains.append(lambda: sent(total, ps.at[tag]))

    def put(src, dst, k):
        pltpu.make_async_copy(src, dst, osem.at[k]).start()
        drains.append(lambda: pltpu.make_async_copy(src, dst, osem.at[k]).wait())

    def rows(i, n):
        return pl.ds(pl.multiple_of(i * n, n), n)

    def size(n):
        return X.at[pl.ds(0, n)]

    bar = pltpu.get_barrier_semaphore()
    for j in (1, 2, 3):
        pl.semaphore_signal(bar, inc=1, device_id=peer(j), device_id_type=MESH)
    for k in (1, 2, 3):
        pl.semaphore_signal(bar, inc=1, device_id=plane((z + k) % 4), device_id_type=MESH)
    pl.semaphore_signal(bar, inc=1, device_id=partner, device_id_type=MESH)
    small_cp = [pltpu.make_async_copy(small_in[k], small[k], ps.at[8 + k]) for k in range(8)]
    for cp in small_cp:
        cp.start()
    wo_cp = pltpu.make_async_copy(wo_in, WO.at[z, c, s], osem.at[2])
    local = [
        pltpu.make_async_copy(wq_in.at[:, rows(s, 768)], WQ.at[rows(4 * g + s, 32)], osem.at[1]),
        pltpu.make_async_copy(x_in, X.at[rows(s, 128)], osem.at[0]),
        pltpu.make_async_copy(wb_in, WB.at[rows(g, 128)], osem.at[3]),
        pltpu.make_async_copy(cot_in, cot, osem.at[4]),
    ]
    for cp in [wo_cp] + local:
        cp.start()
    for i in range(8):
        pltpu.make_async_copy(
            wi_in.at[:, rows(4 * i + s, 128)], WI.at[rows(4 * g + s, 32), pl.ds(128 * i, 128)], osem.at[5]
        ).start()
    lane = lax.broadcasted_iota(jnp.int32, (1, 128), 1)
    for cp in small_cp:
        cp.wait()
    qv_in, ob_in, g1_in, b1_in, ib_in, bb_in, g2_in, b2_in = small
    packf[...] = jnp.zeros_like(packf)
    twice = jnp.concatenate([qv_in[...].astype(F32)] * 2, axis=1)
    for k in range(3):
        packf[k : k + 1, :] = jnp.where(lane // 64 + 4 * ((s + 1) // 2) == s // 2 + 4 * k, twice, 0.0)
    for k, ref in ((3, ob_in), (4, g1_in), (5, b1_in), (6, bb_in), (7, g2_in), (8, b2_in)):
        four = jnp.concatenate([ref[...].astype(F32)] * 4, axis=1)
        packf[k : k + 1, :] = jnp.where(lane // 32 == s, four, 0.0)
    packf[9:10, :] = ib_in[...].astype(F32)
    pack[...] = packf[...].astype(BF)
    PK[z, c, s] = pack[...]
    pl.semaphore_wait(bar, 7)

    def ck(ref):
        return lambda o, cc: ref.at[rows(2 * o + cc, 128)]

    chunk = {
        A_PACK: lambda o, cc: PK.at[o, cc],
        A_WO: lambda o, cc: WO.at[o, cc, s],
        A_WQ: ck(WQ),
        A_WI: ck(WI),
        A_WB: ck(WB),
    }
    chunks = {
        A_PACK: lambda n: PK.at[pl.ds(0, n), 0],
        A_WO: lambda n: size(32 * n),
        A_WQ: lambda n: WQ.at[pl.ds(0, 128 * n)],
        A_WI: lambda n: size(128 * n),
        A_WB: lambda n: size(128 * n),
    }

    def zag_one(tag, o, t, far, ref=None):
        ref = chunk[tag](o, c) if ref is None else ref
        rc(ref, ref, zs.at[tag], zr.at[tag, far], plane(t)).start()

    def zag_start(tag, pieces=(None,)):
        for ref in pieces:
            zag_one(tag, z, two_off, is_outer, ref)
        for ref in pieces:
            zag_one(tag, z, inward, 0, ref)

        def drain():
            @pl.when(inner)
            def _():
                sent(chunks[tag](4), zs.at[tag])

            @pl.when(outer)
            def _():
                sent(chunks[tag](2), zs.at[tag])

        drains.append(drain)

    def zag_outward(tag):
        @pl.when(inner)
        def _():
            zag_one(tag, z, outward, 0)

    def zag_ffn(tag):
        zag_one(tag, z, two_off, is_outer)
        zag_one(tag, z, inward, 0)
        zag_outward(tag)

    def core_send(tag, o):
        ref = chunk[tag](o, c)
        rc(ref, ref, cs.at[tag], cr.at[tag], partner).start()

    def zag_relay(tag, core=True):
        @pl.when(inner)
        def _():
            got(chunk[tag](far_end, c), zr.at[tag, 1])
            zag_one(tag, far_end, outward, 1)
            if core:
                core_send(tag, far_end)

    def zag_near(tag, core=True):
        got(chunks[tag](2), zr.at[tag, 0])
        if core:
            core_send(tag, pair)
            core_send(tag, across)

    def zag_far(tag, core=True):
        @pl.when(outer)
        def _():
            got(chunk[tag](far_end, c), zr.at[tag, 1])
            if core:
                core_send(tag, far_end)

    def zag_core(tag):
        got(chunks[tag](4), cr.at[tag])
        drains.append(lambda: sent(chunks[tag](4), cs.at[tag]))

    spread(T_PACK, [(j, pack, PK.at[z, c, s]) for j in (1, 2, 3)], PK.at[0, 0, pl.ds(0, 3)])
    spread(
        T_WQ, [(j, wq_in.at[:, rows(rank[j], 768)], WQ.at[rows(4 * g + s, 32)]) for j in (1, 2, 3)],
        WQ.at[pl.ds(0, 96)],
    )
    wo_cp.wait()
    zag_start(A_WO)
    zag_outward(A_WO)
    local[0].wait()
    zag_one(A_WQ, z, two_off, is_outer, WQ.at[rows(4 * g + s, 32)])
    zag_one(A_WQ, z, inward, 0, WQ.at[rows(4 * g + s, 32)])
    spread(
        T_WI,
        [
            (
                j, wi_in.at[:, rows(4 * i + rank[j], 128)],
                WI.at[rows(4 * g + s, 32), pl.ds(128 * i, 128)],
            )
            for j in (1, 2, 3)
            for i in range(8)
        ],
        size(96),
    )
    spread(T_TOK, [(j, x_in, X.at[rows(s, 128)]) for j in (1, 2, 3)], size(384))
    for cp in local[1:]:
        cp.wait()
    got(PK.at[0, 0, pl.ds(0, 3)], pr.at[T_PACK])
    zag_start(A_PACK)
    zag_outward(A_PACK)
    core_send(A_PACK, z)
    got(WQ.at[pl.ds(0, 96)], pr.at[T_WQ])
    zag_start(A_WQ, [WQ.at[rows(4 * g + rank[j], 32)] for j in (1, 2, 3)])
    core_send(A_WQ, z)
    core_send(A_WB, z)

    def wo_plane(o):
        for j in (1, 2, 3):
            ref = WO.at[o, c, s]
            rc(ref, ref, ps.at[T_WO], pr.at[T_WO], peer(j)).start()

    zag_relay(A_WO, core=False)
    zag_relay(A_PACK)
    zag_outward(A_WQ)
    wo_plane(z)

    @pl.when(inner)
    def _():
        wo_plane(far_end)

    zag_near(A_WO, core=False)
    wo_plane(pair)
    wo_plane(across)
    zag_near(A_PACK)
    got(size(96), pr.at[T_WI])
    wi_own = WI.at[rows(4 * g + s, 32)]
    pltpu.make_async_copy(wi_own, wi_own, osem.at[5]).wait()
    core_send(A_WI, z)

    @pl.when(outer)
    def _():
        for tag in (A_WI, A_WB):
            zag_one(tag, z, two_off, 1)
            zag_one(tag, z, inward, 0)

    zag_relay(A_WQ)

    @pl.when(inner)
    def _():
        for t, far in ((two_off, 0), (inward, 0), (outward, 0)):
            zag_one(A_WI, z, t, far)

    def drain_ffn():
        for tag in (A_WI, A_WB):
            @pl.when(inner)
            def _():
                sent(chunks[tag](4), zs.at[tag])

            @pl.when(outer)
            def _():
                sent(chunks[tag](2), zs.at[tag])

    drains.append(drain_ffn)
    zag_far(A_PACK)
    zag_far(A_WO, core=False)

    @pl.when(outer)
    def _():
        wo_plane(far_end)

    drains.append(lambda: sent(size(384), ps.at[T_WO]))
    zag_near(A_WQ)
    zag_core(A_PACK)
    for gg in range(8):
        tot = PK[gg // 2, gg % 2, 0].astype(F32)
        for r in (1, 2, 3):
            tot = tot + PK[gg // 2, gg % 2, r].astype(F32)
        VEC[:, gg * 128 : (gg + 1) * 128] = tot
        IB[:, gg * 128 : (gg + 1) * 128] = PK[gg // 2, gg % 2, s].astype(F32)
    for cc in range(2):
        tot = PK[s, cc, 0].astype(F32)
        for r in (1, 2, 3):
            tot = tot + PK[s, cc, r].astype(F32)
        for k in range(3):
            BQ[0:1, (3 * cc + k) * 128 : (3 * cc + k + 1) * 128] = tot[k : k + 1, :]
    zag_far(A_WQ)
    got(size(384), pr.at[T_TOK])
    zag_core(A_WQ)

    def qkv(t, carry):
        cols = rows(t, 256)
        MIX[:, cols] = (dot_nn(X[...], WQ[:, cols]) + BQ[0:1, cols]).astype(BF)
        return carry

    lax.fori_loop(0, 3, qkv, 0)

    factor = 1.0 / math.sqrt(HD)

    def attend(n, carry):
        rr = rows(n, 256)
        ok = lax.broadcasted_iota(jnp.int32, (1, 256), 1) < lens[n]
        outs = []
        for i in range(4):
            q = MIX[rr, 192 * i : 192 * i + 64]
            k = MIX[rr, 192 * i + 64 : 192 * i + 128]
            v = MIX[rr, 192 * i + 128 : 192 * i + 192]
            sc = jnp.where(ok, dot_nt(q, k) * factor, -1e30)
            e = jnp.exp(sc - jnp.max(sc, axis=-1, keepdims=True))
            p = e * (1.0 / jnp.sum(e, axis=-1, keepdims=True))
            PROB[n, i] = p
            outs.append(dot_nn(p.astype(BF), v).astype(BF))
        CTX[rr, 0:128] = jnp.concatenate(outs[:2], axis=1)
        CTX[rr, 128:256] = jnp.concatenate(outs[2:], axis=1)
        return carry

    lax.fori_loop(0, 1, attend, 0)
    zag_relay(A_WI)

    @pl.when(inner)
    def _():
        for t, far in ((two_off, 0), (inward, 0), (outward, 0)):
            zag_one(A_WB, z, t, far)

    lax.fori_loop(1, 2, attend, 0)
    spread(
        T_CTX, [(j, CTX.at[rows(rank[j], 128)], CTXO.at[:, rows(s, 256)]) for j in (1, 2, 3)],
        CTX.at[pl.ds(0, 384)],
    )
    CTXO[:, rows(s, 256)] = CTX[rows(s, 128), :]
    got(size(384), pr.at[T_WO])
    send(WO.at[:, c], WO.at[:, c], cs.at[A_WO], cr.at[A_WO], partner)
    zag_near(A_WI)
    got(WO.at[:, 1 - c], cr.at[A_WO])
    got(CTX.at[pl.ds(0, 384)], pr.at[T_CTX])

    def proj(t, carry):
        cols = rows(t, 256)
        w = WO[:, :, :, :, cols].reshape(1024, 256)
        XH1[:, cols] = X[rows(s, 128), cols].astype(F32) + (dot_nn(CTXO[...], w) + VEC[3:4, cols])
        return carry

    lax.fori_loop(0, 4, proj, 0)

    def own_rows(h, q):
        return pl.ds(pl.multiple_of(h * 256 + s * 64 + q * 32, 32), 32)

    def halves(h):
        return pl.ds(256 * h, 256)

    def mine_of(h):
        return pl.ds(pl.multiple_of(h * 256 + s * 64, 64), 64)

    def rank_of(h, j):
        return pl.ds(pl.multiple_of(h * 256 + rank[j] * 64, 64), 64)

    def norm_one(h):
        def body(q, carry):
            rr = rows(2 * h + q, 32)
            hid = XH1[rr, :]
            ctr = hid - jnp.mean(hid, axis=-1, keepdims=True)
            rstd = lax.rsqrt(jnp.mean(ctr * ctr, axis=-1, keepdims=True) + NORM_EPS)
            xh = ctr * rstd
            nf = xh * VEC[4:5, :] + VEC[5:6, :]
            XH1[rr, :] = xh
            RS1[rr, :] = jnp.broadcast_to(rstd, (32, 128))
            NF[rr, :] = nf
            N[own_rows(h, q), :] = nf.astype(BF)
            return carry

        lax.fori_loop(0, 2, body, 0)

    for h in (0, 1):
        norm_one(h)
        spread(T_N + h, [(j, N.at[mine_of(h)], N.at[mine_of(h)]) for j in (1, 2, 3)], size(192))
    zag_relay(A_WB)
    zag_far(A_WI)
    zag_core(A_WI)

    def ffn_in(h):
        rr = halves(h)

        def body(t, carry):
            cols = rows(t, 256)
            pre = dot_nn(N[rr, :], WI[:, cols]) + IB[9:10, cols]
            cdf = 0.5 * (1.0 + lax.erf(pre * math.sqrt(0.5)))
            ACT[rr, cols] = (pre * cdf).astype(BF)
            DG[rr, cols] = cdf + pre * jnp.exp(-0.5 * (pre * pre)) * (1.0 / math.sqrt(2.0 * math.pi))
            return carry

        lax.fori_loop(0, 4, body, 0)

    def ffn_out(h):
        rr = halves(h)

        def body(t, carry):
            cols = rows(t, 256)
            part = dot_nn(ACT[rr, :], WB[:, cols])
            SB[rr, cols] = part.astype(BF)
            ACC[:, cols] = part
            return carry

        lax.fori_loop(0, 4, body, 0)
        spread(T_RSF + h, [(j, SB.at[rank_of(h, j)], RB.at[h, j - 1]) for j in (1, 2, 3)], size(192))
        OWN[pl.ds(64 * h, 64), :] = ACC[rows(s, 64), :]

    for h in (0, 1):
        got(size(192), pr.at[T_N + h])
        ffn_in(h)
    zag_near(A_WB)
    zag_far(A_WB)
    zag_core(A_WB)
    ffn_out(0)
    ffn_out(1)
    GV[...] = jnp.zeros_like(GV)

    def norm_two(h):
        def body(q, carry):
            rr = rows(2 * h + q, 32)
            part = rows(q, 32)
            hid = OWN[rr, :] + RB[h, 0, part, :].astype(F32) + RB[h, 1, part, :].astype(F32)
            hid = NF[rr, :] + (hid + RB[h, 2, part, :].astype(F32) + VEC[6:7, :])
            ctr = hid - jnp.mean(hid, axis=-1, keepdims=True)
            rstd = lax.rsqrt(jnp.mean(ctr * ctr, axis=-1, keepdims=True) + NORM_EPS)
            xh = ctr * rstd
            OUT[rr, :] = (xh * VEC[7:8, :] + VEC[8:9, :]).astype(BF)
            place = (s % 2) * 128 + (2 * h + q) * 32 + lax.broadcasted_iota(jnp.int32, (32, 1), 0)
            seed = jnp.where(place < lens[s // 2], cot[rr, :].astype(F32), 0.0)
            GV[7:8, :] += jnp.sum(seed * xh, axis=0, keepdims=True)
            GV[8:9, :] += jnp.sum(seed, axis=0, keepdims=True)
            u = seed * VEC[7:8, :]
            gs = rstd * (u - jnp.mean(u, axis=-1, keepdims=True) - xh * jnp.mean(u * xh, axis=-1, keepdims=True))
            GV[6:7, :] += jnp.sum(gs, axis=0, keepdims=True)
            GS[rr, :] = gs
            G[own_rows(h, q), :] = gs.astype(BF)
            return carry

        lax.fori_loop(0, 2, body, 0)

    for h in (0, 1):
        got(size(192), pr.at[T_RSF + h])
        norm_two(h)
        spread(T_G + h, [(j, G.at[mine_of(h)], G.at[mine_of(h)]) for j in (1, 2, 3)], size(192))
    put(OUT, out_o, 0)

    def bwd_act(h):
        rr = halves(h)

        def body(t, carry):
            cols = rows(t, 256)
            gp = dot_nt(G[rr, :], WB[cols, :]) * DG[rr, cols]
            GV[9:10, cols] += jnp.sum(gp, axis=0, keepdims=True)
            GPB[rr, cols] = gp.astype(BF)
            return carry

        lax.fori_loop(0, 4, body, 0)

    def bwd_in(h):
        rr = halves(h)

        def body(t, carry):
            cols = rows(t, 256)
            part = dot_nt(GPB[rr, :], WI[cols, :])
            SB2[rr, cols] = part.astype(BF)
            ACC[:, cols] = part
            return carry

        lax.fori_loop(0, 4, body, 0)
        spread(T_RSB + h, [(j, SB2.at[rank_of(h, j)], RB2.at[h, j - 1]) for j in (1, 2, 3)], size(192))
        OWN[pl.ds(64 * h, 64), :] = ACC[rows(s, 64), :]

    def turn(i):
        return (3 - z + (4 - z) * i) % 5

    def core_start(tag, t, csend, crecv):
        rc(csend.at[t], crecv.at[t], cs2.at[tag], cr2.at[tag, t], partner).start()

    def wgrad(tag, lhs, rhs, mine, csend, crecv, cols):
        def body(i, carry):
            t = turn(i)
            ACC[:, 0:cols] = dot_tn(lhs[:, rows(t, 256)], rhs[...])
            csend[t] = ACC[rows(1 - c, 128), 0:cols].astype(BF)
            mine[t] = ACC[rows(c, 128), 0:cols]
            core_start(tag, t, csend, crecv)
            return carry

        lax.fori_loop(0, 4, body, 0)
        drains.append(lambda: sent(csend, cs2.at[tag]))

    def wgrad_first(lhs, rhs, mine, theirs):
        def body(t, carry):
            ACC[...] = dot_tn(lhs[halves(0), rows(t, 256)], rhs[halves(0), :])
            mine[t] = ACC[rows(c, 128), :]
            theirs[t] = ACC[rows(1 - c, 128), :]
            return carry

        lax.fori_loop(0, 4, body, 0)

    def wgrad_second(tag, lhs, rhs, mine, theirs, csend, crecv):
        def body(i, carry):
            t = turn(i)
            ACC[...] = dot_tn(lhs[halves(1), rows(t, 256)], rhs[halves(1), :])
            csend[t] = (theirs[t] + ACC[rows(1 - c, 128), :]).astype(BF)
            core_start(tag, t, csend, crecv)
            mine[t] += ACC[rows(c, 128), :]
            return carry

        lax.fori_loop(0, 4, body, 0)
        drains.append(lambda: sent(csend, cs2.at[tag]))

    def zrs_send(tag, t, zsend, zrecv, relay, sub):
        @pl.when(jnp.logical_or(t == pair, t == across))
        def _():
            rc(zsend.at[t, sub], zrecv.at[z, sub], zs2.at[tag], zr2.at[tag, 0], plane(t)).start()

        @pl.when(jnp.logical_and(outer, t == far_end))
        def _():
            rc(zsend.at[t, sub], relay.at[sub], zs2.at[tag], zr2.at[tag, 1], plane(inward)).start()

    def zrs_drain(tag, zsend, sub):
        drains.append(lambda: sent(zsend.at[pl.ds(0, 3), sub], zs2.at[tag]))

    def core_sum(tag, mine, crecv, zsend, zrecv, relay, sub):
        def body(i, carry):
            t = turn(i)
            got(crecv.at[t], cr2.at[tag, t])
            v = mine[t] + crecv[t].astype(F32)
            mine[t] = v
            zsend[t] = v.astype(BF)
            zrs_send(tag, t, zsend, zrecv, relay, sub)
            return carry

        lax.fori_loop(0, 4, body, 0)
        zrs_drain(tag, zsend, sub)

    def zrs_start(tag, zsend, zrecv, relay, sub):
        def body(i, carry):
            zrs_send(tag, turn(i), zsend, zrecv, relay, sub)
            return carry

        lax.fori_loop(0, 4, body, 0)

    def zrs_relay(tag, mine, zsend, zrecv, relay, sub):
        @pl.when(inner)
        def _():
            got(relay.at[sub], zr2.at[tag, 1])
            zsend[far_end, sub] = (mine[far_end, sub] + relay[sub].astype(F32)).astype(BF)
            rc(
                zsend.at[far_end, sub], zrecv.at[z, sub], zs2.at[tag], zr2.at[tag, 0], plane(far_end)
            ).start()

    def zrs_end(tag, mine, zrecv, res, sub):
        @pl.when(outer)
        def _():
            got(zrecv.at[pl.ds(0, 2), sub], zr2.at[tag, 0])
            res[sub] = mine[z, sub] + zrecv[pair, sub].astype(F32) + zrecv[across, sub].astype(F32)

        @pl.when(inner)
        def _():
            got(zrecv.at[pl.ds(0, 3), sub], zr2.at[tag, 0])
            res[sub] = (
                mine[z, sub] + zrecv[pair, sub].astype(F32) + zrecv[across, sub].astype(F32)
                + zrecv[far_end, sub].astype(F32)
            )

    every, first, last, quarter = pl.ds(0, 128), pl.ds(0, 64), pl.ds(64, 64), pl.ds(0, 32)
    got(size(192), pr.at[T_G])
    bwd_act(0)
    bwd_in(0)
    wgrad_first(ACT, G, mB, mO)
    got(size(192), pr.at[T_G2])
    wgrad_second(R_GB, ACT, G, mB, mO, csB, crB)
    bwd_act(1)
    core_sum(R_GB, mB, crB, zsB, zrB, rlB, first)
    bwd_in(1)
    wgrad(R_GI, N, GPB, mI, csI, crI, 1024)

    def norm_one_bwd(h):
        def body(q, carry):
            rr = rows(2 * h + q, 32)
            part = rows(q, 32)
            gn = OWN[rr, :] + RB2[h, 0, part, :].astype(F32) + RB2[h, 1, part, :].astype(F32)
            gn = GS[rr, :] + (gn + RB2[h, 2, part, :].astype(F32))
            xh = XH1[rr, :]
            GV[4:5, :] += jnp.sum(gn * xh, axis=0, keepdims=True)
            GV[5:6, :] += jnp.sum(gn, axis=0, keepdims=True)
            u = gn * VEC[4:5, :]
            gf = RS1[rr, 0:1] * (
                u - jnp.mean(u, axis=-1, keepdims=True) - xh * jnp.mean(u * xh, axis=-1, keepdims=True)
            )
            GV[3:4, :] += jnp.sum(gf, axis=0, keepdims=True)
            GF[rr, :] = gf
            GFB[rr, :] = gf.astype(BF)
            return carry

        lax.fori_loop(0, 2, body, 0)

    got(size(192), pr.at[T_RSB])
    norm_one_bwd(0)
    core_sum(R_GI, mI, crI, zsI, zrI, rlI, every)
    got(size(192), pr.at[T_RSB2])
    norm_one_bwd(1)

    def gctx(t, carry):
        w = WO[t].reshape(256, 1024)
        GCS[t] = dot_nt(GFB[...], w).astype(BF)
        return carry

    lax.fori_loop(0, 4, gctx, 0)
    me = rows(s, 128)
    spread(T_GC, [(j, GCS.at[rank[j]], GC.at[me]) for j in (1, 2, 3)], CTX.at[pl.ds(0, 384)])
    GC[me, :] = GCS[s]
    zrs_relay(R_GB, mB, zsB, zrB, rlB, first)
    wgrad(R_GO, CTXO, GFB, mO, csO, crO, 1024)

    def go_core(t, carry):
        got(crO.at[t], cr2.at[R_GO, t])
        v = mO[t] + crO[t].astype(F32)
        mO[t] = v
        for r in range(4):
            psO[r, t] = v[32 * r : 32 * r + 32, :].astype(BF)
        return carry

    lax.fori_loop(0, 4, go_core, 0)
    spread(T_GO, [(j, psO.at[rank[j]], prO.at[j - 1]) for j in (1, 2, 3)], prO)
    got(CTX.at[pl.ds(0, 384)], pr.at[T_GC])

    BQ[...] = jnp.zeros_like(BQ)

    def attend_bwd(n, carry):
        rr = rows(n, 256)
        for two in range(2):
            parts = []
            for i in (2 * two, 2 * two + 1):
                q = MIX[rr, 192 * i : 192 * i + 64]
                k = MIX[rr, 192 * i + 64 : 192 * i + 128]
                v = MIX[rr, 192 * i + 128 : 192 * i + 192]
                gc = GC[rr, 64 * i : 64 * i + 64]
                p = PROB[n, i]
                gp = dot_nt(gc, v)
                inside = jnp.sum(p * gp, axis=-1, keepdims=True)
                gsc = (p * (gp - inside) * factor).astype(BF)
                parts += [dot_nn(gsc, k), dot_tn(gsc, q), dot_tn(p.astype(BF), gc)]
            both = jnp.concatenate([x.astype(BF) for x in parts], axis=1)
            GM[rr, 384 * two : 384 * two + 384] = both
            BQ[0:1, 384 * two : 384 * two + 384] += jnp.sum(both.astype(F32), axis=0, keepdims=True)
        return carry

    lax.fori_loop(0, 2, attend_bwd, 0)
    wgrad(R_GQ, X, GM, mQ, csQ, crQ, 768)
    for k in range(6):
        GV[k % 3 : k % 3 + 1, rows(2 * s + k // 3, 128)] = BQ[0:1, 128 * k : 128 * k + 128]
    for gg in range(8):
        GVC[gg % 2, gg // 2] = GV[:, 128 * gg : 128 * gg + 128]
    send(GVC.at[1 - c], RVC, cs2.at[R_SV], cr2.at[R_SV, 0], partner)
    zrs_relay(R_GI, mI, zsI, zrI, rlI, every)
    core_sum(R_GQ, mQ, crQ, zsQ, zrQ, rlQ, every)
    got(RVC, cr2.at[R_SV, 0])
    TVZ[...] = GVC[c] + RVC[...]
    for k in (1, 2, 3):
        t = (z + k) % 4
        rc(TVZ.at[t], RVZ.at[k - 1], zs2.at[R_SV], zr2.at[R_SV, 0], plane(t)).start()
    drains.append(lambda: sent(RVZ, zs2.at[R_SV]))

    got(prO, pr.at[T_GO])

    def go_plane(t, carry):
        v = mO[t, rows(s, 32), :]
        for j in (1, 2, 3):
            v = v + prO[j - 1, t].astype(F32)
        zO[t] = v
        zsO[t] = v.astype(BF)
        return carry

    lax.fori_loop(0, 4, go_plane, 0)

    def last_sums():
        zrs_start(R_GO, zsO, zrO, rlO, quarter)
        zrs_start(R_GBL, zsB, zrB, rlB, last)

    pl.when(outer)(last_sums)
    zrs_drain(R_GO, zsO, quarter)
    zrs_drain(R_GBL, zsB, last)

    def gtok(rr, j):
        def body(t, carry):
            cols = rows(t, 256)
            part = dot_nt(GM[rr, :], WQ[cols, :])
            if j == 0:
                OWN[:, cols] = part
            else:
                SB3[j - 1, :, cols] = part.astype(BF)
            return carry

        lax.fori_loop(0, 4, body, 0)

    for j in (1, 2, 3):
        gtok(rows(rank[j], 128), j)
        rc(SB3.at[j - 1], RB3.at[j - 1], ps.at[T_GT], pr.at[T_GT], peer(j)).start()
    drains.append(lambda: sent(size(384), ps.at[T_GT]))
    gtok(me, 0)
    zrs_end(R_GB, mB, zrB, GBF, first)
    put(GBF.at[first], gb_o.at[first], 1)
    zrs_relay(R_GQ, mQ, zsQ, zrQ, rlQ, every)
    pl.when(inner)(last_sums)
    got(size(384), pr.at[T_GT])

    def gtok_sum(t, carry):
        rr = rows(t, 32)
        h = OWN[rr, :] + RB3[0, rr, :].astype(F32) + RB3[1, rr, :].astype(F32) + RB3[2, rr, :].astype(F32)
        GTS[rr, :] = GF[rr, :] + h
        return carry

    lax.fori_loop(0, 4, gtok_sum, 0)
    put(GTS, gtok_o, 2)
    zrs_end(R_GI, mI, zrI, resI, every)
    for j in (1, 2, 3):
        siI[j - 1] = resI[rows(rank[j], 32), :].astype(BF)
    spread(T_GI, [(j, siI.at[j - 1], riI.at[j - 1]) for j in (1, 2, 3)], riI)
    zrs_relay(R_GO, zO, zsO, zrO, rlO, quarter)
    got(RVZ, zr2.at[R_SV, 0])
    PV[...] = TVZ[z] + RVZ[0] + RVZ[1] + RVZ[2]
    spread(T_SV, [(j, PV, RVP.at[j - 1]) for j in (1, 2, 3)], RVP)
    for i in range(8):
        GIF[:, rows(4 * i + s, 128)] = resI[rows(s, 32), 128 * i : 128 * i + 128]
    got(riI, pr.at[T_GI])
    for j in (1, 2, 3):
        for i in range(8):
            GIF[:, rows(4 * i + rank[j], 128)] = riI[j - 1, :, 128 * i : 128 * i + 128].astype(F32)
    put(GIF, gi_o, 3)
    got(RVP, pr.at[T_SV])
    tot = PV[...] + RVP[0] + RVP[1] + RVP[2]
    row = lax.broadcasted_iota(jnp.int32, (16, 128), 0)
    RVC[0] = jnp.where(row == 9, PV[...], tot)
    put(RVC.at[0], sv_o, 6)
    zrs_end(R_GQ, mQ, zrQ, resQ, every)
    for j in (1, 2, 3):
        siQ[j - 1] = resQ[rows(rank[j], 32), :].astype(BF)
    spread(T_GQ, [(j, siQ.at[j - 1], riQ.at[j - 1]) for j in (1, 2, 3)], riQ)
    zrs_relay(R_GBL, mB, zsB, zrB, rlB, last)
    zrs_end(R_GO, zO, zrO, GOF, quarter)
    put(GOF, go_o, 4)
    GQF[:, rows(s, 768)] = resQ[rows(s, 32), :]
    got(riQ, pr.at[T_GQ])
    for j in (1, 2, 3):
        GQF[:, rows(rank[j], 768)] = riQ[j - 1].astype(F32)
    put(GQF, gq_o, 5)
    zrs_end(R_GBL, mB, zrB, GBF, last)
    put(GBF.at[last], gb_o.at[last], 7)
    for drain in drains:
        drain()


def hand_over(*refs):
    sources, targets, kept, (isem, osem) = refs[:7], refs[7:21], refs[21:36], refs[36:]
    s = lax.axis_index("seq")
    ins = [pltpu.make_async_copy(src, mid, isem.at[k]) for k, (src, mid) in enumerate(zip(sources, kept))]
    held = kept[:6] + kept[7:]
    outs = [pltpu.make_async_copy(mid, dst, osem.at[k]) for k, (mid, dst) in enumerate(zip(held, targets))]
    for k in (6, 0, 1, 2, 3, 4, 5):
        ins[k].start()
    qv, ob, g1, b1, ib, bb, g2, b2 = kept[7:]
    sums = kept[6]
    ins[6].wait()
    turned = pltpu.roll(sums[...], (128 - 32 * s) % 128, 1)
    for k, ref in ((3, ob), (4, g1), (5, b1), (6, bb), (7, g2), (8, b2)):
        ref[...] = turned[k : k + 1, 0:32]
    ib[...] = sums[9:10, :]
    line = jnp.where(s == 0, sums[0:1, :], jnp.where(s == 3, sums[2:3, :], sums[1:2, :]))
    qv[...] = jnp.where(s // 2 == 0, line[:, 0:64], line[:, 64:128])
    for k in range(6, 14):
        outs[k].start()
    for k in range(6):
        ins[k].wait()
        outs[k].start()
    for out in outs:
        out.wait()


def fused_shards(
    tokens, cotangent, slot_lengths, w_qkv, qv_bias, w_out, out_bias, ln1_gain, ln1_bias,
    w_in, in_bias, w_back, back_bias, ln2_gain, ln2_bias,
):
    vm = pltpu.VMEM
    dma = pltpu.SemaphoreType.DMA

    def item(n):
        return [
            vm((4, 128, n), F32), vm((4, 128, n), BF), vm((4, 128, n), BF),
            vm((4, 128, n), BF), vm((4, 128, n), BF), vm((128, n), BF),
        ]

    lengths = (64, 32, 32, 32, 128, 32, 32, 32)
    scratch = [vm((1, n), BF) for n in lengths]
    scratch += [
        vm((16, 128), BF), vm((16, 128), F32), vm((128, 1024), BF), vm((512, 1024), BF), vm((1024, 768), BF), vm((1024, 1024), BF), vm((1024, 1024), BF),
        vm((4, 2, 4, 32, 1024), BF), vm((4, 2, 4, 16, 128), BF), vm((16, 1024), F32), vm((16, 1024), F32),
        vm((8, 768), F32),
        vm((512, 768), BF), vm((2, 4, 256, 256), F32), vm((512, 256), BF), vm((128, 1024), BF),
        vm((128, 1024), F32), vm((128, 1024), F32), vm((128, 128), F32), vm((512, 1024), BF),
        vm((512, 1024), F32), vm((512, 1024), BF), vm((512, 1024), BF), vm((2, 3, 64, 1024), BF),
        vm((128, 1024), F32),
        vm((512, 1024), BF), vm((128, 1024), F32), vm((512, 1024), BF), vm((512, 1024), BF),
        vm((2, 3, 64, 1024), BF), vm((128, 1024), F32), vm((128, 1024), BF), vm((4, 128, 256), BF),
        vm((512, 256), BF), vm((512, 768), BF), vm((3, 128, 1024), BF), vm((3, 128, 1024), BF),
        vm((256, 1024), F32),
    ]
    scratch += item(1024) + item(1024) + item(768)
    scratch += [
        vm((4, 128, 1024), BF), vm((4, 128, 1024), BF), vm((4, 128, 1024), F32),
        vm((4, 4, 32, 1024), BF), vm((3, 4, 32, 1024), BF), vm((4, 32, 1024), F32),
        vm((4, 32, 1024), BF), vm((4, 32, 1024), BF), vm((32, 1024), BF),
        vm((3, 32, 1024), BF), vm((3, 32, 1024), BF), vm((3, 32, 768), BF), vm((3, 32, 768), BF),
        vm((128, 1024), F32), vm((128, 768), F32),
        vm((16, 1024), F32), vm((2, 4, 16, 128), F32), vm((4, 16, 128), F32), vm((4, 16, 128), F32),
        vm((3, 16, 128), F32), vm((16, 128), F32), vm((3, 16, 128), F32),
        vm((128, 1024), BF), vm((128, 1024), F32), vm((32, 3072), F32), vm((32, 1024), F32),
        vm((32, 4096), F32), vm((128, 1024), F32),
        dma((8,)), dma((20,)), dma((20,)), dma((5,)), dma((5, 2)), dma((5,)), dma((5,)),
        dma((6,)), dma((6, 4)), dma((6,)), dma((6, 2)),
    ]
    shapes = [
        ((128, 1024), BF), ((128, 1024), F32), ((32, 3072), F32), ((32, 1024), F32),
        ((32, 4096), F32), ((128, 1024), F32), ((16, 128), F32),
    ]
    hbm = pl.BlockSpec(memory_space=pl.ANY)
    smem = pl.BlockSpec(memory_space=pltpu.SMEM)
    small = [v.reshape(1, -1) for v in (qv_bias, out_bias, ln1_gain, ln1_bias, in_bias, back_bias, ln2_gain, ln2_bias)]
    results = pl.pallas_call(
        layer_kernel,
        out_shape=[jax.ShapeDtypeStruct(a, b) for a, b in shapes],
        in_specs=[hbm] * 6 + [smem] + [hbm] * 8,
        out_specs=[hbm] * 7,
        scratch_shapes=scratch,
        compiler_params=pltpu.CompilerParams(
            collective_id=0, has_side_effects=True, vmem_limit_bytes=67_000_000
        ),
        name="encoder_layer",
    )(tokens, cotangent, w_qkv, w_out, w_in, w_back, slot_lengths, *small)
    final = pl.pallas_call(
        hand_over,
        out_shape=[jax.ShapeDtypeStruct(a, b) for a, b in shapes[:6]]
        + [jax.ShapeDtypeStruct((1, n), F32) for n in lengths],
        in_specs=[hbm] * 7,
        out_specs=[hbm] * 14,
        scratch_shapes=[vm(a, b) for a, b in shapes] + [vm((1, n), F32) for n in lengths] + [dma((7,)), dma((14,))],
        name="hand_over",
    )(*results)
    output, grad_tokens, grad_qkv, grad_wo, grad_wi, grad_wb = final[:6]
    qv, ob, g1, b1, ib, bb, g2, b2 = [v.reshape(-1) for v in final[6:]]
    return (output, grad_tokens, grad_qkv, qv, grad_wo, ob, g1, b1, grad_wi, ib, grad_wb, bb, g2, b2)


def solution(mesh):
    placed = (
        P(("grp", "seq"), None),
        P(("grp", "seq"), None),
        P("grp"),
        P(("grp", "seq"), None),
        P(("grp", "seq")),
        P(("grp", "seq"), None),
        P(("grp", "seq")),
        P(("grp", "seq")),
        P(("grp", "seq")),
        P(("grp", "seq"), None),
        P(("grp", "seq")),
        P(("grp", "seq"), None),
        P(("grp", "seq")),
        P(("grp", "seq")),
        P(("grp", "seq")),
    )
    fused = mesh.shape["grp"] == 2 * PLANES and mesh.shape["seq"] == RANKS
    return jax.shard_map(
        fused_shards if fused else shards,
        mesh=mesh,
        in_specs=placed,
        out_specs=(
            P(("grp", "seq"), None),
            P(("grp", "seq"), None),
            P(("grp", "seq"), None),
            P(("grp", "seq")),
            P(("grp", "seq"), None),
            P(("grp", "seq")),
            P(("grp", "seq")),
            P(("grp", "seq")),
            P(("grp", "seq"), None),
            P(("grp", "seq")),
            P(("grp", "seq"), None),
            P(("grp", "seq")),
            P(("grp", "seq")),
            P(("grp", "seq")),
        ),
        check_vma=False,
    )
```

```python
from functools import partial
import math

import jax
import jax.numpy as jnp
from jax import lax
from jax.experimental import pallas as pl
from jax.experimental.pallas import tpu as pltpu
from jax.sharding import PartitionSpec as P

D = 1024
H = 16
HD = 64
SLOT_DEV = 64
SLOTS = 2


NORM_EPS = 1e-06


def layer_norm(hidden, gain, shift):
    center = hidden - jnp.mean(hidden, axis=-1, keepdims=True)
    spread = jnp.mean(center * center, axis=-1, keepdims=True)
    return center * lax.rsqrt(spread + NORM_EPS) * gain + shift


def exact_gelu(values):
    return jax.nn.gelu(values, approximate=False)


def full_bias(pair_bias):
    pairs = pair_bias.reshape(H, 2, HD)
    return jnp.stack([pairs[:, 0], jnp.zeros_like(pairs[:, 0]), pairs[:, 1]], axis=1).reshape(3 * D)


def contract_rows(left, right):
    return lax.dot_general(
        left, right, (((0,), (0,)), ((), ())), preferred_element_type=jnp.float32
    )


def contract_cols(left, right):
    return lax.dot_general(
        left, right, (((1,), (1,)), ((), ())), preferred_element_type=jnp.float32
    )


def slot_scores(mixed, length, factor):
    slot_width = mixed.shape[0]
    queries = mixed[:, :, 0]
    key_rows = mixed[:, :, 1]
    value_rows = mixed[:, :, 2]
    products = jnp.einsum("qhd,khd->hqk", queries, key_rows, preferred_element_type=jnp.float32)
    key_valid = (jnp.arange(slot_width) < length)[None, None, :]
    scores = jnp.where(key_valid, products * factor, -1e30)
    return (queries, key_rows, value_rows, scores)


def slot_forward(item, factor):
    mixed, length = item
    queries, key_rows, value_rows, scores = slot_scores(mixed, length, factor)
    row_max = jnp.max(scores, axis=-1, keepdims=True)
    expon = jnp.exp(scores - row_max)
    total = jnp.sum(expon, axis=-1, keepdims=True)
    probs = expon / total
    context = jnp.einsum(
        "hqk,khd->qhd", probs.astype(jnp.bfloat16), value_rows, preferred_element_type=jnp.float32
    )
    return (context.astype(jnp.bfloat16), row_max + jnp.log(total))


def slot_backward(item, factor):
    mixed, grad_context, log_total, length = item
    queries, key_rows, value_rows, scores = slot_scores(mixed, length, factor)
    probs = jnp.exp(scores - log_total)
    grad_probs = jnp.einsum(
        "qhd,khd->hqk", grad_context, value_rows, preferred_element_type=jnp.float32
    )
    inner = jnp.sum(probs * grad_probs, axis=-1, keepdims=True)
    grad_scores = (probs * (grad_probs - inner) * factor).astype(jnp.bfloat16)
    grad_queries = jnp.einsum(
        "hqk,khd->qhd", grad_scores, key_rows, preferred_element_type=jnp.float32
    )
    grad_keys = jnp.einsum("hqk,qhd->khd", grad_scores, queries, preferred_element_type=jnp.float32)
    grad_values = jnp.einsum(
        "hqk,qhd->khd", probs.astype(jnp.bfloat16), grad_context, preferred_element_type=jnp.float32
    )
    return jnp.stack([grad_queries, grad_keys, grad_values], axis=2).astype(jnp.bfloat16)


def shards(
    tokens,
    cotangent,
    slot_lengths,
    w_qkv,
    qv_bias,
    w_out,
    out_bias,
    ln1_gain,
    ln1_bias,
    w_in,
    in_bias,
    w_back,
    back_bias,
    ln2_gain,
    ln2_bias,
):
    seq_count = lax.axis_size("seq")
    local_rows = tokens.shape[0]
    slot_width = SLOT_DEV * seq_count
    heads_here = H // seq_count
    factor = 1.0 / math.sqrt(HD)
    full_qkv, full_qv, full_out, full_obias, gain_one, shift_one = (
        lax.all_gather(w_qkv, ("grp", "seq"), axis=0, tiled=True),
        lax.all_gather(qv_bias, ("grp", "seq"), axis=0, tiled=True),
        lax.all_gather(w_out, ("grp", "seq"), axis=0, tiled=True),
        lax.all_gather(out_bias, ("grp", "seq"), axis=0, tiled=True),
        lax.all_gather(ln1_gain, ("grp", "seq"), axis=0, tiled=True),
        lax.all_gather(ln1_bias, ("grp", "seq"), axis=0, tiled=True),
    )
    full_in, full_ibias, full_back, full_bbias, gain_two, shift_two = (
        lax.all_gather(w_in, ("grp", "seq"), axis=0, tiled=True),
        lax.all_gather(in_bias, ("grp", "seq"), axis=0, tiled=True),
        lax.all_gather(w_back, ("grp", "seq"), axis=0, tiled=True),
        lax.all_gather(back_bias, ("grp", "seq"), axis=0, tiled=True),
        lax.all_gather(ln2_gain, ("grp", "seq"), axis=0, tiled=True),
        lax.all_gather(ln2_bias, ("grp", "seq"), axis=0, tiled=True),
    )
    mixed = (
        jnp.dot(tokens, full_qkv, preferred_element_type=jnp.float32) + full_bias(full_qv)
    ).astype(jnp.bfloat16)
    gathered = lax.all_to_all(mixed, "seq", split_axis=1, concat_axis=0, tiled=True)
    per_slot = gathered.reshape(SLOTS, slot_width, heads_here, 3, HD)
    contexts, log_totals = lax.map(partial(slot_forward, factor=factor), (per_slot, slot_lengths))
    context_heads = contexts.reshape(SLOTS * slot_width, heads_here * HD)
    context = lax.all_to_all(context_heads, "seq", split_axis=0, concat_axis=1, tiled=True)
    attended = jnp.dot(context, full_out, preferred_element_type=jnp.float32) + full_obias
    first_in = tokens.astype(jnp.float32) + attended
    normed, norm_one_pull = jax.vjp(layer_norm, first_in, gain_one, shift_one)
    normed_low = normed.astype(jnp.bfloat16)
    pre_act = jnp.dot(normed_low, full_in, preferred_element_type=jnp.float32) + full_ibias
    activated, gelu_pull = jax.vjp(exact_gelu, pre_act)
    act_low = activated.astype(jnp.bfloat16)
    ffn_out = jnp.dot(act_low, full_back, preferred_element_type=jnp.float32) + full_bbias
    output, norm_two_pull = jax.vjp(layer_norm, normed + ffn_out, gain_two, shift_two)
    row_index = lax.axis_index("seq") * local_rows + jnp.arange(local_rows)
    slot_index = row_index // slot_width
    place = row_index % slot_width
    row_length = jnp.sum(
        jnp.where(slot_index[:, None] == jnp.arange(SLOTS)[None, :], slot_lengths[None, :], 0),
        axis=1,
    )
    row_valid = (place < row_length).astype(jnp.float32)
    seed_grad = cotangent.astype(jnp.float32) * row_valid[:, None]
    grad_second, grad_gain_two, grad_shift_two = norm_two_pull(seed_grad)
    grad_ffn_low = grad_second.astype(jnp.bfloat16)
    grad_back_w = contract_rows(act_low, grad_ffn_low)
    grad_back_b = jnp.sum(grad_second, axis=0)
    (grad_pre,) = gelu_pull(contract_cols(grad_ffn_low, full_back))
    grad_pre_low = grad_pre.astype(jnp.bfloat16)
    grad_in_w = contract_rows(normed_low, grad_pre_low)
    grad_in_b = jnp.sum(grad_pre, axis=0)
    grad_normed = grad_second + contract_cols(grad_pre_low, full_in)
    grad_first, grad_gain_one, grad_shift_one = norm_one_pull(grad_normed)
    grad_attn_low = grad_first.astype(jnp.bfloat16)
    grad_out_w = contract_rows(context, grad_attn_low)
    grad_out_b = jnp.sum(grad_first, axis=0)
    grad_context = contract_cols(grad_attn_low, full_out).astype(jnp.bfloat16)
    grad_heads = lax.all_to_all(grad_context, "seq", split_axis=1, concat_axis=0, tiled=True)
    grad_slots = grad_heads.reshape(SLOTS, slot_width, heads_here, HD)
    grad_mixed_heads = lax.map(
        partial(slot_backward, factor=factor), (per_slot, grad_slots, log_totals, slot_lengths)
    )
    grad_mixed = lax.all_to_all(
        grad_mixed_heads.reshape(SLOTS * slot_width, heads_here * 3 * HD),
        "seq",
        split_axis=0,
        concat_axis=1,
        tiled=True,
    )
    grad_qkv_w = contract_rows(tokens, grad_mixed)
    summed_bias = jnp.sum(grad_mixed.astype(jnp.float32), axis=0).reshape(H, 3, HD)
    grad_qv = jnp.stack([summed_bias[:, 0], summed_bias[:, 2]], axis=1).reshape(2 * D)
    input_grad = grad_first + contract_cols(grad_mixed, full_qkv)
    sums = (
        lax.psum_scatter(grad_qkv_w, ("grp", "seq"), scatter_dimension=0, tiled=True),
        lax.psum_scatter(grad_qv, ("grp", "seq"), scatter_dimension=0, tiled=True),
        lax.psum_scatter(grad_out_w, ("grp", "seq"), scatter_dimension=0, tiled=True),
        lax.psum_scatter(grad_out_b, ("grp", "seq"), scatter_dimension=0, tiled=True),
        lax.psum_scatter(
            grad_gain_one.astype(jnp.float32), ("grp", "seq"), scatter_dimension=0, tiled=True
        ),
        lax.psum_scatter(
            grad_shift_one.astype(jnp.float32), ("grp", "seq"), scatter_dimension=0, tiled=True
        ),
        lax.psum_scatter(grad_in_w, ("grp", "seq"), scatter_dimension=0, tiled=True),
        lax.psum_scatter(grad_in_b, ("grp", "seq"), scatter_dimension=0, tiled=True),
        lax.psum_scatter(grad_back_w, ("grp", "seq"), scatter_dimension=0, tiled=True),
        lax.psum_scatter(grad_back_b, ("grp", "seq"), scatter_dimension=0, tiled=True),
        lax.psum_scatter(
            grad_gain_two.astype(jnp.float32), ("grp", "seq"), scatter_dimension=0, tiled=True
        ),
        lax.psum_scatter(
            grad_shift_two.astype(jnp.float32), ("grp", "seq"), scatter_dimension=0, tiled=True
        ),
    )
    return (
        output.astype(jnp.bfloat16),
        input_grad,
        sums[0],
        sums[1],
        sums[2],
        sums[3],
        sums[4],
        sums[5],
        sums[6],
        sums[7],
        sums[8],
        sums[9],
        sums[10],
        sums[11],
    )


BF = jnp.bfloat16
F32 = jnp.float32
MESH = pl.DeviceIdType.MESH
PLANES = 4
RANKS = 4
(
    T_PACK, T_WQ, T_WI, T_TOK, T_WO, T_CTX, T_CA, T_CB, T_N, T_N2, T_RSF, T_RSF2, T_RSF3, T_RSF4,
    T_G, T_G2, T_G3, T_RSB, T_RSB2, T_GC, T_GF, T_GO, T_GT, T_GI, T_GQ, T_SV,
) = range(26)
(A_PACK, A_WO, A_WQ, A_WI, A_WB, A_WB2, A_WB3, A_WB4) = range(8)
(R_GB, R_GB2, R_GB3, R_GI, R_GO, R_GQ, R_SV) = range(7)
PARTS = ((0, 256), (256, 256), (512, 256), (768, 256))
GPARTS = ((0, 256), (256, 256), (512, 512))


def dot_nn(a, b):
    return jnp.dot(a, b, preferred_element_type=F32)


def dot_nt(a, b):
    return lax.dot_general(a, b, (((1,), (1,)), ((), ())), preferred_element_type=F32)


def dot_tn(a, b):
    return lax.dot_general(a, b, (((0,), (0,)), ((), ())), preferred_element_type=F32)


def layer_kernel(
    x_in, cot_in, wq_in, wo_in, wi_in, wb_in, lens, *refs
):
    (
        small_in, (out_o, gtok_o, gq_o, go_o, gi_o, gb_o, sv_o), small,
        (
            pack, packf, cot, X, WQ, WI, WB, WO, PK, VEC, IB, BQ,
            MIX, PROB, CTX, CALL, XH1, NF, RS1, N, DG, ACT, SB, RB, OWN,
            G, GS, GPB, SB2, RB2, GF, GFB, GFC, GCS, GC, GM, SB3, RB3,
            ACC,
            mB, csB, crB, zsB, zrB, rlB,
            mI, csI, crI, zsI, zrI, rlI,
            mQ, csQ, crQ, zsQ, zrQ, rlQ,
            mO, csO, crO, zsO, zrO, rlO,
            siI, riI, siQ, riQ, siO, riO, resI, resQ, resO,
            GV, GVC, RVC, TVZ, RVZ, PV, RVP,
            OUT, GTS, GQF, GOF, GIF, GBF,
            osem, ps, pr, zs, zr, cs, cr, cs2, cr2, zs2, zr2,
        ),
    ) = refs[:8], refs[8:15], refs[15:23], refs[23:]
    g = lax.axis_index("grp")
    s = lax.axis_index("seq")
    z = g // 2
    c = g % 2
    rank = {1: s + 1 - 2 * (s % 2), 2: (s + 2) % 4, 3: 3 - s}
    partner = (g + 1 - 2 * c, s)
    inner = jnp.logical_and(z >= 1, z <= 2)
    outer = jnp.logical_or(z == 0, z == 3)
    two_off, inward, outward = (z + 2) % 4, 1 + z % 2, 3 * (z // 2)
    pair, across, far_end = z + 1 - 2 * (z % 2), 2 - z // 2, 3 * (1 - z // 2)
    is_outer = (z // 2 + z % 2 + 1) % 2
    drains = []

    def peer(j):
        return (g, rank[j])

    def plane(t):
        return (2 * t + c, s)

    def rc(src, dst, ss, rs, dev):
        return pltpu.make_async_remote_copy(
            src_ref=src, dst_ref=dst, send_sem=ss, recv_sem=rs, device_id=dev, device_id_type=MESH
        )

    def got(dst, rs):
        rc(dst, dst, osem.at[0], rs, partner).wait_recv()

    def sent(src, ss):
        rc(src, src, ss, pr.at[0], partner).wait_send()

    def send(src, dst, ss, rs, dev):
        rc(src, dst, ss, rs, dev).start()
        drains.append(lambda: sent(src, ss))

    def spread(tag, pieces, total):
        for j, src, dst in pieces:
            rc(src, dst, ps.at[tag], pr.at[tag], peer(j)).start()
        drains.append(lambda: sent(total, ps.at[tag]))

    def put(src, dst, k):
        pltpu.make_async_copy(src, dst, osem.at[k]).start()
        drains.append(lambda: pltpu.make_async_copy(src, dst, osem.at[k]).wait())

    def rows(i, n):
        return pl.ds(pl.multiple_of(i * n, n), n)

    def size(n):
        return X.at[pl.ds(0, n)]

    bar = pltpu.get_barrier_semaphore()
    for j in (1, 2, 3):
        pl.semaphore_signal(bar, inc=1, device_id=peer(j), device_id_type=MESH)
    for k in (1, 2, 3):
        pl.semaphore_signal(bar, inc=1, device_id=plane((z + k) % 4), device_id_type=MESH)
    pl.semaphore_signal(bar, inc=1, device_id=partner, device_id_type=MESH)
    small_cp = [pltpu.make_async_copy(small_in[k], small[k], ps.at[8 + k]) for k in range(8)]
    for cp in small_cp:
        cp.start()
    wo_cp = pltpu.make_async_copy(wo_in, WO.at[z, c, s], osem.at[2])
    local = [
        pltpu.make_async_copy(wq_in.at[:, rows(s, 768)], WQ.at[rows(4 * g + s, 32)], osem.at[1]),
        pltpu.make_async_copy(x_in, X.at[rows(s, 128)], osem.at[0]),
        pltpu.make_async_copy(wb_in, WB.at[rows(g, 128)], osem.at[3]),
        pltpu.make_async_copy(cot_in, cot, osem.at[4]),
    ]
    for cp in [wo_cp] + local:
        cp.start()
    for i in range(8):
        pltpu.make_async_copy(
            wi_in.at[:, rows(4 * i + s, 128)], WI.at[rows(4 * g + s, 32), pl.ds(128 * i, 128)], osem.at[5]
        ).start()
    lane = lax.broadcasted_iota(jnp.int32, (1, 128), 1)
    for cp in small_cp:
        cp.wait()
    qv_in, ob_in, g1_in, b1_in, ib_in, bb_in, g2_in, b2_in = small
    packf[...] = jnp.zeros_like(packf)
    twice = jnp.concatenate([qv_in[...].astype(F32)] * 2, axis=1)
    for k in range(3):
        packf[k : k + 1, :] = jnp.where(lane // 64 + 4 * ((s + 1) // 2) == s // 2 + 4 * k, twice, 0.0)
    for k, ref in ((3, ob_in), (4, g1_in), (5, b1_in), (6, bb_in), (7, g2_in), (8, b2_in)):
        four = jnp.concatenate([ref[...].astype(F32)] * 4, axis=1)
        packf[k : k + 1, :] = jnp.where(lane // 32 == s, four, 0.0)
    packf[9:10, :] = ib_in[...].astype(F32)
    pack[...] = packf[...].astype(BF)
    PK[z, c, s] = pack[...]
    pl.semaphore_wait(bar, 7)

    def ck(ref):
        return lambda o, cc: ref.at[rows(2 * o + cc, 128)]

    chunk = {
        A_PACK: lambda o, cc: PK.at[o, cc],
        A_WO: lambda o, cc: WO.at[o, cc, s],
        A_WQ: ck(WQ),
        A_WI: ck(WI),
    }
    for k, part in enumerate(PARTS):
        chunk[A_WB + k] = lambda o, cc, part=part: WB.at[rows(2 * o + cc, 128), pl.ds(*part)]
    chunks = {
        A_PACK: lambda n: PK.at[pl.ds(0, n), 0],
        A_WO: lambda n: size(32 * n),
        A_WQ: lambda n: WQ.at[pl.ds(0, 128 * n)],
        A_WI: lambda n: size(128 * n),
    }
    for k, (_, wide) in enumerate(PARTS):
        chunks[A_WB + k] = lambda n, wide=wide: size(128 * n * wide // 1024)

    def zag_one(tag, o, t, far, ref=None):
        ref = chunk[tag](o, c) if ref is None else ref
        rc(ref, ref, zs.at[tag], zr.at[tag, far], plane(t)).start()

    def zag_start(tag, pieces=(None,)):
        for ref in pieces:
            zag_one(tag, z, two_off, is_outer, ref)
        for ref in pieces:
            zag_one(tag, z, inward, 0, ref)

        def drain():
            @pl.when(inner)
            def _():
                sent(chunks[tag](4), zs.at[tag])

            @pl.when(outer)
            def _():
                sent(chunks[tag](2), zs.at[tag])

        drains.append(drain)

    def zag_outward(tag):
        @pl.when(inner)
        def _():
            zag_one(tag, z, outward, 0)

    def zag_ffn(tag):
        zag_one(tag, z, two_off, is_outer)
        zag_one(tag, z, inward, 0)
        zag_outward(tag)

    def core_send(tag, o):
        ref = chunk[tag](o, c)
        rc(ref, ref, cs.at[tag], cr.at[tag], partner).start()

    def zag_relay(tag, core=True):
        @pl.when(inner)
        def _():
            got(chunk[tag](far_end, c), zr.at[tag, 1])
            zag_one(tag, far_end, outward, 1)
            if core:
                core_send(tag, far_end)

    def zag_near(tag, core=True):
        got(chunks[tag](2), zr.at[tag, 0])
        if core:
            core_send(tag, pair)
            core_send(tag, across)

    def zag_far(tag, core=True):
        @pl.when(outer)
        def _():
            got(chunk[tag](far_end, c), zr.at[tag, 1])
            if core:
                core_send(tag, far_end)

    def zag_core(tag):
        got(chunks[tag](4), cr.at[tag])
        drains.append(lambda: sent(chunks[tag](4), cs.at[tag]))

    spread(T_PACK, [(j, pack, PK.at[z, c, s]) for j in (1, 2, 3)], PK.at[0, 0, pl.ds(0, 3)])
    spread(
        T_WQ, [(j, wq_in.at[:, rows(rank[j], 768)], WQ.at[rows(4 * g + s, 32)]) for j in (1, 2, 3)],
        WQ.at[pl.ds(0, 96)],
    )
    wo_cp.wait()
    zag_start(A_WO)
    zag_outward(A_WO)
    local[0].wait()
    zag_one(A_WQ, z, two_off, is_outer, WQ.at[rows(4 * g + s, 32)])
    zag_one(A_WQ, z, inward, 0, WQ.at[rows(4 * g + s, 32)])
    spread(
        T_WI,
        [
            (
                j, wi_in.at[:, rows(4 * i + rank[j], 128)],
                WI.at[rows(4 * g + s, 32), pl.ds(128 * i, 128)],
            )
            for j in (1, 2, 3)
            for i in range(8)
        ],
        size(96),
    )
    spread(T_TOK, [(j, x_in, X.at[rows(s, 128)]) for j in (1, 2, 3)], size(384))
    for cp in local[1:]:
        cp.wait()
    got(PK.at[0, 0, pl.ds(0, 3)], pr.at[T_PACK])
    zag_start(A_PACK)
    zag_outward(A_PACK)
    core_send(A_PACK, z)
    got(WQ.at[pl.ds(0, 96)], pr.at[T_WQ])
    zag_start(A_WQ, [WQ.at[rows(4 * g + rank[j], 32)] for j in (1, 2, 3)])
    core_send(A_WQ, z)
    for tag in (A_WB, A_WB2, A_WB3, A_WB4):
        core_send(tag, z)

    def wo_plane(o):
        for j in (1, 2, 3):
            ref = WO.at[o, c, s]
            rc(ref, ref, ps.at[T_WO], pr.at[T_WO], peer(j)).start()

    zag_relay(A_WO, core=False)
    zag_relay(A_PACK)
    zag_outward(A_WQ)
    wo_plane(z)

    @pl.when(inner)
    def _():
        wo_plane(far_end)

    zag_near(A_WO, core=False)
    wo_plane(pair)
    wo_plane(across)
    zag_near(A_PACK)
    got(size(96), pr.at[T_WI])
    wi_own = WI.at[rows(4 * g + s, 32)]
    pltpu.make_async_copy(wi_own, wi_own, osem.at[5]).wait()
    core_send(A_WI, z)

    @pl.when(outer)
    def _():
        for tag in (A_WI, A_WB, A_WB2, A_WB3, A_WB4):
            zag_one(tag, z, two_off, 1)
            zag_one(tag, z, inward, 0)

    zag_relay(A_WQ)

    @pl.when(inner)
    def _():
        for t, far in ((two_off, 0), (inward, 0), (outward, 0)):
            zag_one(A_WI, z, t, far)

    def drain_ffn():
        for tag in (A_WI, A_WB, A_WB2, A_WB3, A_WB4):
            @pl.when(inner)
            def _():
                sent(chunks[tag](4), zs.at[tag])

            @pl.when(outer)
            def _():
                sent(chunks[tag](2), zs.at[tag])

    drains.append(drain_ffn)

    def zag_own(tag):
        @pl.when(inner)
        def _():
            for t in (two_off, inward, outward):
                zag_one(tag, z, t, 0)

    zag_far(A_PACK)
    zag_far(A_WO, core=False)

    @pl.when(outer)
    def _():
        wo_plane(far_end)

    drains.append(lambda: sent(size(384), ps.at[T_WO]))
    zag_near(A_WQ)
    zag_core(A_PACK)
    for gg in range(8):
        tot = PK[gg // 2, gg % 2, 0].astype(F32)
        for r in (1, 2, 3):
            tot = tot + PK[gg // 2, gg % 2, r].astype(F32)
        VEC[:, gg * 128 : (gg + 1) * 128] = tot
        IB[:, gg * 128 : (gg + 1) * 128] = PK[gg // 2, gg % 2, s].astype(F32)
    for cc in range(2):
        tot = PK[s, cc, 0].astype(F32)
        for r in (1, 2, 3):
            tot = tot + PK[s, cc, r].astype(F32)
        for k in range(3):
            BQ[0:1, (3 * cc + k) * 128 : (3 * cc + k + 1) * 128] = tot[k : k + 1, :]
    zag_far(A_WQ)
    got(size(384), pr.at[T_TOK])
    zag_core(A_WQ)

    def qkv(t, carry):
        cols = rows(t, 256)
        MIX[:, cols] = (dot_nn(X[...], WQ[:, cols]) + BQ[0:1, cols]).astype(BF)
        return carry

    lax.fori_loop(0, 3, qkv, 0)

    factor = 1.0 / math.sqrt(HD)

    def attend(n, carry):
        rr = rows(n, 256)
        ok = lax.broadcasted_iota(jnp.int32, (1, 256), 1) < lens[n]
        outs = []
        for i in range(4):
            q = MIX[rr, 192 * i : 192 * i + 64]
            k = MIX[rr, 192 * i + 64 : 192 * i + 128]
            v = MIX[rr, 192 * i + 128 : 192 * i + 192]
            sc = jnp.where(ok, dot_nt(q, k) * factor, -1e30)
            e = jnp.exp(sc - jnp.max(sc, axis=-1, keepdims=True))
            p = e * (1.0 / jnp.sum(e, axis=-1, keepdims=True))
            PROB[n, i] = p
            outs.append(dot_nn(p.astype(BF), v).astype(BF))
        CTX[rr, 0:128] = jnp.concatenate(outs[:2], axis=1)
        CTX[rr, 128:256] = jnp.concatenate(outs[2:], axis=1)
        return carry

    lax.fori_loop(0, 1, attend, 0)
    zag_relay(A_WI)

    zag_own(A_WB)
    lax.fori_loop(1, 2, attend, 0)
    spread(
        T_CTX, [(j, CTX.at[rows(rank[j], 128)], CALL.at[rows(rank[j], 128), rows(s, 256)]) for j in (1, 2, 3)],
        CTX.at[pl.ds(0, 384)],
    )
    CALL[:, rows(s, 256)] = CTX[...]
    got(size(384), pr.at[T_WO])
    send(WO.at[:, c], WO.at[:, c], cs.at[A_WO], cr.at[A_WO], partner)
    got(WO.at[:, 1 - c], cr.at[A_WO])
    got(CTX.at[pl.ds(0, 384)], pr.at[T_CTX])

    def proj(t, carry):
        cols = rows(t, 256)
        w = WO[:, :, :, :, cols].reshape(1024, 256)
        XH1[:, cols] = X[rows(s, 128), cols].astype(F32) + (dot_nn(CALL[rows(s, 128), :], w) + VEC[3:4, cols])
        return carry

    lax.fori_loop(0, 4, proj, 0)

    def own_rows(h, q):
        return pl.ds(pl.multiple_of(h * 256 + s * 64 + q * 32, 32), 32)

    def halves(h):
        return pl.ds(256 * h, 256)

    def mine_of(h):
        return pl.ds(pl.multiple_of(h * 256 + s * 64, 64), 64)

    def rank_of(h, j):
        return pl.ds(pl.multiple_of(h * 256 + rank[j] * 64, 64), 64)

    def norm_one(h):
        def body(q, carry):
            rr = rows(2 * h + q, 32)
            hid = XH1[rr, :]
            ctr = hid - jnp.mean(hid, axis=-1, keepdims=True)
            rstd = lax.rsqrt(jnp.mean(ctr * ctr, axis=-1, keepdims=True) + NORM_EPS)
            xh = ctr * rstd
            nf = xh * VEC[4:5, :] + VEC[5:6, :]
            XH1[rr, :] = xh
            RS1[rr, :] = jnp.broadcast_to(rstd, (32, 128))
            NF[rr, :] = nf
            N[own_rows(h, q), :] = nf.astype(BF)
            return carry

        lax.fori_loop(0, 2, body, 0)

    for h in (0, 1):
        norm_one(h)
        spread(T_N + h, [(j, N.at[mine_of(h)], N.at[mine_of(h)]) for j in (1, 2, 3)], size(192))

    def spread_ctx(tag, blocks):
        pieces = [
            (j, CTX.at[rows(i, 128)], CALL.at[rows(i, 128), rows(s, 256)]) for j in (1, 2, 3) for i in blocks(j)
        ]
        spread(tag, pieces, size(32 * len(pieces)))

    spread_ctx(T_CA, lambda j: [s])
    zag_near(A_WI)
    zag_relay(A_WB)
    zag_own(A_WB2)
    zag_far(A_WI)
    zag_core(A_WI)
    zag_relay(A_WB2)
    zag_own(A_WB3)

    def ffn_in(h):
        rr = halves(h)

        def body(t, carry):
            cols = rows(t, 256)
            pre = dot_nn(N[rr, :], WI[:, cols]) + IB[9:10, cols]
            cdf = 0.5 * (1.0 + lax.erf(pre * math.sqrt(0.5)))
            ACT[rr, cols] = (pre * cdf).astype(BF)
            DG[rr, cols] = cdf + pre * jnp.exp(-0.5 * (pre * pre)) * (1.0 / math.sqrt(2.0 * math.pi))
            return carry

        lax.fori_loop(0, 4, body, 0)

    def spread_cols(tag, piece, hs=(0, 1)):
        for h in hs:
            for j in (1, 2, 3):
                src, dst = piece(h, j)
                rc(src, dst, ps.at[tag], pr.at[tag], peer(j)).start()

    def ffn_out(k):
        start, wide = PARTS[k]
        part_cols = pl.ds(start, wide)
        for h in (0, 1):
            rr = halves(h)

            def body(t, carry):
                cols = rows(start // 256 + t, 256)
                part = dot_nn(ACT[rr, :], WB[:, cols])
                SB[rr, cols] = part.astype(BF)
                ACC[:, cols] = part
                return carry

            lax.fori_loop(0, wide // 256, body, 0)
            spread_cols(
                T_RSF + k, lambda h, j: (SB.at[rank_of(h, j), part_cols], RB.at[h, j - 1, :, part_cols]), (h,)
            )
            OWN[pl.ds(64 * h, 64), part_cols] = ACC[rows(s, 64), part_cols]
        drains.append(lambda: sent(size(384 * wide // 1024), ps.at[T_RSF + k]))

    for h in (0, 1):
        got(size(192), pr.at[T_N + h])
        ffn_in(h)
        if h == 0:
            zag_relay(A_WB3)
            zag_own(A_WB4)
    zag_relay(A_WB4)
    for k in range(4):
        zag_near(A_WB + k)
        zag_far(A_WB + k)
        zag_core(A_WB + k)
        ffn_out(k)
    GV[...] = jnp.zeros_like(GV)

    def norm_two(h):
        def body(q, carry):
            rr = rows(2 * h + q, 32)
            part = rows(q, 32)
            hid = OWN[rr, :] + RB[h, 0, part, :].astype(F32) + RB[h, 1, part, :].astype(F32)
            hid = NF[rr, :] + (hid + RB[h, 2, part, :].astype(F32) + VEC[6:7, :])
            ctr = hid - jnp.mean(hid, axis=-1, keepdims=True)
            rstd = lax.rsqrt(jnp.mean(ctr * ctr, axis=-1, keepdims=True) + NORM_EPS)
            xh = ctr * rstd
            OUT[rr, :] = (xh * VEC[7:8, :] + VEC[8:9, :]).astype(BF)
            place = (s % 2) * 128 + (2 * h + q) * 32 + lax.broadcasted_iota(jnp.int32, (32, 1), 0)
            seed = jnp.where(place < lens[s // 2], cot[rr, :].astype(F32), 0.0)
            GV[7:8, :] += jnp.sum(seed * xh, axis=0, keepdims=True)
            GV[8:9, :] += jnp.sum(seed, axis=0, keepdims=True)
            u = seed * VEC[7:8, :]
            gs = rstd * (u - jnp.mean(u, axis=-1, keepdims=True) - xh * jnp.mean(u * xh, axis=-1, keepdims=True))
            GV[6:7, :] += jnp.sum(gs, axis=0, keepdims=True)
            GS[rr, :] = gs
            G[own_rows(h, q), :] = gs.astype(BF)
            return carry

        lax.fori_loop(0, 2, body, 0)

    def g_piece(k):
        part = pl.ds(*GPARTS[k])
        return lambda h, j: (G.at[mine_of(h), part], G.at[mine_of(h), part])

    def g_size(k):
        return size(384 * GPARTS[k][1] // 1024)

    for k in range(4):
        got(size(384 * PARTS[k][1] // 1024), pr.at[T_RSF + k])
    for h in (0, 1):
        norm_two(h)
        spread_cols(T_G, g_piece(0), (h,))
    for k in (1, 2):
        spread_cols(T_G + k, g_piece(k))
    for k in range(3):
        drains.append(lambda k=k: sent(g_size(k), ps.at[T_G + k]))
    spread_ctx(T_CB, lambda j: [rank[i] for i in (1, 2, 3) if i != j])
    put(OUT, out_o, 0)

    def bwd_act(h):
        rr = halves(h)

        def body(t, carry):
            cols = rows(t, 256)
            gp = dot_nt(G[rr, :], WB[cols, :]) * DG[rr, cols]
            GV[9:10, cols] += jnp.sum(gp, axis=0, keepdims=True)
            GPB[rr, cols] = gp.astype(BF)
            return carry

        lax.fori_loop(0, 4, body, 0)

    def bwd_in(h):
        rr = halves(h)

        def body(t, carry):
            cols = rows(t, 256)
            part = dot_nt(GPB[rr, :], WI[cols, :])
            SB2[rr, cols] = part.astype(BF)
            ACC[:, cols] = part
            return carry

        lax.fori_loop(0, 4, body, 0)
        spread(T_RSB + h, [(j, SB2.at[rank_of(h, j)], RB2.at[h, j - 1]) for j in (1, 2, 3)], size(192))
        OWN[pl.ds(64 * h, 64), :] = ACC[rows(s, 64), :]

    def turn(i):
        return (3 - z + (4 - z) * i) % 5

    def core_start(tag, t, csend, crecv):
        rc(csend.at[t], crecv.at[t], cs2.at[tag], cr2.at[tag, t], partner).start()

    def wgrad(tag, lhs, rhs, mine, csend, crecv, cols):
        def body(i, carry):
            t = turn(i)
            ACC[:, 0:cols] = dot_tn(lhs[:, rows(t, 256)], rhs[...])
            csend[t] = ACC[rows(1 - c, 128), 0:cols].astype(BF)
            mine[t] = ACC[rows(c, 128), 0:cols]
            core_start(tag, t, csend, crecv)
            return carry

        lax.fori_loop(0, 4, body, 0)
        drains.append(lambda: sent(csend, cs2.at[tag]))

    def wgrad_back(k):
        tag, (start, wide) = R_GB + k, GPARTS[k]
        cols = pl.ds(start, wide)

        def body(i, carry):
            t = turn(i)
            ACC[:, 0:wide] = dot_tn(ACT[:, rows(t, 256)], G[:, cols])
            csB[t, :, cols] = ACC[rows(1 - c, 128), 0:wide].astype(BF)
            mB[t, :, cols] = ACC[rows(c, 128), 0:wide]
            rc(csB.at[t, :, cols], crB.at[t, :, cols], cs2.at[tag], cr2.at[tag, t], partner).start()
            return carry

        lax.fori_loop(0, 4, body, 0)
        drains.append(lambda: sent(csB.at[:, :, cols], cs2.at[tag]))

    def zrs_send(tag, t, zsend, zrecv, relay, sub):
        @pl.when(jnp.logical_or(t == pair, t == across))
        def _():
            rc(zsend.at[(t, *sub)], zrecv.at[(z, *sub)], zs2.at[tag], zr2.at[tag, 0], plane(t)).start()

        @pl.when(jnp.logical_and(outer, t == far_end))
        def _():
            rc(zsend.at[(t, *sub)], relay.at[sub], zs2.at[tag], zr2.at[tag, 1], plane(inward)).start()

    def zrs_drain(tag, zsend, sub):
        drains.append(lambda: sent(zsend.at[(pl.ds(0, 3), *sub)], zs2.at[tag]))

    def core_sum(tag, mine, crecv, zsend, zrecv, relay, sub):
        def body(i, carry):
            t = turn(i)
            got(crecv.at[(t, *sub)], cr2.at[tag, t])
            v = mine[(t, *sub)] + crecv[(t, *sub)].astype(F32)
            mine[(t, *sub)] = v
            zsend[(t, *sub)] = v.astype(BF)
            zrs_send(tag, t, zsend, zrecv, relay, sub)
            return carry

        lax.fori_loop(0, 4, body, 0)
        zrs_drain(tag, zsend, sub)

    def zrs_start(tag, zsend, zrecv, relay, sub):
        def body(i, carry):
            zrs_send(tag, turn(i), zsend, zrecv, relay, sub)
            return carry

        lax.fori_loop(0, 4, body, 0)

    def zrs_relay(tag, mine, zsend, zrecv, relay, sub):
        @pl.when(inner)
        def _():
            got(relay.at[sub], zr2.at[tag, 1])
            zsend[(far_end, *sub)] = (mine[(far_end, *sub)] + relay[sub].astype(F32)).astype(BF)
            rc(
                zsend.at[(far_end, *sub)], zrecv.at[(z, *sub)], zs2.at[tag], zr2.at[tag, 0], plane(far_end)
            ).start()

    def zrs_end(tag, mine, zrecv, res, sub):
        @pl.when(outer)
        def _():
            got(zrecv.at[(pl.ds(0, 2), *sub)], zr2.at[tag, 0])
            res[sub] = mine[(z, *sub)] + zrecv[(pair, *sub)].astype(F32) + zrecv[(across, *sub)].astype(F32)

        @pl.when(inner)
        def _():
            got(zrecv.at[(pl.ds(0, 3), *sub)], zr2.at[tag, 0])
            res[sub] = (
                mine[(z, *sub)] + zrecv[(pair, *sub)].astype(F32) + zrecv[(across, *sub)].astype(F32)
                + zrecv[(far_end, *sub)].astype(F32)
            )

    every = (pl.ds(0, 128),)
    back = [(pl.ds(0, 128), pl.ds(*part)) for part in GPARTS]

    def back_sum(k):
        core_sum(R_GB + k, mB, crB, zsB, zrB, rlB, back[k])

    def back_relay(k):
        zrs_relay(R_GB + k, mB, zsB, zrB, rlB, back[k])

    for k in range(3):
        got(g_size(k), pr.at[T_G + k])
        wgrad_back(k)
        if k < 2:
            back_sum(k)
    bwd_act(0)
    back_relay(0)
    back_sum(2)
    bwd_in(0)
    back_relay(1)
    bwd_act(1)
    bwd_in(1)
    wgrad(R_GI, N, GPB, mI, csI, crI, 1024)
    back_relay(2)
    core_sum(R_GI, mI, crI, zsI, zrI, rlI, every)

    def norm_one_bwd(h):
        def body(q, carry):
            rr = rows(2 * h + q, 32)
            part = rows(q, 32)
            gn = OWN[rr, :] + RB2[h, 0, part, :].astype(F32) + RB2[h, 1, part, :].astype(F32)
            gn = GS[rr, :] + (gn + RB2[h, 2, part, :].astype(F32))
            xh = XH1[rr, :]
            GV[4:5, :] += jnp.sum(gn * xh, axis=0, keepdims=True)
            GV[5:6, :] += jnp.sum(gn, axis=0, keepdims=True)
            u = gn * VEC[4:5, :]
            gf = RS1[rr, 0:1] * (
                u - jnp.mean(u, axis=-1, keepdims=True) - xh * jnp.mean(u * xh, axis=-1, keepdims=True)
            )
            GV[3:4, :] += jnp.sum(gf, axis=0, keepdims=True)
            GF[rr, :] = gf
            GFB[rr, :] = gf.astype(BF)
            return carry

        lax.fori_loop(0, 2, body, 0)

    got(size(192), pr.at[T_RSB])
    norm_one_bwd(0)
    got(size(192), pr.at[T_RSB2])
    norm_one_bwd(1)

    def gctx(t):
        GCS[t] = dot_nt(GFB[...], WO[t].reshape(256, 1024)).astype(BF)

    me = rows(s, 128)
    for j in (1, 2, 3):
        gctx(rank[j])
        rc(GCS.at[rank[j]], GC.at[me], ps.at[T_GC], pr.at[T_GC], peer(j)).start()
    drains.append(lambda: sent(CTX.at[pl.ds(0, 384)], ps.at[T_GC]))
    gctx(s)
    spread(T_GF, [(j, GFB.at[:, rows(rank[j], 256)], GFC.at[me]) for j in (1, 2, 3)], CTX.at[pl.ds(0, 384)])
    GC[me, :] = GCS[s]
    GFC[me, :] = GFB[:, rows(s, 256)]
    zrs_relay(R_GI, mI, zsI, zrI, rlI, every)
    got(CTX.at[pl.ds(0, 384)], pr.at[T_GC])

    BQ[...] = jnp.zeros_like(BQ)

    def attend_bwd(n, carry):
        rr = rows(n, 256)
        for two in range(2):
            parts = []
            for i in (2 * two, 2 * two + 1):
                q = MIX[rr, 192 * i : 192 * i + 64]
                k = MIX[rr, 192 * i + 64 : 192 * i + 128]
                v = MIX[rr, 192 * i + 128 : 192 * i + 192]
                gc = GC[rr, 64 * i : 64 * i + 64]
                p = PROB[n, i]
                gp = dot_nt(gc, v)
                inside = jnp.sum(p * gp, axis=-1, keepdims=True)
                gsc = (p * (gp - inside) * factor).astype(BF)
                parts += [dot_nn(gsc, k), dot_tn(gsc, q), dot_tn(p.astype(BF), gc)]
            both = jnp.concatenate([x.astype(BF) for x in parts], axis=1)
            GM[rr, 384 * two : 384 * two + 384] = both
            BQ[0:1, 384 * two : 384 * two + 384] += jnp.sum(both.astype(F32), axis=0, keepdims=True)
        return carry

    lax.fori_loop(0, 2, attend_bwd, 0)
    wgrad(R_GQ, X, GM, mQ, csQ, crQ, 768)
    for k in range(6):
        GV[k % 3 : k % 3 + 1, rows(2 * s + k // 3, 128)] = BQ[0:1, 128 * k : 128 * k + 128]
    for gg in range(8):
        GVC[gg % 2, gg // 2] = GV[:, 128 * gg : 128 * gg + 128]
    send(GVC.at[1 - c], RVC, cs2.at[R_SV], cr2.at[R_SV, 0], partner)
    core_sum(R_GQ, mQ, crQ, zsQ, zrQ, rlQ, every)
    got(RVC, cr2.at[R_SV, 0])
    TVZ[...] = GVC[c] + RVC[...]
    for k in (1, 2, 3):
        t = (z + k) % 4
        rc(TVZ.at[t], RVZ.at[k - 1], zs2.at[R_SV], zr2.at[R_SV, 0], plane(t)).start()
    drains.append(lambda: sent(RVZ, zs2.at[R_SV]))

    def gtok(rr, j):
        def body(t, carry):
            cols = rows(t, 256)
            part = dot_nt(GM[rr, :], WQ[cols, :])
            if j == 0:
                OWN[:, cols] = part
            else:
                SB3[j - 1, :, cols] = part.astype(BF)
            return carry

        lax.fori_loop(0, 4, body, 0)

    for j in (1, 2, 3):
        gtok(rows(rank[j], 128), j)
        rc(SB3.at[j - 1], RB3.at[j - 1], ps.at[T_GT], pr.at[T_GT], peer(j)).start()
    drains.append(lambda: sent(size(384), ps.at[T_GT]))
    zrs_relay(R_GQ, mQ, zsQ, zrQ, rlQ, every)
    gtok(me, 0)
    got(CTX.at[pl.ds(0, 384)], pr.at[T_GF])
    got(size(96), pr.at[T_CA])
    got(size(192), pr.at[T_CB])
    wgrad(R_GO, CALL, GFC, mO, csO, crO, 256)
    core_sum(R_GO, mO, crO, zsO, zrO, rlO, every)
    for k in range(3):
        zrs_end(R_GB + k, mB, zrB, GBF, back[k])
    put(GBF, gb_o, 1)
    zrs_end(R_GI, mI, zrI, resI, every)
    for j in (1, 2, 3):
        siI[j - 1] = resI[rows(rank[j], 32), :].astype(BF)
    spread(T_GI, [(j, siI.at[j - 1], riI.at[j - 1]) for j in (1, 2, 3)], riI)
    for i in range(8):
        GIF[:, rows(4 * i + s, 128)] = resI[rows(s, 32), 128 * i : 128 * i + 128]
    zrs_relay(R_GO, mO, zsO, zrO, rlO, every)
    got(size(384), pr.at[T_GT])

    def gtok_sum(t, carry):
        rr = rows(t, 32)
        h = OWN[rr, :] + RB3[0, rr, :].astype(F32) + RB3[1, rr, :].astype(F32) + RB3[2, rr, :].astype(F32)
        GTS[rr, :] = GF[rr, :] + h
        return carry

    lax.fori_loop(0, 4, gtok_sum, 0)
    put(GTS, gtok_o, 2)
    zrs_end(R_GQ, mQ, zrQ, resQ, every)
    for j in (1, 2, 3):
        siQ[j - 1] = resQ[rows(rank[j], 32), :].astype(BF)
    spread(T_GQ, [(j, siQ.at[j - 1], riQ.at[j - 1]) for j in (1, 2, 3)], riQ)
    got(RVZ, zr2.at[R_SV, 0])
    PV[...] = TVZ[z] + RVZ[0] + RVZ[1] + RVZ[2]
    spread(T_SV, [(j, PV, RVP.at[j - 1]) for j in (1, 2, 3)], RVP)
    got(riI, pr.at[T_GI])
    for j in (1, 2, 3):
        for i in range(8):
            GIF[:, rows(4 * i + rank[j], 128)] = riI[j - 1, :, 128 * i : 128 * i + 128].astype(F32)
    put(GIF, gi_o, 3)
    zrs_end(R_GO, mO, zrO, resO, every)
    for j in (1, 2, 3):
        siO[j - 1] = resO[rows(rank[j], 32), :].astype(BF)
    spread(T_GO, [(j, siO.at[j - 1], riO.at[j - 1]) for j in (1, 2, 3)], riO)
    got(RVP, pr.at[T_SV])
    tot = PV[...] + RVP[0] + RVP[1] + RVP[2]
    row = lax.broadcasted_iota(jnp.int32, (16, 128), 0)
    RVC[0] = jnp.where(row == 9, PV[...], tot)
    put(RVC.at[0], sv_o, 6)
    GQF[:, rows(s, 768)] = resQ[rows(s, 32), :]
    got(riQ, pr.at[T_GQ])
    for j in (1, 2, 3):
        GQF[:, rows(rank[j], 768)] = riQ[j - 1].astype(F32)
    put(GQF, gq_o, 5)
    GOF[:, rows(s, 256)] = resO[rows(s, 32), :]
    got(riO, pr.at[T_GO])
    for j in (1, 2, 3):
        GOF[:, rows(rank[j], 256)] = riO[j - 1].astype(F32)
    put(GOF, go_o, 4)
    for drain in drains:
        drain()


def hand_over(*refs):
    sources, targets, kept, (isem, osem) = refs[:7], refs[7:21], refs[21:36], refs[36:]
    s = lax.axis_index("seq")
    ins = [pltpu.make_async_copy(src, mid, isem.at[k]) for k, (src, mid) in enumerate(zip(sources, kept))]
    held = kept[:6] + kept[7:]
    outs = [pltpu.make_async_copy(mid, dst, osem.at[k]) for k, (mid, dst) in enumerate(zip(held, targets))]
    for k in (6, 0, 1, 2, 3, 4, 5):
        ins[k].start()
    qv, ob, g1, b1, ib, bb, g2, b2 = kept[7:]
    sums = kept[6]
    ins[6].wait()
    turned = pltpu.roll(sums[...], (128 - 32 * s) % 128, 1)
    for k, ref in ((3, ob), (4, g1), (5, b1), (6, bb), (7, g2), (8, b2)):
        ref[...] = turned[k : k + 1, 0:32]
    ib[...] = sums[9:10, :]
    line = jnp.where(s == 0, sums[0:1, :], jnp.where(s == 3, sums[2:3, :], sums[1:2, :]))
    qv[...] = jnp.where(s // 2 == 0, line[:, 0:64], line[:, 64:128])
    for k in range(6, 14):
        outs[k].start()
    for k in range(6):
        ins[k].wait()
        outs[k].start()
    for out in outs:
        out.wait()


def fused_shards(
    tokens, cotangent, slot_lengths, w_qkv, qv_bias, w_out, out_bias, ln1_gain, ln1_bias,
    w_in, in_bias, w_back, back_bias, ln2_gain, ln2_bias,
):
    vm = pltpu.VMEM
    dma = pltpu.SemaphoreType.DMA

    def item(n):
        return [
            vm((4, 128, n), F32), vm((4, 128, n), BF), vm((4, 128, n), BF),
            vm((4, 128, n), BF), vm((4, 128, n), BF), vm((128, n), BF),
        ]

    lengths = (64, 32, 32, 32, 128, 32, 32, 32)
    scratch = [vm((1, n), BF) for n in lengths]
    scratch += [
        vm((16, 128), BF), vm((16, 128), F32), vm((128, 1024), BF), vm((512, 1024), BF), vm((1024, 768), BF), vm((1024, 1024), BF), vm((1024, 1024), BF),
        vm((4, 2, 4, 32, 1024), BF), vm((4, 2, 4, 16, 128), BF), vm((16, 1024), F32), vm((16, 1024), F32),
        vm((8, 768), F32),
        vm((512, 768), BF), vm((2, 4, 256, 256), F32), vm((512, 256), BF), vm((512, 1024), BF),
        vm((128, 1024), F32), vm((128, 1024), F32), vm((128, 128), F32), vm((512, 1024), BF),
        vm((512, 1024), F32), vm((512, 1024), BF), vm((512, 1024), BF), vm((2, 3, 64, 1024), BF),
        vm((128, 1024), F32),
        vm((512, 1024), BF), vm((128, 1024), F32), vm((512, 1024), BF), vm((512, 1024), BF),
        vm((2, 3, 64, 1024), BF), vm((128, 1024), F32), vm((128, 1024), BF), vm((512, 256), BF), vm((4, 128, 256), BF),
        vm((512, 256), BF), vm((512, 768), BF), vm((3, 128, 1024), BF), vm((3, 128, 1024), BF),
        vm((256, 1024), F32),
    ]
    scratch += item(1024) + item(1024) + item(768) + item(256)
    scratch += [
        vm((3, 32, 1024), BF), vm((3, 32, 1024), BF), vm((3, 32, 768), BF), vm((3, 32, 768), BF),
        vm((3, 32, 256), BF), vm((3, 32, 256), BF),
        vm((128, 1024), F32), vm((128, 768), F32), vm((128, 256), F32),
        vm((16, 1024), F32), vm((2, 4, 16, 128), F32), vm((4, 16, 128), F32), vm((4, 16, 128), F32),
        vm((3, 16, 128), F32), vm((16, 128), F32), vm((3, 16, 128), F32),
        vm((128, 1024), BF), vm((128, 1024), F32), vm((32, 3072), F32), vm((32, 1024), F32),
        vm((32, 4096), F32), vm((128, 1024), F32),
        dma((8,)), dma((26,)), dma((26,)), dma((8,)), dma((8, 2)), dma((8,)), dma((8,)),
        dma((7,)), dma((7, 4)), dma((7,)), dma((7, 2)),
    ]
    shapes = [
        ((128, 1024), BF), ((128, 1024), F32), ((32, 3072), F32), ((32, 1024), F32),
        ((32, 4096), F32), ((128, 1024), F32), ((16, 128), F32),
    ]
    hbm = pl.BlockSpec(memory_space=pl.ANY)
    smem = pl.BlockSpec(memory_space=pltpu.SMEM)
    small = [v.reshape(1, -1) for v in (qv_bias, out_bias, ln1_gain, ln1_bias, in_bias, back_bias, ln2_gain, ln2_bias)]
    results = pl.pallas_call(
        layer_kernel,
        out_shape=[jax.ShapeDtypeStruct(a, b) for a, b in shapes],
        in_specs=[hbm] * 6 + [smem] + [hbm] * 8,
        out_specs=[hbm] * 7,
        scratch_shapes=scratch,
        compiler_params=pltpu.CompilerParams(
            collective_id=0, has_side_effects=True, vmem_limit_bytes=67_000_000
        ),
        name="encoder_layer",
    )(tokens, cotangent, w_qkv, w_out, w_in, w_back, slot_lengths, *small)
    final = pl.pallas_call(
        hand_over,
        out_shape=[jax.ShapeDtypeStruct(a, b) for a, b in shapes[:6]]
        + [jax.ShapeDtypeStruct((1, n), F32) for n in lengths],
        in_specs=[hbm] * 7,
        out_specs=[hbm] * 14,
        scratch_shapes=[vm(a, b) for a, b in shapes] + [vm((1, n), F32) for n in lengths] + [dma((7,)), dma((14,))],
        name="hand_over",
    )(*results)
    output, grad_tokens, grad_qkv, grad_wo, grad_wi, grad_wb = final[:6]
    qv, ob, g1, b1, ib, bb, g2, b2 = [v.reshape(-1) for v in final[6:]]
    return (output, grad_tokens, grad_qkv, qv, grad_wo, ob, g1, b1, grad_wi, ib, grad_wb, bb, g2, b2)


def solution(mesh):
    placed = (
        P(("grp", "seq"), None),
        P(("grp", "seq"), None),
        P("grp"),
        P(("grp", "seq"), None),
        P(("grp", "seq")),
        P(("grp", "seq"), None),
        P(("grp", "seq")),
        P(("grp", "seq")),
        P(("grp", "seq")),
        P(("grp", "seq"), None),
        P(("grp", "seq")),
        P(("grp", "seq"), None),
        P(("grp", "seq")),
        P(("grp", "seq")),
        P(("grp", "seq")),
    )
    fused = mesh.shape["grp"] == 2 * PLANES and mesh.shape["seq"] == RANKS
    return jax.shard_map(
        fused_shards if fused else shards,
        mesh=mesh,
        in_specs=placed,
        out_specs=(
            P(("grp", "seq"), None),
            P(("grp", "seq"), None),
            P(("grp", "seq"), None),
            P(("grp", "seq")),
            P(("grp", "seq"), None),
            P(("grp", "seq")),
            P(("grp", "seq")),
            P(("grp", "seq")),
            P(("grp", "seq"), None),
            P(("grp", "seq")),
            P(("grp", "seq"), None),
            P(("grp", "seq")),
            P(("grp", "seq")),
            P(("grp", "seq")),
        ),
        check_vma=False,
    )
```

```python
from functools import partial
import math

import jax
import jax.numpy as jnp
from jax import lax
from jax.experimental import pallas as pl
from jax.experimental.pallas import tpu as pltpu
from jax.sharding import PartitionSpec as P

D = 1024
H = 16
HD = 64
SLOT_DEV = 64
SLOTS = 2


NORM_EPS = 1e-06


def layer_norm(hidden, gain, shift):
    center = hidden - jnp.mean(hidden, axis=-1, keepdims=True)
    spread = jnp.mean(center * center, axis=-1, keepdims=True)
    return center * lax.rsqrt(spread + NORM_EPS) * gain + shift


def exact_gelu(values):
    return jax.nn.gelu(values, approximate=False)


def full_bias(pair_bias):
    pairs = pair_bias.reshape(H, 2, HD)
    return jnp.stack([pairs[:, 0], jnp.zeros_like(pairs[:, 0]), pairs[:, 1]], axis=1).reshape(3 * D)


def contract_rows(left, right):
    return lax.dot_general(
        left, right, (((0,), (0,)), ((), ())), preferred_element_type=jnp.float32
    )


def contract_cols(left, right):
    return lax.dot_general(
        left, right, (((1,), (1,)), ((), ())), preferred_element_type=jnp.float32
    )


def slot_scores(mixed, length, factor):
    slot_width = mixed.shape[0]
    queries = mixed[:, :, 0]
    key_rows = mixed[:, :, 1]
    value_rows = mixed[:, :, 2]
    products = jnp.einsum("qhd,khd->hqk", queries, key_rows, preferred_element_type=jnp.float32)
    key_valid = (jnp.arange(slot_width) < length)[None, None, :]
    scores = jnp.where(key_valid, products * factor, -1e30)
    return (queries, key_rows, value_rows, scores)


def slot_forward(item, factor):
    mixed, length = item
    queries, key_rows, value_rows, scores = slot_scores(mixed, length, factor)
    row_max = jnp.max(scores, axis=-1, keepdims=True)
    expon = jnp.exp(scores - row_max)
    total = jnp.sum(expon, axis=-1, keepdims=True)
    probs = expon / total
    context = jnp.einsum(
        "hqk,khd->qhd", probs.astype(jnp.bfloat16), value_rows, preferred_element_type=jnp.float32
    )
    return (context.astype(jnp.bfloat16), row_max + jnp.log(total))


def slot_backward(item, factor):
    mixed, grad_context, log_total, length = item
    queries, key_rows, value_rows, scores = slot_scores(mixed, length, factor)
    probs = jnp.exp(scores - log_total)
    grad_probs = jnp.einsum(
        "qhd,khd->hqk", grad_context, value_rows, preferred_element_type=jnp.float32
    )
    inner = jnp.sum(probs * grad_probs, axis=-1, keepdims=True)
    grad_scores = (probs * (grad_probs - inner) * factor).astype(jnp.bfloat16)
    grad_queries = jnp.einsum(
        "hqk,khd->qhd", grad_scores, key_rows, preferred_element_type=jnp.float32
    )
    grad_keys = jnp.einsum("hqk,qhd->khd", grad_scores, queries, preferred_element_type=jnp.float32)
    grad_values = jnp.einsum(
        "hqk,qhd->khd", probs.astype(jnp.bfloat16), grad_context, preferred_element_type=jnp.float32
    )
    return jnp.stack([grad_queries, grad_keys, grad_values], axis=2).astype(jnp.bfloat16)


def shards(
    tokens,
    cotangent,
    slot_lengths,
    w_qkv,
    qv_bias,
    w_out,
    out_bias,
    ln1_gain,
    ln1_bias,
    w_in,
    in_bias,
    w_back,
    back_bias,
    ln2_gain,
    ln2_bias,
):
    seq_count = lax.axis_size("seq")
    local_rows = tokens.shape[0]
    slot_width = SLOT_DEV * seq_count
    heads_here = H // seq_count
    factor = 1.0 / math.sqrt(HD)
    full_qkv, full_qv, full_out, full_obias, gain_one, shift_one = (
        lax.all_gather(w_qkv, ("grp", "seq"), axis=0, tiled=True),
        lax.all_gather(qv_bias, ("grp", "seq"), axis=0, tiled=True),
        lax.all_gather(w_out, ("grp", "seq"), axis=0, tiled=True),
        lax.all_gather(out_bias, ("grp", "seq"), axis=0, tiled=True),
        lax.all_gather(ln1_gain, ("grp", "seq"), axis=0, tiled=True),
        lax.all_gather(ln1_bias, ("grp", "seq"), axis=0, tiled=True),
    )
    full_in, full_ibias, full_back, full_bbias, gain_two, shift_two = (
        lax.all_gather(w_in, ("grp", "seq"), axis=0, tiled=True),
        lax.all_gather(in_bias, ("grp", "seq"), axis=0, tiled=True),
        lax.all_gather(w_back, ("grp", "seq"), axis=0, tiled=True),
        lax.all_gather(back_bias, ("grp", "seq"), axis=0, tiled=True),
        lax.all_gather(ln2_gain, ("grp", "seq"), axis=0, tiled=True),
        lax.all_gather(ln2_bias, ("grp", "seq"), axis=0, tiled=True),
    )
    mixed = (
        jnp.dot(tokens, full_qkv, preferred_element_type=jnp.float32) + full_bias(full_qv)
    ).astype(jnp.bfloat16)
    gathered = lax.all_to_all(mixed, "seq", split_axis=1, concat_axis=0, tiled=True)
    per_slot = gathered.reshape(SLOTS, slot_width, heads_here, 3, HD)
    contexts, log_totals = lax.map(partial(slot_forward, factor=factor), (per_slot, slot_lengths))
    context_heads = contexts.reshape(SLOTS * slot_width, heads_here * HD)
    context = lax.all_to_all(context_heads, "seq", split_axis=0, concat_axis=1, tiled=True)
    attended = jnp.dot(context, full_out, preferred_element_type=jnp.float32) + full_obias
    first_in = tokens.astype(jnp.float32) + attended
    normed, norm_one_pull = jax.vjp(layer_norm, first_in, gain_one, shift_one)
    normed_low = normed.astype(jnp.bfloat16)
    pre_act = jnp.dot(normed_low, full_in, preferred_element_type=jnp.float32) + full_ibias
    activated, gelu_pull = jax.vjp(exact_gelu, pre_act)
    act_low = activated.astype(jnp.bfloat16)
    ffn_out = jnp.dot(act_low, full_back, preferred_element_type=jnp.float32) + full_bbias
    output, norm_two_pull = jax.vjp(layer_norm, normed + ffn_out, gain_two, shift_two)
    row_index = lax.axis_index("seq") * local_rows + jnp.arange(local_rows)
    slot_index = row_index // slot_width
    place = row_index % slot_width
    row_length = jnp.sum(
        jnp.where(slot_index[:, None] == jnp.arange(SLOTS)[None, :], slot_lengths[None, :], 0),
        axis=1,
    )
    row_valid = (place < row_length).astype(jnp.float32)
    seed_grad = cotangent.astype(jnp.float32) * row_valid[:, None]
    grad_second, grad_gain_two, grad_shift_two = norm_two_pull(seed_grad)
    grad_ffn_low = grad_second.astype(jnp.bfloat16)
    grad_back_w = contract_rows(act_low, grad_ffn_low)
    grad_back_b = jnp.sum(grad_second, axis=0)
    (grad_pre,) = gelu_pull(contract_cols(grad_ffn_low, full_back))
    grad_pre_low = grad_pre.astype(jnp.bfloat16)
    grad_in_w = contract_rows(normed_low, grad_pre_low)
    grad_in_b = jnp.sum(grad_pre, axis=0)
    grad_normed = grad_second + contract_cols(grad_pre_low, full_in)
    grad_first, grad_gain_one, grad_shift_one = norm_one_pull(grad_normed)
    grad_attn_low = grad_first.astype(jnp.bfloat16)
    grad_out_w = contract_rows(context, grad_attn_low)
    grad_out_b = jnp.sum(grad_first, axis=0)
    grad_context = contract_cols(grad_attn_low, full_out).astype(jnp.bfloat16)
    grad_heads = lax.all_to_all(grad_context, "seq", split_axis=1, concat_axis=0, tiled=True)
    grad_slots = grad_heads.reshape(SLOTS, slot_width, heads_here, HD)
    grad_mixed_heads = lax.map(
        partial(slot_backward, factor=factor), (per_slot, grad_slots, log_totals, slot_lengths)
    )
    grad_mixed = lax.all_to_all(
        grad_mixed_heads.reshape(SLOTS * slot_width, heads_here * 3 * HD),
        "seq",
        split_axis=0,
        concat_axis=1,
        tiled=True,
    )
    grad_qkv_w = contract_rows(tokens, grad_mixed)
    summed_bias = jnp.sum(grad_mixed.astype(jnp.float32), axis=0).reshape(H, 3, HD)
    grad_qv = jnp.stack([summed_bias[:, 0], summed_bias[:, 2]], axis=1).reshape(2 * D)
    input_grad = grad_first + contract_cols(grad_mixed, full_qkv)
    sums = (
        lax.psum_scatter(grad_qkv_w, ("grp", "seq"), scatter_dimension=0, tiled=True),
        lax.psum_scatter(grad_qv, ("grp", "seq"), scatter_dimension=0, tiled=True),
        lax.psum_scatter(grad_out_w, ("grp", "seq"), scatter_dimension=0, tiled=True),
        lax.psum_scatter(grad_out_b, ("grp", "seq"), scatter_dimension=0, tiled=True),
        lax.psum_scatter(
            grad_gain_one.astype(jnp.float32), ("grp", "seq"), scatter_dimension=0, tiled=True
        ),
        lax.psum_scatter(
            grad_shift_one.astype(jnp.float32), ("grp", "seq"), scatter_dimension=0, tiled=True
        ),
        lax.psum_scatter(grad_in_w, ("grp", "seq"), scatter_dimension=0, tiled=True),
        lax.psum_scatter(grad_in_b, ("grp", "seq"), scatter_dimension=0, tiled=True),
        lax.psum_scatter(grad_back_w, ("grp", "seq"), scatter_dimension=0, tiled=True),
        lax.psum_scatter(grad_back_b, ("grp", "seq"), scatter_dimension=0, tiled=True),
        lax.psum_scatter(
            grad_gain_two.astype(jnp.float32), ("grp", "seq"), scatter_dimension=0, tiled=True
        ),
        lax.psum_scatter(
            grad_shift_two.astype(jnp.float32), ("grp", "seq"), scatter_dimension=0, tiled=True
        ),
    )
    return (
        output.astype(jnp.bfloat16),
        input_grad,
        sums[0],
        sums[1],
        sums[2],
        sums[3],
        sums[4],
        sums[5],
        sums[6],
        sums[7],
        sums[8],
        sums[9],
        sums[10],
        sums[11],
    )


BF = jnp.bfloat16
F32 = jnp.float32
MESH = pl.DeviceIdType.MESH
PLANES = 4
RANKS = 4
(
    T_PACK, T_WQ, T_WI, T_TOK, T_WO, T_CTX, T_CA, T_CB, T_N, T_N2, T_RSF, T_RSF2, T_RSF3, T_RSF4,
    T_G, T_G2, T_G3, T_RSB, T_RSB2, T_GC, T_GF, T_GO, T_GT, T_GI, T_GQ, T_SV,
) = range(26)
(A_PACK, A_WO, A_WQ, A_WI, A_WB, A_WB2, A_WB3, A_WB4) = range(8)
(R_GB, R_GB2, R_GB3, R_GI, R_GO, R_GQ, R_SV) = range(7)
PARTS = ((0, 256), (256, 256), (512, 256), (768, 256))
GPARTS = ((0, 384), (384, 384), (768, 256))


def dot_nn(a, b):
    return jnp.dot(a, b, preferred_element_type=F32)


def dot_nt(a, b):
    return lax.dot_general(a, b, (((1,), (1,)), ((), ())), preferred_element_type=F32)


def dot_tn(a, b):
    return lax.dot_general(a, b, (((0,), (0,)), ((), ())), preferred_element_type=F32)


def layer_kernel(
    x_in, cot_in, wq_in, wo_in, wi_in, wb_in, lens, *refs
):
    (
        small_in, (out_o, gtok_o, gq_o, go_o, gi_o, gb_o, sv_o), small,
        (
            pack, packf, cot, X, WQ, WI, WB, WO, PK, VEC, IB, BQ,
            MIX, PROB, CTX, CALL, XH1, NF, RS1, N, DG, ACT, SB, RB, OWN,
            G, GS, GPB, SB2, RB2, GF, GFB, GFC, GCS, GC, GM, SB3, RB3,
            ACC,
            mB, csB, crB, zsB, zrB, rlB,
            mI, csI, crI, zsI, zrI, rlI,
            mQ, csQ, crQ, zsQ, zrQ, rlQ,
            mO, csO, crO, zsO, zrO, rlO,
            siI, riI, siQ, riQ, siO, riO, resI, resQ, resO,
            GV, GVC, RVC, TVZ, RVZ, PV, RVP,
            OUT, GTS, GQF, GOF, GIF, GBF,
            osem, ps, pr, zs, zr, cs, cr, cs2, cr2, zs2, zr2,
        ),
    ) = refs[:8], refs[8:15], refs[15:23], refs[23:]
    g = lax.axis_index("grp")
    s = lax.axis_index("seq")
    z = g // 2
    c = g % 2
    rank = {1: s + 1 - 2 * (s % 2), 2: (s + 2) % 4, 3: 3 - s}
    partner = (g + 1 - 2 * c, s)
    inner = jnp.logical_and(z >= 1, z <= 2)
    outer = jnp.logical_or(z == 0, z == 3)
    two_off, inward, outward = (z + 2) % 4, 1 + z % 2, 3 * (z // 2)
    pair, across, far_end = z + 1 - 2 * (z % 2), 2 - z // 2, 3 * (1 - z // 2)
    is_outer = (z // 2 + z % 2 + 1) % 2
    drains = []

    def peer(j):
        return (g, rank[j])

    def plane(t):
        return (2 * t + c, s)

    def rc(src, dst, ss, rs, dev):
        return pltpu.make_async_remote_copy(
            src_ref=src, dst_ref=dst, send_sem=ss, recv_sem=rs, device_id=dev, device_id_type=MESH
        )

    def got(dst, rs):
        rc(dst, dst, osem.at[0], rs, partner).wait_recv()

    def sent(src, ss):
        rc(src, src, ss, pr.at[0], partner).wait_send()

    def send(src, dst, ss, rs, dev):
        rc(src, dst, ss, rs, dev).start()
        drains.append(lambda: sent(src, ss))

    def spread(tag, pieces, total):
        for j, src, dst in pieces:
            rc(src, dst, ps.at[tag], pr.at[tag], peer(j)).start()
        drains.append(lambda: sent(total, ps.at[tag]))

    def put(src, dst, k):
        pltpu.make_async_copy(src, dst, osem.at[k]).start()
        drains.append(lambda: pltpu.make_async_copy(src, dst, osem.at[k]).wait())

    def rows(i, n):
        return pl.ds(pl.multiple_of(i * n, n), n)

    def size(n):
        return X.at[pl.ds(0, n)]

    bar = pltpu.get_barrier_semaphore()
    for j in (1, 2, 3):
        pl.semaphore_signal(bar, inc=1, device_id=peer(j), device_id_type=MESH)
    for k in (1, 2, 3):
        pl.semaphore_signal(bar, inc=1, device_id=plane((z + k) % 4), device_id_type=MESH)
    pl.semaphore_signal(bar, inc=1, device_id=partner, device_id_type=MESH)
    small_cp = [pltpu.make_async_copy(small_in[k], small[k], ps.at[8 + k]) for k in range(8)]
    for cp in small_cp:
        cp.start()
    wo_cp = pltpu.make_async_copy(wo_in, WO.at[z, c, s], osem.at[2])
    local = [
        pltpu.make_async_copy(wq_in.at[:, rows(s, 768)], WQ.at[rows(4 * g + s, 32)], osem.at[1]),
        pltpu.make_async_copy(x_in, X.at[rows(s, 128)], osem.at[0]),
        pltpu.make_async_copy(wb_in, WB.at[rows(g, 128)], osem.at[3]),
        pltpu.make_async_copy(cot_in, cot, osem.at[4]),
    ]
    for cp in [wo_cp] + local:
        cp.start()
    for i in range(8):
        pltpu.make_async_copy(
            wi_in.at[:, rows(4 * i + s, 128)], WI.at[rows(4 * g + s, 32), pl.ds(128 * i, 128)], osem.at[5]
        ).start()
    lane = lax.broadcasted_iota(jnp.int32, (1, 128), 1)
    for cp in small_cp:
        cp.wait()
    qv_in, ob_in, g1_in, b1_in, ib_in, bb_in, g2_in, b2_in = small
    packf[...] = jnp.zeros_like(packf)
    twice = jnp.concatenate([qv_in[...].astype(F32)] * 2, axis=1)
    for k in range(3):
        packf[k : k + 1, :] = jnp.where(lane // 64 + 4 * ((s + 1) // 2) == s // 2 + 4 * k, twice, 0.0)
    for k, ref in ((3, ob_in), (4, g1_in), (5, b1_in), (6, bb_in), (7, g2_in), (8, b2_in)):
        four = jnp.concatenate([ref[...].astype(F32)] * 4, axis=1)
        packf[k : k + 1, :] = jnp.where(lane // 32 == s, four, 0.0)
    packf[9:10, :] = ib_in[...].astype(F32)
    pack[...] = packf[...].astype(BF)
    PK[z, c, s] = pack[...]
    pl.semaphore_wait(bar, 7)

    def ck(ref):
        return lambda o, cc: ref.at[rows(2 * o + cc, 128)]

    chunk = {
        A_PACK: lambda o, cc: PK.at[o, cc],
        A_WO: lambda o, cc: WO.at[o, cc, s],
        A_WQ: ck(WQ),
        A_WI: ck(WI),
    }
    for k, part in enumerate(PARTS):
        chunk[A_WB + k] = lambda o, cc, part=part: WB.at[rows(2 * o + cc, 128), pl.ds(*part)]
    chunks = {
        A_PACK: lambda n: PK.at[pl.ds(0, n), 0],
        A_WO: lambda n: size(32 * n),
        A_WQ: lambda n: WQ.at[pl.ds(0, 128 * n)],
        A_WI: lambda n: size(128 * n),
    }
    for k, (_, wide) in enumerate(PARTS):
        chunks[A_WB + k] = lambda n, wide=wide: size(128 * n * wide // 1024)

    def zag_one(tag, o, t, far, ref=None):
        ref = chunk[tag](o, c) if ref is None else ref
        rc(ref, ref, zs.at[tag], zr.at[tag, far], plane(t)).start()

    def zag_start(tag, pieces=(None,)):
        for ref in pieces:
            zag_one(tag, z, two_off, is_outer, ref)
        for ref in pieces:
            zag_one(tag, z, inward, 0, ref)

        def drain():
            @pl.when(inner)
            def _():
                sent(chunks[tag](4), zs.at[tag])

            @pl.when(outer)
            def _():
                sent(chunks[tag](2), zs.at[tag])

        drains.append(drain)

    def zag_outward(tag):
        @pl.when(inner)
        def _():
            zag_one(tag, z, outward, 0)

    def zag_ffn(tag):
        zag_one(tag, z, two_off, is_outer)
        zag_one(tag, z, inward, 0)
        zag_outward(tag)

    def zag_own(tag):
        @pl.when(inner)
        def _():
            for t in (two_off, inward, outward):
                zag_one(tag, z, t, 0)

    def core_send(tag, o):
        ref = chunk[tag](o, c)
        rc(ref, ref, cs.at[tag], cr.at[tag], partner).start()

    def zag_relay(tag, core=True):
        @pl.when(inner)
        def _():
            got(chunk[tag](far_end, c), zr.at[tag, 1])
            zag_one(tag, far_end, outward, 1)
            if core:
                core_send(tag, far_end)

    def zag_near(tag, core=True):
        got(chunks[tag](2), zr.at[tag, 0])
        if core:
            core_send(tag, pair)
            core_send(tag, across)

    def zag_far(tag, core=True):
        @pl.when(outer)
        def _():
            got(chunk[tag](far_end, c), zr.at[tag, 1])
            if core:
                core_send(tag, far_end)

    def zag_core(tag):
        got(chunks[tag](4), cr.at[tag])
        drains.append(lambda: sent(chunks[tag](4), cs.at[tag]))

    spread(T_PACK, [(j, pack, PK.at[z, c, s]) for j in (1, 2, 3)], PK.at[0, 0, pl.ds(0, 3)])
    spread(
        T_WQ, [(j, wq_in.at[:, rows(rank[j], 768)], WQ.at[rows(4 * g + s, 32)]) for j in (1, 2, 3)],
        WQ.at[pl.ds(0, 96)],
    )
    wo_cp.wait()
    zag_start(A_WO)
    zag_outward(A_WO)
    local[0].wait()
    zag_one(A_WQ, z, two_off, is_outer, WQ.at[rows(4 * g + s, 32)])
    zag_one(A_WQ, z, inward, 0, WQ.at[rows(4 * g + s, 32)])
    spread(
        T_WI,
        [
            (
                j, wi_in.at[:, rows(4 * i + rank[j], 128)],
                WI.at[rows(4 * g + s, 32), pl.ds(128 * i, 128)],
            )
            for j in (1, 2, 3)
            for i in range(8)
        ],
        size(96),
    )
    spread(T_TOK, [(j, x_in, X.at[rows(s, 128)]) for j in (1, 2, 3)], size(384))
    for cp in local[1:]:
        cp.wait()
    got(PK.at[0, 0, pl.ds(0, 3)], pr.at[T_PACK])
    zag_start(A_PACK)
    zag_outward(A_PACK)
    core_send(A_PACK, z)
    got(WQ.at[pl.ds(0, 96)], pr.at[T_WQ])
    zag_start(A_WQ, [WQ.at[rows(4 * g + rank[j], 32)] for j in (1, 2, 3)])
    core_send(A_WQ, z)
    for tag in (A_WB, A_WB2, A_WB3, A_WB4):
        core_send(tag, z)

    def wo_plane(o):
        for j in (1, 2, 3):
            ref = WO.at[o, c, s]
            rc(ref, ref, ps.at[T_WO], pr.at[T_WO], peer(j)).start()

    zag_relay(A_WO, core=False)
    zag_relay(A_PACK)
    zag_outward(A_WQ)
    wo_plane(z)

    @pl.when(inner)
    def _():
        wo_plane(far_end)

    zag_near(A_WO, core=False)
    wo_plane(pair)
    wo_plane(across)
    zag_near(A_PACK)
    got(size(96), pr.at[T_WI])
    wi_own = WI.at[rows(4 * g + s, 32)]
    pltpu.make_async_copy(wi_own, wi_own, osem.at[5]).wait()
    core_send(A_WI, z)

    zag_relay(A_WQ)

    zag_outward(A_WI)
    def drain_ffn():
        for tag in (A_WI, A_WB, A_WB2, A_WB3, A_WB4):
            @pl.when(inner)
            def _():
                sent(chunks[tag](4), zs.at[tag])

            @pl.when(outer)
            def _():
                sent(chunks[tag](2), zs.at[tag])

    drains.append(drain_ffn)
    zag_far(A_PACK)
    zag_far(A_WO, core=False)

    @pl.when(outer)
    def _():
        wo_plane(far_end)

    drains.append(lambda: sent(size(384), ps.at[T_WO]))
    zag_near(A_WQ)

    @pl.when(outer)
    def _():
        for tag in (A_WI, A_WB, A_WB2, A_WB3, A_WB4):
            zag_one(tag, z, two_off, 1)
            zag_one(tag, z, inward, 0)


    @pl.when(inner)
    def _():
        zag_one(A_WI, z, two_off, 0)
        zag_one(A_WI, z, inward, 0)

    zag_own(A_WB)
    zag_core(A_PACK)
    for gg in range(8):
        tot = PK[gg // 2, gg % 2, 0].astype(F32)
        for r in (1, 2, 3):
            tot = tot + PK[gg // 2, gg % 2, r].astype(F32)
        VEC[:, gg * 128 : (gg + 1) * 128] = tot
        IB[:, gg * 128 : (gg + 1) * 128] = PK[gg // 2, gg % 2, s].astype(F32)
    for cc in range(2):
        tot = PK[s, cc, 0].astype(F32)
        for r in (1, 2, 3):
            tot = tot + PK[s, cc, r].astype(F32)
        for k in range(3):
            BQ[0:1, (3 * cc + k) * 128 : (3 * cc + k + 1) * 128] = tot[k : k + 1, :]
    zag_far(A_WQ)
    got(size(384), pr.at[T_TOK])
    zag_core(A_WQ)

    def qkv(t, carry):
        cols = rows(t, 256)
        MIX[:, cols] = (dot_nn(X[...], WQ[:, cols]) + BQ[0:1, cols]).astype(BF)
        return carry

    lax.fori_loop(0, 3, qkv, 0)

    factor = 1.0 / math.sqrt(HD)

    def attend(n, carry):
        rr = rows(n, 256)
        ok = lax.broadcasted_iota(jnp.int32, (1, 256), 1) < lens[n]
        outs = []
        for i in range(4):
            q = MIX[rr, 192 * i : 192 * i + 64]
            k = MIX[rr, 192 * i + 64 : 192 * i + 128]
            v = MIX[rr, 192 * i + 128 : 192 * i + 192]
            sc = jnp.where(ok, dot_nt(q, k) * factor, -1e30)
            e = jnp.exp(sc - jnp.max(sc, axis=-1, keepdims=True))
            p = e * (1.0 / jnp.sum(e, axis=-1, keepdims=True))
            PROB[n, i] = p
            outs.append(dot_nn(p.astype(BF), v).astype(BF))
        CTX[rr, 0:128] = jnp.concatenate(outs[:2], axis=1)
        CTX[rr, 128:256] = jnp.concatenate(outs[2:], axis=1)
        return carry

    lax.fori_loop(0, 1, attend, 0)
    zag_relay(A_WI)

    zag_own(A_WB2)
    lax.fori_loop(1, 2, attend, 0)
    spread(
        T_CTX, [(j, CTX.at[rows(rank[j], 128)], CALL.at[rows(rank[j], 128), rows(s, 256)]) for j in (1, 2, 3)],
        CTX.at[pl.ds(0, 384)],
    )
    CALL[:, rows(s, 256)] = CTX[...]
    got(size(384), pr.at[T_WO])
    send(WO.at[:, c], WO.at[:, c], cs.at[A_WO], cr.at[A_WO], partner)
    got(WO.at[:, 1 - c], cr.at[A_WO])
    got(CTX.at[pl.ds(0, 384)], pr.at[T_CTX])

    zag_relay(A_WB)
    zag_own(A_WB3)
    def proj(t, carry):
        cols = rows(t, 256)
        w = WO[:, :, :, :, cols].reshape(1024, 256)
        XH1[:, cols] = X[rows(s, 128), cols].astype(F32) + (dot_nn(CALL[rows(s, 128), :], w) + VEC[3:4, cols])
        return carry

    lax.fori_loop(0, 4, proj, 0)

    def own_rows(h, q):
        return pl.ds(pl.multiple_of(h * 256 + s * 64 + q * 32, 32), 32)

    def halves(h):
        return pl.ds(256 * h, 256)

    def mine_of(h):
        return pl.ds(pl.multiple_of(h * 256 + s * 64, 64), 64)

    def rank_of(h, j):
        return pl.ds(pl.multiple_of(h * 256 + rank[j] * 64, 64), 64)

    def norm_one(h):
        def body(q, carry):
            rr = rows(2 * h + q, 32)
            hid = XH1[rr, :]
            ctr = hid - jnp.mean(hid, axis=-1, keepdims=True)
            rstd = lax.rsqrt(jnp.mean(ctr * ctr, axis=-1, keepdims=True) + NORM_EPS)
            xh = ctr * rstd
            nf = xh * VEC[4:5, :] + VEC[5:6, :]
            XH1[rr, :] = xh
            RS1[rr, :] = jnp.broadcast_to(rstd, (32, 128))
            NF[rr, :] = nf
            N[own_rows(h, q), :] = nf.astype(BF)
            return carry

        lax.fori_loop(0, 2, body, 0)

    for h in (0, 1):
        norm_one(h)
        spread(T_N + h, [(j, N.at[mine_of(h)], N.at[mine_of(h)]) for j in (1, 2, 3)], size(192))

    def spread_ctx(tag, blocks):
        pieces = [
            (j, CTX.at[rows(i, 128)], CALL.at[rows(i, 128), rows(s, 256)]) for j in (1, 2, 3) for i in blocks(j)
        ]
        spread(tag, pieces, size(32 * len(pieces)))

    zag_near(A_WI)
    zag_relay(A_WB2)
    zag_own(A_WB4)
    zag_far(A_WI)
    zag_core(A_WI)
    zag_relay(A_WB3)

    def ffn_in(h):
        rr = halves(h)

        def body(t, carry):
            cols = rows(t, 256)
            pre = dot_nn(N[rr, :], WI[:, cols]) + IB[9:10, cols]
            cdf = 0.5 * (1.0 + lax.erf(pre * math.sqrt(0.5)))
            ACT[rr, cols] = (pre * cdf).astype(BF)
            DG[rr, cols] = cdf + pre * jnp.exp(-0.5 * (pre * pre)) * (1.0 / math.sqrt(2.0 * math.pi))
            return carry

        lax.fori_loop(0, 4, body, 0)

    def spread_cols(tag, piece, hs=(0, 1)):
        for h in hs:
            for j in (1, 2, 3):
                src, dst = piece(h, j)
                rc(src, dst, ps.at[tag], pr.at[tag], peer(j)).start()

    def ffn_out(k):
        start, wide = PARTS[k]
        part_cols = pl.ds(start, wide)
        for h in (0, 1):
            rr = halves(h)

            def body(t, carry):
                cols = rows(start // 256 + t, 256)
                part = dot_nn(ACT[rr, :], WB[:, cols])
                SB[rr, cols] = part.astype(BF)
                ACC[:, cols] = part
                return carry

            lax.fori_loop(0, wide // 256, body, 0)
            spread_cols(
                T_RSF + k, lambda h, j: (SB.at[rank_of(h, j), part_cols], RB.at[h, j - 1, :, part_cols]), (h,)
            )
            OWN[pl.ds(64 * h, 64), part_cols] = ACC[rows(s, 64), part_cols]
        drains.append(lambda: sent(size(384 * wide // 1024), ps.at[T_RSF + k]))

    for h in (0, 1):
        got(size(192), pr.at[T_N + h])
        ffn_in(h)
        if h == 0:
            zag_relay(A_WB4)
            zag_near(A_WB)
            zag_far(A_WB)
    for k in range(4):
        if k >= 1:
            zag_near(A_WB + k)
            zag_far(A_WB + k)
        zag_core(A_WB + k)
        ffn_out(k)
    GV[...] = jnp.zeros_like(GV)

    def norm_two(h):
        def body(q, carry):
            rr = rows(2 * h + q, 32)
            part = rows(q, 32)
            hid = OWN[rr, :] + RB[h, 0, part, :].astype(F32) + RB[h, 1, part, :].astype(F32)
            hid = NF[rr, :] + (hid + RB[h, 2, part, :].astype(F32) + VEC[6:7, :])
            ctr = hid - jnp.mean(hid, axis=-1, keepdims=True)
            rstd = lax.rsqrt(jnp.mean(ctr * ctr, axis=-1, keepdims=True) + NORM_EPS)
            xh = ctr * rstd
            OUT[rr, :] = (xh * VEC[7:8, :] + VEC[8:9, :]).astype(BF)
            place = (s % 2) * 128 + (2 * h + q) * 32 + lax.broadcasted_iota(jnp.int32, (32, 1), 0)
            seed = jnp.where(place < lens[s // 2], cot[rr, :].astype(F32), 0.0)
            GV[7:8, :] += jnp.sum(seed * xh, axis=0, keepdims=True)
            GV[8:9, :] += jnp.sum(seed, axis=0, keepdims=True)
            u = seed * VEC[7:8, :]
            gs = rstd * (u - jnp.mean(u, axis=-1, keepdims=True) - xh * jnp.mean(u * xh, axis=-1, keepdims=True))
            GV[6:7, :] += jnp.sum(gs, axis=0, keepdims=True)
            GS[rr, :] = gs
            G[own_rows(h, q), :] = gs.astype(BF)
            return carry

        lax.fori_loop(0, 2, body, 0)

    def g_piece(k):
        part = pl.ds(*GPARTS[k])
        return lambda h, j: (G.at[mine_of(h), part], G.at[mine_of(h), part])

    def g_size(k):
        return size(384 * GPARTS[k][1] // 1024)

    for k in range(4):
        got(size(384 * PARTS[k][1] // 1024), pr.at[T_RSF + k])
    for h in (0, 1):
        norm_two(h)
        spread_cols(T_G, g_piece(0), (h,))
    for k in (1, 2):
        spread_cols(T_G + k, g_piece(k))
    for k in range(3):
        drains.append(lambda k=k: sent(g_size(k), ps.at[T_G + k]))
    spread_ctx(T_CA, lambda j: [s])
    put(OUT, out_o, 0)

    def act_first():
        def body(t, carry):
            cols = rows(t, 256)
            mI[:, :, cols] = dot_nt(G[:, 0:768], WB[cols, 0:768]).reshape(4, 128, 256)
            return carry

        lax.fori_loop(0, 4, body, 0)

    def bwd_act(h):
        rr = halves(h)

        def body(t, carry):
            cols = rows(t, 256)
            gp = mI[2 * h : 2 * h + 2, :, cols].reshape(256, 256)
            gp = (gp + dot_nt(G[rr, 768:1024], WB[cols, 768:1024])) * DG[rr, cols]
            GV[9:10, cols] += jnp.sum(gp, axis=0, keepdims=True)
            GPB[rr, cols] = gp.astype(BF)
            return carry

        lax.fori_loop(0, 4, body, 0)

    def bwd_in(h):
        rr = halves(h)

        def body(t, carry):
            cols = rows(t, 256)
            part = dot_nt(GPB[rr, :], WI[cols, :])
            SB2[rr, cols] = part.astype(BF)
            ACC[:, cols] = part
            return carry

        lax.fori_loop(0, 4, body, 0)
        spread(T_RSB + h, [(j, SB2.at[rank_of(h, j)], RB2.at[h, j - 1]) for j in (1, 2, 3)], size(192))
        OWN[pl.ds(64 * h, 64), :] = ACC[rows(s, 64), :]

    def turn(i):
        return (3 - z + (4 - z) * i) % 5

    def core_start(tag, t, csend, crecv):
        rc(csend.at[t], crecv.at[t], cs2.at[tag], cr2.at[tag, t], partner).start()

    def wgrad(tag, lhs, rhs, mine, csend, crecv, cols):
        def body(i, carry):
            t = turn(i)
            ACC[:, 0:cols] = dot_tn(lhs[:, rows(t, 256)], rhs[...])
            csend[t] = ACC[rows(1 - c, 128), 0:cols].astype(BF)
            mine[t] = ACC[rows(c, 128), 0:cols]
            core_start(tag, t, csend, crecv)
            return carry

        lax.fori_loop(0, 4, body, 0)
        drains.append(lambda: sent(csend, cs2.at[tag]))

    def wgrad_back(k):
        tag, (start, wide) = R_GB + k, GPARTS[k]
        cols = pl.ds(start, wide)

        def body(i, carry):
            t = turn(i)
            ACC[:, 0:wide] = dot_tn(ACT[:, rows(t, 256)], G[:, cols])
            csB[t, :, cols] = ACC[rows(1 - c, 128), 0:wide].astype(BF)
            mB[t, :, cols] = ACC[rows(c, 128), 0:wide]
            rc(csB.at[t, :, cols], crB.at[t, :, cols], cs2.at[tag], cr2.at[tag, t], partner).start()
            return carry

        lax.fori_loop(0, 4, body, 0)
        drains.append(lambda: sent(csB.at[:, :, cols], cs2.at[tag]))

    def zrs_send(tag, t, zsend, zrecv, relay, sub):
        @pl.when(jnp.logical_or(t == pair, t == across))
        def _():
            rc(zsend.at[(t, *sub)], zrecv.at[(z, *sub)], zs2.at[tag], zr2.at[tag, 0], plane(t)).start()

        @pl.when(jnp.logical_and(outer, t == far_end))
        def _():
            rc(zsend.at[(t, *sub)], relay.at[sub], zs2.at[tag], zr2.at[tag, 1], plane(inward)).start()

    def zrs_drain(tag, zsend, sub):
        drains.append(lambda: sent(zsend.at[(pl.ds(0, 3), *sub)], zs2.at[tag]))

    def core_sum(tag, mine, crecv, zsend, zrecv, relay, sub, start=True):
        def body(i, carry):
            t = turn(i)
            got(crecv.at[(t, *sub)], cr2.at[tag, t])
            v = mine[(t, *sub)] + crecv[(t, *sub)].astype(F32)
            mine[(t, *sub)] = v
            zsend[(t, *sub)] = v.astype(BF)
            if start:
                zrs_send(tag, t, zsend, zrecv, relay, sub)
            return carry

        lax.fori_loop(0, 4, body, 0)
        zrs_drain(tag, zsend, sub)

    def zrs_start(tag, zsend, zrecv, relay, sub):
        def body(i, carry):
            zrs_send(tag, turn(i), zsend, zrecv, relay, sub)
            return carry

        lax.fori_loop(0, 4, body, 0)

    def zrs_relay(tag, mine, zsend, zrecv, relay, sub):
        @pl.when(inner)
        def _():
            got(relay.at[sub], zr2.at[tag, 1])
            zsend[(far_end, *sub)] = (mine[(far_end, *sub)] + relay[sub].astype(F32)).astype(BF)
            rc(
                zsend.at[(far_end, *sub)], zrecv.at[(z, *sub)], zs2.at[tag], zr2.at[tag, 0], plane(far_end)
            ).start()

    def zrs_end(tag, mine, zrecv, res, sub):
        @pl.when(outer)
        def _():
            got(zrecv.at[(pl.ds(0, 2), *sub)], zr2.at[tag, 0])
            res[sub] = mine[(z, *sub)] + zrecv[(pair, *sub)].astype(F32) + zrecv[(across, *sub)].astype(F32)

        @pl.when(inner)
        def _():
            got(zrecv.at[(pl.ds(0, 3), *sub)], zr2.at[tag, 0])
            res[sub] = (
                mine[(z, *sub)] + zrecv[(pair, *sub)].astype(F32) + zrecv[(across, *sub)].astype(F32)
                + zrecv[(far_end, *sub)].astype(F32)
            )

    every = (pl.ds(0, 128),)
    back = [(pl.ds(0, 128), pl.ds(*part)) for part in GPARTS]

    def back_sum(k):
        core_sum(R_GB + k, mB, crB, zsB, zrB, rlB, back[k], k < 2)

    def back_relay(k):
        zrs_relay(R_GB + k, mB, zsB, zrB, rlB, back[k])

    for k in range(2):
        got(g_size(k), pr.at[T_G + k])
        wgrad_back(k)
        if k == 1:
            back_relay(0)
            pl.when(c == 1)(act_first)
        back_sum(k)
    pl.when(c == 0)(act_first)
    got(g_size(2), pr.at[T_G + 2])
    bwd_act(0)
    bwd_in(0)
    back_relay(1)
    bwd_act(1)
    wgrad(R_GI, N, GPB, mI, csI, crI, 1024)
    bwd_in(1)
    core_sum(R_GI, mI, crI, zsI, zrI, rlI, every)
    wgrad_back(2)

    def norm_one_bwd(h):
        def body(q, carry):
            rr = rows(2 * h + q, 32)
            part = rows(q, 32)
            gn = OWN[rr, :] + RB2[h, 0, part, :].astype(F32) + RB2[h, 1, part, :].astype(F32)
            gn = GS[rr, :] + (gn + RB2[h, 2, part, :].astype(F32))
            xh = XH1[rr, :]
            GV[4:5, :] += jnp.sum(gn * xh, axis=0, keepdims=True)
            GV[5:6, :] += jnp.sum(gn, axis=0, keepdims=True)
            u = gn * VEC[4:5, :]
            gf = RS1[rr, 0:1] * (
                u - jnp.mean(u, axis=-1, keepdims=True) - xh * jnp.mean(u * xh, axis=-1, keepdims=True)
            )
            GV[3:4, :] += jnp.sum(gf, axis=0, keepdims=True)
            GF[rr, :] = gf
            GFB[rr, :] = gf.astype(BF)
            return carry

        lax.fori_loop(0, 2, body, 0)

    got(size(192), pr.at[T_RSB])
    norm_one_bwd(0)
    back_sum(2)
    got(size(192), pr.at[T_RSB2])
    norm_one_bwd(1)

    def gctx(t):
        GCS[t] = dot_nt(GFB[...], WO[t].reshape(256, 1024)).astype(BF)

    me = rows(s, 128)
    for j in (1, 2, 3):
        gctx(rank[j])
        rc(GCS.at[rank[j]], GC.at[me], ps.at[T_GC], pr.at[T_GC], peer(j)).start()
    drains.append(lambda: sent(CTX.at[pl.ds(0, 384)], ps.at[T_GC]))
    gctx(s)
    GC[me, :] = GCS[s]
    GFC[me, :] = GFB[:, rows(s, 256)]
    zrs_relay(R_GI, mI, zsI, zrI, rlI, every)
    got(CTX.at[pl.ds(0, 384)], pr.at[T_GC])

    BQ[...] = jnp.zeros_like(BQ)

    def attend_bwd(n, carry):
        rr = rows(n, 256)
        for two in range(2):
            parts = []
            for i in (2 * two, 2 * two + 1):
                q = MIX[rr, 192 * i : 192 * i + 64]
                k = MIX[rr, 192 * i + 64 : 192 * i + 128]
                v = MIX[rr, 192 * i + 128 : 192 * i + 192]
                gc = GC[rr, 64 * i : 64 * i + 64]
                p = PROB[n, i]
                gp = dot_nt(gc, v)
                inside = jnp.sum(p * gp, axis=-1, keepdims=True)
                gsc = (p * (gp - inside) * factor).astype(BF)
                parts += [dot_nn(gsc, k), dot_tn(gsc, q), dot_tn(p.astype(BF), gc)]
            both = jnp.concatenate([x.astype(BF) for x in parts], axis=1)
            GM[rr, 384 * two : 384 * two + 384] = both
            BQ[0:1, 384 * two : 384 * two + 384] += jnp.sum(both.astype(F32), axis=0, keepdims=True)
        return carry

    lax.fori_loop(0, 1, attend_bwd, 0)
    spread(T_GF, [(j, GFB.at[:, rows(rank[j], 256)], GFC.at[me]) for j in (1, 2, 3)], CTX.at[pl.ds(0, 384)])
    spread_ctx(T_CB, lambda j: [rank[i] for i in (1, 2, 3) if i != j])
    lax.fori_loop(1, 2, attend_bwd, 0)
    for k in range(6):
        GV[k % 3 : k % 3 + 1, rows(2 * s + k // 3, 128)] = BQ[0:1, 128 * k : 128 * k + 128]
    for gg in range(8):
        GVC[gg % 2, gg // 2] = GV[:, 128 * gg : 128 * gg + 128]
    send(GVC.at[1 - c], RVC, cs2.at[R_SV], cr2.at[R_SV, 0], partner)
    wgrad(R_GQ, X, GM, mQ, csQ, crQ, 768)
    got(RVC, cr2.at[R_SV, 0])
    TVZ[...] = GVC[c] + RVC[...]
    for k in (1, 2, 3):
        t = (z + k) % 4
        rc(TVZ.at[t], RVZ.at[k - 1], zs2.at[R_SV], zr2.at[R_SV, 0], plane(t)).start()
    drains.append(lambda: sent(RVZ, zs2.at[R_SV]))
    core_sum(R_GQ, mQ, crQ, zsQ, zrQ, rlQ, every)
    def gtok(rr, j):
        def body(t, carry):
            cols = rows(t, 256)
            part = dot_nt(GM[rr, :], WQ[cols, :])
            if j == 0:
                OWN[:, cols] = part
            else:
                SB3[j - 1, :, cols] = part.astype(BF)
            return carry

        lax.fori_loop(0, 4, body, 0)

    for j in (1, 2, 3):
        gtok(rows(rank[j], 128), j)
        rc(SB3.at[j - 1], RB3.at[j - 1], ps.at[T_GT], pr.at[T_GT], peer(j)).start()
    drains.append(lambda: sent(size(384), ps.at[T_GT]))
    zrs_relay(R_GQ, mQ, zsQ, zrQ, rlQ, every)
    gtok(me, 0)
    got(CTX.at[pl.ds(0, 384)], pr.at[T_GF])
    got(size(96), pr.at[T_CA])
    got(size(192), pr.at[T_CB])
    wgrad(R_GO, CALL, GFC, mO, csO, crO, 256)
    core_sum(R_GO, mO, crO, zsO, zrO, rlO, every)
    def last_part():
        zrs_start(R_GB3, zsB, zrB, rlB, back[2])

    pl.when(outer)(last_part)
    for k in range(2):
        zrs_end(R_GB + k, mB, zrB, GBF, back[k])
    put(GBF.at[:, pl.ds(0, 768)], gb_o.at[:, pl.ds(0, 768)], 1)
    zrs_end(R_GI, mI, zrI, resI, every)
    for j in (1, 2, 3):
        siI[j - 1] = resI[rows(rank[j], 32), :].astype(BF)
    spread(T_GI, [(j, siI.at[j - 1], riI.at[j - 1]) for j in (1, 2, 3)], riI)
    for i in range(8):
        GIF[:, rows(4 * i + s, 128)] = resI[rows(s, 32), 128 * i : 128 * i + 128]
    got(RVZ, zr2.at[R_SV, 0])
    PV[...] = TVZ[z] + RVZ[0] + RVZ[1] + RVZ[2]
    spread(T_SV, [(j, PV, RVP.at[j - 1]) for j in (1, 2, 3)], RVP)
    zrs_relay(R_GO, mO, zsO, zrO, rlO, every)
    pl.when(inner)(last_part)
    got(size(384), pr.at[T_GT])

    def gtok_sum(t, carry):
        rr = rows(t, 32)
        h = OWN[rr, :] + RB3[0, rr, :].astype(F32) + RB3[1, rr, :].astype(F32) + RB3[2, rr, :].astype(F32)
        GTS[rr, :] = GF[rr, :] + h
        return carry

    lax.fori_loop(0, 4, gtok_sum, 0)
    put(GTS, gtok_o, 2)
    zrs_end(R_GQ, mQ, zrQ, resQ, every)
    for j in (1, 2, 3):
        siQ[j - 1] = resQ[rows(rank[j], 32), :].astype(BF)
    spread(T_GQ, [(j, siQ.at[j - 1], riQ.at[j - 1]) for j in (1, 2, 3)], riQ)
    back_relay(2)
    got(riI, pr.at[T_GI])
    for j in (1, 2, 3):
        for i in range(8):
            GIF[:, rows(4 * i + rank[j], 128)] = riI[j - 1, :, 128 * i : 128 * i + 128].astype(F32)
    put(GIF, gi_o, 3)
    zrs_end(R_GO, mO, zrO, resO, every)
    for j in (1, 2, 3):
        siO[j - 1] = resO[rows(rank[j], 32), :].astype(BF)
    spread(T_GO, [(j, siO.at[j - 1], riO.at[j - 1]) for j in (1, 2, 3)], riO)
    zrs_end(R_GB3, mB, zrB, GBF, back[2])
    put(GBF.at[:, pl.ds(768, 256)], gb_o.at[:, pl.ds(768, 256)], 7)
    got(RVP, pr.at[T_SV])
    tot = PV[...] + RVP[0] + RVP[1] + RVP[2]
    row = lax.broadcasted_iota(jnp.int32, (16, 128), 0)
    RVC[0] = jnp.where(row == 9, PV[...], tot)
    put(RVC.at[0], sv_o, 6)
    GQF[:, rows(s, 768)] = resQ[rows(s, 32), :]
    got(riQ, pr.at[T_GQ])
    for j in (1, 2, 3):
        GQF[:, rows(rank[j], 768)] = riQ[j - 1].astype(F32)
    put(GQF, gq_o, 5)
    GOF[:, rows(s, 256)] = resO[rows(s, 32), :]
    got(riO, pr.at[T_GO])
    for j in (1, 2, 3):
        GOF[:, rows(rank[j], 256)] = riO[j - 1].astype(F32)
    put(GOF, go_o, 4)
    for drain in drains:
        drain()


def hand_over(*refs):
    sources, targets, kept, (isem, osem) = refs[:7], refs[7:21], refs[21:36], refs[36:]
    s = lax.axis_index("seq")
    ins = [pltpu.make_async_copy(src, mid, isem.at[k]) for k, (src, mid) in enumerate(zip(sources, kept))]
    held = kept[:6] + kept[7:]
    outs = [pltpu.make_async_copy(mid, dst, osem.at[k]) for k, (mid, dst) in enumerate(zip(held, targets))]
    for k in (6, 0, 1, 2, 3, 4, 5):
        ins[k].start()
    qv, ob, g1, b1, ib, bb, g2, b2 = kept[7:]
    sums = kept[6]
    ins[6].wait()
    turned = pltpu.roll(sums[...], (128 - 32 * s) % 128, 1)
    for k, ref in ((3, ob), (4, g1), (5, b1), (6, bb), (7, g2), (8, b2)):
        ref[...] = turned[k : k + 1, 0:32]
    ib[...] = sums[9:10, :]
    line = jnp.where(s == 0, sums[0:1, :], jnp.where(s == 3, sums[2:3, :], sums[1:2, :]))
    qv[...] = jnp.where(s // 2 == 0, line[:, 0:64], line[:, 64:128])
    for k in range(6, 14):
        outs[k].start()
    for k in range(6):
        ins[k].wait()
        outs[k].start()
    for out in outs:
        out.wait()


def fused_shards(
    tokens, cotangent, slot_lengths, w_qkv, qv_bias, w_out, out_bias, ln1_gain, ln1_bias,
    w_in, in_bias, w_back, back_bias, ln2_gain, ln2_bias,
):
    vm = pltpu.VMEM
    dma = pltpu.SemaphoreType.DMA

    def item(n):
        return [
            vm((4, 128, n), F32), vm((4, 128, n), BF), vm((4, 128, n), BF),
            vm((4, 128, n), BF), vm((4, 128, n), BF), vm((128, n), BF),
        ]

    lengths = (64, 32, 32, 32, 128, 32, 32, 32)
    scratch = [vm((1, n), BF) for n in lengths]
    scratch += [
        vm((16, 128), BF), vm((16, 128), F32), vm((128, 1024), BF), vm((512, 1024), BF), vm((1024, 768), BF), vm((1024, 1024), BF), vm((1024, 1024), BF),
        vm((4, 2, 4, 32, 1024), BF), vm((4, 2, 4, 16, 128), BF), vm((16, 1024), F32), vm((16, 1024), F32),
        vm((8, 768), F32),
        vm((512, 768), BF), vm((2, 4, 256, 256), F32), vm((512, 256), BF), vm((512, 1024), BF),
        vm((128, 1024), F32), vm((128, 1024), F32), vm((128, 128), F32), vm((512, 1024), BF),
        vm((512, 1024), F32), vm((512, 1024), BF), vm((512, 1024), BF), vm((2, 3, 64, 1024), BF),
        vm((128, 1024), F32),
        vm((512, 1024), BF), vm((128, 1024), F32), vm((512, 1024), BF), vm((512, 1024), BF),
        vm((2, 3, 64, 1024), BF), vm((128, 1024), F32), vm((128, 1024), BF), vm((512, 256), BF), vm((4, 128, 256), BF),
        vm((512, 256), BF), vm((512, 768), BF), vm((3, 128, 1024), BF), vm((3, 128, 1024), BF),
        vm((256, 1024), F32),
    ]
    scratch += item(1024) + item(1024) + item(768) + item(256)
    scratch += [
        vm((3, 32, 1024), BF), vm((3, 32, 1024), BF), vm((3, 32, 768), BF), vm((3, 32, 768), BF),
        vm((3, 32, 256), BF), vm((3, 32, 256), BF),
        vm((128, 1024), F32), vm((128, 768), F32), vm((128, 256), F32),
        vm((16, 1024), F32), vm((2, 4, 16, 128), F32), vm((4, 16, 128), F32), vm((4, 16, 128), F32),
        vm((3, 16, 128), F32), vm((16, 128), F32), vm((3, 16, 128), F32),
        vm((128, 1024), BF), vm((128, 1024), F32), vm((32, 3072), F32), vm((32, 1024), F32),
        vm((32, 4096), F32), vm((128, 1024), F32),
        dma((8,)), dma((26,)), dma((26,)), dma((8,)), dma((8, 2)), dma((8,)), dma((8,)),
        dma((7,)), dma((7, 4)), dma((7,)), dma((7, 2)),
    ]
    shapes = [
        ((128, 1024), BF), ((128, 1024), F32), ((32, 3072), F32), ((32, 1024), F32),
        ((32, 4096), F32), ((128, 1024), F32), ((16, 128), F32),
    ]
    hbm = pl.BlockSpec(memory_space=pl.ANY)
    smem = pl.BlockSpec(memory_space=pltpu.SMEM)
    small = [v.reshape(1, -1) for v in (qv_bias, out_bias, ln1_gain, ln1_bias, in_bias, back_bias, ln2_gain, ln2_bias)]
    results = pl.pallas_call(
        layer_kernel,
        out_shape=[jax.ShapeDtypeStruct(a, b) for a, b in shapes],
        in_specs=[hbm] * 6 + [smem] + [hbm] * 8,
        out_specs=[hbm] * 7,
        scratch_shapes=scratch,
        compiler_params=pltpu.CompilerParams(
            collective_id=0, has_side_effects=True, vmem_limit_bytes=67_000_000
        ),
        name="encoder_layer",
    )(tokens, cotangent, w_qkv, w_out, w_in, w_back, slot_lengths, *small)
    final = pl.pallas_call(
        hand_over,
        out_shape=[jax.ShapeDtypeStruct(a, b) for a, b in shapes[:6]]
        + [jax.ShapeDtypeStruct((1, n), F32) for n in lengths],
        in_specs=[hbm] * 7,
        out_specs=[hbm] * 14,
        scratch_shapes=[vm(a, b) for a, b in shapes] + [vm((1, n), F32) for n in lengths] + [dma((7,)), dma((14,))],
        name="hand_over",
    )(*results)
    output, grad_tokens, grad_qkv, grad_wo, grad_wi, grad_wb = final[:6]
    qv, ob, g1, b1, ib, bb, g2, b2 = [v.reshape(-1) for v in final[6:]]
    return (output, grad_tokens, grad_qkv, qv, grad_wo, ob, g1, b1, grad_wi, ib, grad_wb, bb, g2, b2)


def solution(mesh):
    placed = (
        P(("grp", "seq"), None),
        P(("grp", "seq"), None),
        P("grp"),
        P(("grp", "seq"), None),
        P(("grp", "seq")),
        P(("grp", "seq"), None),
        P(("grp", "seq")),
        P(("grp", "seq")),
        P(("grp", "seq")),
        P(("grp", "seq"), None),
        P(("grp", "seq")),
        P(("grp", "seq"), None),
        P(("grp", "seq")),
        P(("grp", "seq")),
        P(("grp", "seq")),
    )
    fused = mesh.shape["grp"] == 2 * PLANES and mesh.shape["seq"] == RANKS
    return jax.shard_map(
        fused_shards if fused else shards,
        mesh=mesh,
        in_specs=placed,
        out_specs=(
            P(("grp", "seq"), None),
            P(("grp", "seq"), None),
            P(("grp", "seq"), None),
            P(("grp", "seq")),
            P(("grp", "seq"), None),
            P(("grp", "seq")),
            P(("grp", "seq")),
            P(("grp", "seq")),
            P(("grp", "seq"), None),
            P(("grp", "seq")),
            P(("grp", "seq"), None),
            P(("grp", "seq")),
            P(("grp", "seq")),
            P(("grp", "seq")),
        ),
        check_vma=False,
    )
```

```python
from functools import partial
import math

import jax
import jax.numpy as jnp
from jax import lax
from jax.experimental import pallas as pl
from jax.experimental.pallas import tpu as pltpu
from jax.sharding import PartitionSpec as P

D = 1024
H = 16
HD = 64
SLOT_DEV = 64
SLOTS = 2


NORM_EPS = 1e-06


def layer_norm(hidden, gain, shift):
    center = hidden - jnp.mean(hidden, axis=-1, keepdims=True)
    spread = jnp.mean(center * center, axis=-1, keepdims=True)
    return center * lax.rsqrt(spread + NORM_EPS) * gain + shift


def exact_gelu(values):
    return jax.nn.gelu(values, approximate=False)


def full_bias(pair_bias):
    pairs = pair_bias.reshape(H, 2, HD)
    return jnp.stack([pairs[:, 0], jnp.zeros_like(pairs[:, 0]), pairs[:, 1]], axis=1).reshape(3 * D)


def contract_rows(left, right):
    return lax.dot_general(
        left, right, (((0,), (0,)), ((), ())), preferred_element_type=jnp.float32
    )


def contract_cols(left, right):
    return lax.dot_general(
        left, right, (((1,), (1,)), ((), ())), preferred_element_type=jnp.float32
    )


def slot_scores(mixed, length, factor):
    slot_width = mixed.shape[0]
    queries = mixed[:, :, 0]
    key_rows = mixed[:, :, 1]
    value_rows = mixed[:, :, 2]
    products = jnp.einsum("qhd,khd->hqk", queries, key_rows, preferred_element_type=jnp.float32)
    key_valid = (jnp.arange(slot_width) < length)[None, None, :]
    scores = jnp.where(key_valid, products * factor, -1e30)
    return (queries, key_rows, value_rows, scores)


def slot_forward(item, factor):
    mixed, length = item
    queries, key_rows, value_rows, scores = slot_scores(mixed, length, factor)
    row_max = jnp.max(scores, axis=-1, keepdims=True)
    expon = jnp.exp(scores - row_max)
    total = jnp.sum(expon, axis=-1, keepdims=True)
    probs = expon / total
    context = jnp.einsum(
        "hqk,khd->qhd", probs.astype(jnp.bfloat16), value_rows, preferred_element_type=jnp.float32
    )
    return (context.astype(jnp.bfloat16), row_max + jnp.log(total))


def slot_backward(item, factor):
    mixed, grad_context, log_total, length = item
    queries, key_rows, value_rows, scores = slot_scores(mixed, length, factor)
    probs = jnp.exp(scores - log_total)
    grad_probs = jnp.einsum(
        "qhd,khd->hqk", grad_context, value_rows, preferred_element_type=jnp.float32
    )
    inner = jnp.sum(probs * grad_probs, axis=-1, keepdims=True)
    grad_scores = (probs * (grad_probs - inner) * factor).astype(jnp.bfloat16)
    grad_queries = jnp.einsum(
        "hqk,khd->qhd", grad_scores, key_rows, preferred_element_type=jnp.float32
    )
    grad_keys = jnp.einsum("hqk,qhd->khd", grad_scores, queries, preferred_element_type=jnp.float32)
    grad_values = jnp.einsum(
        "hqk,qhd->khd", probs.astype(jnp.bfloat16), grad_context, preferred_element_type=jnp.float32
    )
    return jnp.stack([grad_queries, grad_keys, grad_values], axis=2).astype(jnp.bfloat16)


def shards(
    tokens,
    cotangent,
    slot_lengths,
    w_qkv,
    qv_bias,
    w_out,
    out_bias,
    ln1_gain,
    ln1_bias,
    w_in,
    in_bias,
    w_back,
    back_bias,
    ln2_gain,
    ln2_bias,
):
    seq_count = lax.axis_size("seq")
    local_rows = tokens.shape[0]
    slot_width = SLOT_DEV * seq_count
    heads_here = H // seq_count
    factor = 1.0 / math.sqrt(HD)
    full_qkv, full_qv, full_out, full_obias, gain_one, shift_one = (
        lax.all_gather(w_qkv, ("grp", "seq"), axis=0, tiled=True),
        lax.all_gather(qv_bias, ("grp", "seq"), axis=0, tiled=True),
        lax.all_gather(w_out, ("grp", "seq"), axis=0, tiled=True),
        lax.all_gather(out_bias, ("grp", "seq"), axis=0, tiled=True),
        lax.all_gather(ln1_gain, ("grp", "seq"), axis=0, tiled=True),
        lax.all_gather(ln1_bias, ("grp", "seq"), axis=0, tiled=True),
    )
    full_in, full_ibias, full_back, full_bbias, gain_two, shift_two = (
        lax.all_gather(w_in, ("grp", "seq"), axis=0, tiled=True),
        lax.all_gather(in_bias, ("grp", "seq"), axis=0, tiled=True),
        lax.all_gather(w_back, ("grp", "seq"), axis=0, tiled=True),
        lax.all_gather(back_bias, ("grp", "seq"), axis=0, tiled=True),
        lax.all_gather(ln2_gain, ("grp", "seq"), axis=0, tiled=True),
        lax.all_gather(ln2_bias, ("grp", "seq"), axis=0, tiled=True),
    )
    mixed = (
        jnp.dot(tokens, full_qkv, preferred_element_type=jnp.float32) + full_bias(full_qv)
    ).astype(jnp.bfloat16)
    gathered = lax.all_to_all(mixed, "seq", split_axis=1, concat_axis=0, tiled=True)
    per_slot = gathered.reshape(SLOTS, slot_width, heads_here, 3, HD)
    contexts, log_totals = lax.map(partial(slot_forward, factor=factor), (per_slot, slot_lengths))
    context_heads = contexts.reshape(SLOTS * slot_width, heads_here * HD)
    context = lax.all_to_all(context_heads, "seq", split_axis=0, concat_axis=1, tiled=True)
    attended = jnp.dot(context, full_out, preferred_element_type=jnp.float32) + full_obias
    first_in = tokens.astype(jnp.float32) + attended
    normed, norm_one_pull = jax.vjp(layer_norm, first_in, gain_one, shift_one)
    normed_low = normed.astype(jnp.bfloat16)
    pre_act = jnp.dot(normed_low, full_in, preferred_element_type=jnp.float32) + full_ibias
    activated, gelu_pull = jax.vjp(exact_gelu, pre_act)
    act_low = activated.astype(jnp.bfloat16)
    ffn_out = jnp.dot(act_low, full_back, preferred_element_type=jnp.float32) + full_bbias
    output, norm_two_pull = jax.vjp(layer_norm, normed + ffn_out, gain_two, shift_two)
    row_index = lax.axis_index("seq") * local_rows + jnp.arange(local_rows)
    slot_index = row_index // slot_width
    place = row_index % slot_width
    row_length = jnp.sum(
        jnp.where(slot_index[:, None] == jnp.arange(SLOTS)[None, :], slot_lengths[None, :], 0),
        axis=1,
    )
    row_valid = (place < row_length).astype(jnp.float32)
    seed_grad = cotangent.astype(jnp.float32) * row_valid[:, None]
    grad_second, grad_gain_two, grad_shift_two = norm_two_pull(seed_grad)
    grad_ffn_low = grad_second.astype(jnp.bfloat16)
    grad_back_w = contract_rows(act_low, grad_ffn_low)
    grad_back_b = jnp.sum(grad_second, axis=0)
    (grad_pre,) = gelu_pull(contract_cols(grad_ffn_low, full_back))
    grad_pre_low = grad_pre.astype(jnp.bfloat16)
    grad_in_w = contract_rows(normed_low, grad_pre_low)
    grad_in_b = jnp.sum(grad_pre, axis=0)
    grad_normed = grad_second + contract_cols(grad_pre_low, full_in)
    grad_first, grad_gain_one, grad_shift_one = norm_one_pull(grad_normed)
    grad_attn_low = grad_first.astype(jnp.bfloat16)
    grad_out_w = contract_rows(context, grad_attn_low)
    grad_out_b = jnp.sum(grad_first, axis=0)
    grad_context = contract_cols(grad_attn_low, full_out).astype(jnp.bfloat16)
    grad_heads = lax.all_to_all(grad_context, "seq", split_axis=1, concat_axis=0, tiled=True)
    grad_slots = grad_heads.reshape(SLOTS, slot_width, heads_here, HD)
    grad_mixed_heads = lax.map(
        partial(slot_backward, factor=factor), (per_slot, grad_slots, log_totals, slot_lengths)
    )
    grad_mixed = lax.all_to_all(
        grad_mixed_heads.reshape(SLOTS * slot_width, heads_here * 3 * HD),
        "seq",
        split_axis=0,
        concat_axis=1,
        tiled=True,
    )
    grad_qkv_w = contract_rows(tokens, grad_mixed)
    summed_bias = jnp.sum(grad_mixed.astype(jnp.float32), axis=0).reshape(H, 3, HD)
    grad_qv = jnp.stack([summed_bias[:, 0], summed_bias[:, 2]], axis=1).reshape(2 * D)
    input_grad = grad_first + contract_cols(grad_mixed, full_qkv)
    sums = (
        lax.psum_scatter(grad_qkv_w, ("grp", "seq"), scatter_dimension=0, tiled=True),
        lax.psum_scatter(grad_qv, ("grp", "seq"), scatter_dimension=0, tiled=True),
        lax.psum_scatter(grad_out_w, ("grp", "seq"), scatter_dimension=0, tiled=True),
        lax.psum_scatter(grad_out_b, ("grp", "seq"), scatter_dimension=0, tiled=True),
        lax.psum_scatter(
            grad_gain_one.astype(jnp.float32), ("grp", "seq"), scatter_dimension=0, tiled=True
        ),
        lax.psum_scatter(
            grad_shift_one.astype(jnp.float32), ("grp", "seq"), scatter_dimension=0, tiled=True
        ),
        lax.psum_scatter(grad_in_w, ("grp", "seq"), scatter_dimension=0, tiled=True),
        lax.psum_scatter(grad_in_b, ("grp", "seq"), scatter_dimension=0, tiled=True),
        lax.psum_scatter(grad_back_w, ("grp", "seq"), scatter_dimension=0, tiled=True),
        lax.psum_scatter(grad_back_b, ("grp", "seq"), scatter_dimension=0, tiled=True),
        lax.psum_scatter(
            grad_gain_two.astype(jnp.float32), ("grp", "seq"), scatter_dimension=0, tiled=True
        ),
        lax.psum_scatter(
            grad_shift_two.astype(jnp.float32), ("grp", "seq"), scatter_dimension=0, tiled=True
        ),
    )
    return (
        output.astype(jnp.bfloat16),
        input_grad,
        sums[0],
        sums[1],
        sums[2],
        sums[3],
        sums[4],
        sums[5],
        sums[6],
        sums[7],
        sums[8],
        sums[9],
        sums[10],
        sums[11],
    )


BF = jnp.bfloat16
F32 = jnp.float32
MESH = pl.DeviceIdType.MESH
PLANES = 4
RANKS = 4
(
    T_PACK, T_WQ, T_WI, T_TOK, T_WO, T_CTX, T_CA, T_CB, T_N, T_N2, T_RSF, T_RSF2, T_RSF3, T_RSF4,
    T_G, T_G2, T_G3, T_RSB, T_RSB2, T_GC, T_GF, T_GO, T_GT, T_GI, T_GQ, T_SV,
) = range(26)
(A_PACK, A_WO, A_WQ, A_WI, A_WB, A_WB2, A_WB3, A_WB4) = range(8)
(R_GB, R_GB2, R_GB3, R_GI, R_GO, R_GQ, R_SV) = range(7)
PARTS = ((0, 256), (256, 256), (512, 256), (768, 256))
GPARTS = ((0, 384), (384, 384), (768, 256))


def dot_nn(a, b):
    return jnp.dot(a, b, preferred_element_type=F32)


def dot_nt(a, b):
    return lax.dot_general(a, b, (((1,), (1,)), ((), ())), preferred_element_type=F32)


def dot_tn(a, b):
    return lax.dot_general(a, b, (((0,), (0,)), ((), ())), preferred_element_type=F32)


def layer_kernel(
    x_in, cot_in, wq_in, wo_in, wi_in, wb_in, lens, *refs
):
    (
        small_in, (out_o, gtok_o, gq_o, go_o, gi_o, gb_o, sv_o), small,
        (
            pack, packf, cot, X, WQ, WI, WB, WO, PK, VEC, IB, BQ,
            MIX, PROB, CTX, CALL, XH1, NF, RS1, N, DG, ACT, SB, RB, OWN,
            G, GS, GPB, SB2, RB2, GF, GFB, GFC, GCS, GC, GM, SB3, RB3,
            ACC,
            mB, csB, crB, zsB, zrB, rlB,
            mI, csI, crI, zsI, zrI, rlI,
            mQ, csQ, crQ, zsQ, zrQ, rlQ,
            mO, csO, crO, zsO, zrO, rlO,
            siI, riI, siQ, riQ, siO, riO, resI, resQ, resO,
            GV, GVC, RVC, TVZ, RVZ, PV, RVP,
            OUT, GTS, GQF, GOF, GIF, GBF,
            osem, ps, pr, zs, zr, cs, cr, cs2, cr2, zs2, zr2,
        ),
    ) = refs[:8], refs[8:15], refs[15:23], refs[23:]
    g = lax.axis_index("grp")
    s = lax.axis_index("seq")
    z = g // 2
    c = g % 2
    rank = {1: s + 1 - 2 * (s % 2), 2: (s + 2) % 4, 3: 3 - s}
    partner = (g + 1 - 2 * c, s)
    inner = jnp.logical_and(z >= 1, z <= 2)
    outer = jnp.logical_or(z == 0, z == 3)
    two_off, inward, outward = (z + 2) % 4, 1 + z % 2, 3 * (z // 2)
    pair, across, far_end = z + 1 - 2 * (z % 2), 2 - z // 2, 3 * (1 - z // 2)
    is_outer = (z // 2 + z % 2 + 1) % 2
    drains = []

    def peer(j):
        return (g, rank[j])

    def plane(t):
        return (2 * t + c, s)

    def rc(src, dst, ss, rs, dev):
        return pltpu.make_async_remote_copy(
            src_ref=src, dst_ref=dst, send_sem=ss, recv_sem=rs, device_id=dev, device_id_type=MESH
        )

    def got(dst, rs):
        rc(dst, dst, osem.at[0], rs, partner).wait_recv()

    def sent(src, ss):
        rc(src, src, ss, pr.at[0], partner).wait_send()

    def send(src, dst, ss, rs, dev):
        rc(src, dst, ss, rs, dev).start()
        drains.append(lambda: sent(src, ss))

    def spread(tag, pieces, total):
        for j, src, dst in pieces:
            rc(src, dst, ps.at[tag], pr.at[tag], peer(j)).start()
        drains.append(lambda: sent(total, ps.at[tag]))

    def put(src, dst, k):
        pltpu.make_async_copy(src, dst, osem.at[k]).start()
        drains.append(lambda: pltpu.make_async_copy(src, dst, osem.at[k]).wait())

    def rows(i, n):
        return pl.ds(pl.multiple_of(i * n, n), n)

    def size(n):
        return X.at[pl.ds(0, n)]

    bar = pltpu.get_barrier_semaphore()
    for j in (1, 2, 3):
        pl.semaphore_signal(bar, inc=1, device_id=peer(j), device_id_type=MESH)
    for k in (1, 2, 3):
        pl.semaphore_signal(bar, inc=1, device_id=plane((z + k) % 4), device_id_type=MESH)
    pl.semaphore_signal(bar, inc=1, device_id=partner, device_id_type=MESH)
    small_cp = [pltpu.make_async_copy(small_in[k], small[k], ps.at[8 + k]) for k in range(8)]
    for cp in small_cp:
        cp.start()
    wo_cp = pltpu.make_async_copy(wo_in, WO.at[z, c, s], osem.at[2])
    local = [
        pltpu.make_async_copy(wq_in.at[:, rows(s, 768)], WQ.at[rows(4 * g + s, 32)], osem.at[1]),
        pltpu.make_async_copy(x_in, X.at[rows(s, 128)], osem.at[0]),
        pltpu.make_async_copy(wb_in, WB.at[rows(g, 128)], osem.at[3]),
        pltpu.make_async_copy(cot_in, cot, osem.at[4]),
    ]
    for cp in [wo_cp] + local:
        cp.start()
    for i in range(8):
        pltpu.make_async_copy(
            wi_in.at[:, rows(4 * i + s, 128)], WI.at[rows(4 * g + s, 32), pl.ds(128 * i, 128)], osem.at[5]
        ).start()
    lane = lax.broadcasted_iota(jnp.int32, (1, 128), 1)
    for cp in small_cp:
        cp.wait()
    qv_in, ob_in, g1_in, b1_in, ib_in, bb_in, g2_in, b2_in = small
    packf[...] = jnp.zeros_like(packf)
    twice = jnp.concatenate([qv_in[...].astype(F32)] * 2, axis=1)
    for k in range(3):
        packf[k : k + 1, :] = jnp.where(lane // 64 + 4 * ((s + 1) // 2) == s // 2 + 4 * k, twice, 0.0)
    for k, ref in ((3, ob_in), (4, g1_in), (5, b1_in), (6, bb_in), (7, g2_in), (8, b2_in)):
        four = jnp.concatenate([ref[...].astype(F32)] * 4, axis=1)
        packf[k : k + 1, :] = jnp.where(lane // 32 == s, four, 0.0)
    packf[9:10, :] = ib_in[...].astype(F32)
    pack[...] = packf[...].astype(BF)
    PK[z, c, s] = pack[...]
    pl.semaphore_wait(bar, 7)

    def ck(ref):
        return lambda o, cc: ref.at[rows(2 * o + cc, 128)]

    chunk = {
        A_PACK: lambda o, cc: PK.at[o, cc],
        A_WO: lambda o, cc: WO.at[o, cc, s],
        A_WQ: ck(WQ),
        A_WI: ck(WI),
    }
    for k, part in enumerate(PARTS):
        chunk[A_WB + k] = lambda o, cc, part=part: WB.at[rows(2 * o + cc, 128), pl.ds(*part)]
    chunks = {
        A_PACK: lambda n: PK.at[pl.ds(0, n), 0],
        A_WO: lambda n: size(32 * n),
        A_WQ: lambda n: WQ.at[pl.ds(0, 128 * n)],
        A_WI: lambda n: size(128 * n),
    }
    for k, (_, wide) in enumerate(PARTS):
        chunks[A_WB + k] = lambda n, wide=wide: size(128 * n * wide // 1024)

    def zag_one(tag, o, t, far, ref=None):
        ref = chunk[tag](o, c) if ref is None else ref
        rc(ref, ref, zs.at[tag], zr.at[tag, far], plane(t)).start()

    def zag_start(tag, pieces=(None,)):
        for ref in pieces:
            zag_one(tag, z, two_off, is_outer, ref)
        for ref in pieces:
            zag_one(tag, z, inward, 0, ref)

        def drain():
            @pl.when(inner)
            def _():
                sent(chunks[tag](4), zs.at[tag])

            @pl.when(outer)
            def _():
                sent(chunks[tag](2), zs.at[tag])

        drains.append(drain)

    def zag_outward(tag):
        @pl.when(inner)
        def _():
            zag_one(tag, z, outward, 0)

    def zag_ffn(tag):
        zag_one(tag, z, two_off, is_outer)
        zag_one(tag, z, inward, 0)
        zag_outward(tag)

    def zag_own(tag):
        @pl.when(inner)
        def _():
            for t in (two_off, inward, outward):
                zag_one(tag, z, t, 0)

    def core_send(tag, o):
        ref = chunk[tag](o, c)
        rc(ref, ref, cs.at[tag], cr.at[tag], partner).start()

    def zag_relay(tag, core=True):
        @pl.when(inner)
        def _():
            got(chunk[tag](far_end, c), zr.at[tag, 1])
            zag_one(tag, far_end, outward, 1)
            if core:
                core_send(tag, far_end)

    def zag_near(tag, core=True):
        got(chunks[tag](2), zr.at[tag, 0])
        if core:
            core_send(tag, pair)
            core_send(tag, across)

    def zag_far(tag, core=True):
        @pl.when(outer)
        def _():
            got(chunk[tag](far_end, c), zr.at[tag, 1])
            if core:
                core_send(tag, far_end)

    def zag_core(tag):
        got(chunks[tag](4), cr.at[tag])
        drains.append(lambda: sent(chunks[tag](4), cs.at[tag]))

    spread(T_PACK, [(j, pack, PK.at[z, c, s]) for j in (1, 2, 3)], PK.at[0, 0, pl.ds(0, 3)])
    spread(
        T_WQ, [(j, wq_in.at[:, rows(rank[j], 768)], WQ.at[rows(4 * g + s, 32)]) for j in (1, 2, 3)],
        WQ.at[pl.ds(0, 96)],
    )
    wo_cp.wait()
    zag_start(A_WO)
    zag_outward(A_WO)
    local[0].wait()
    zag_one(A_WQ, z, two_off, is_outer, WQ.at[rows(4 * g + s, 32)])
    zag_one(A_WQ, z, inward, 0, WQ.at[rows(4 * g + s, 32)])
    spread(
        T_WI,
        [
            (
                j, wi_in.at[:, rows(4 * i + rank[j], 128)],
                WI.at[rows(4 * g + s, 32), pl.ds(128 * i, 128)],
            )
            for j in (1, 2, 3)
            for i in range(8)
        ],
        size(96),
    )
    spread(T_TOK, [(j, x_in, X.at[rows(s, 128)]) for j in (1, 2, 3)], size(384))
    for cp in local[1:]:
        cp.wait()
    got(PK.at[0, 0, pl.ds(0, 3)], pr.at[T_PACK])
    zag_start(A_PACK)
    zag_outward(A_PACK)
    core_send(A_PACK, z)
    got(WQ.at[pl.ds(0, 96)], pr.at[T_WQ])
    zag_start(A_WQ, [WQ.at[rows(4 * g + rank[j], 32)] for j in (1, 2, 3)])
    core_send(A_WQ, z)
    for tag in (A_WB, A_WB2, A_WB3, A_WB4):
        core_send(tag, z)

    def wo_plane(o):
        for j in (1, 2, 3):
            ref = WO.at[o, c, s]
            rc(ref, ref, ps.at[T_WO], pr.at[T_WO], peer(j)).start()

    zag_relay(A_WO, core=False)
    zag_relay(A_PACK)
    zag_outward(A_WQ)
    wo_plane(z)

    @pl.when(inner)
    def _():
        wo_plane(far_end)

    zag_near(A_WO, core=False)
    wo_plane(pair)
    wo_plane(across)
    zag_near(A_PACK)
    got(size(96), pr.at[T_WI])
    wi_own = WI.at[rows(4 * g + s, 32)]
    pltpu.make_async_copy(wi_own, wi_own, osem.at[5]).wait()
    core_send(A_WI, z)

    zag_relay(A_WQ)

    zag_outward(A_WI)
    def drain_ffn():
        for tag in (A_WI, A_WB, A_WB2, A_WB3, A_WB4):
            @pl.when(inner)
            def _():
                sent(chunks[tag](4), zs.at[tag])

            @pl.when(outer)
            def _():
                sent(chunks[tag](2), zs.at[tag])

    drains.append(drain_ffn)
    zag_far(A_PACK)
    zag_far(A_WO, core=False)

    @pl.when(outer)
    def _():
        wo_plane(far_end)

    drains.append(lambda: sent(size(384), ps.at[T_WO]))
    zag_near(A_WQ)

    @pl.when(outer)
    def _():
        for tag in (A_WI, A_WB, A_WB2, A_WB3, A_WB4):
            zag_one(tag, z, two_off, 1)
            zag_one(tag, z, inward, 0)


    @pl.when(inner)
    def _():
        zag_one(A_WI, z, two_off, 0)
        zag_one(A_WI, z, inward, 0)

    zag_own(A_WB)
    zag_core(A_PACK)
    for gg in range(8):
        tot = PK[gg // 2, gg % 2, 0].astype(F32)
        for r in (1, 2, 3):
            tot = tot + PK[gg // 2, gg % 2, r].astype(F32)
        VEC[:, gg * 128 : (gg + 1) * 128] = tot
        IB[:, gg * 128 : (gg + 1) * 128] = PK[gg // 2, gg % 2, s].astype(F32)
    for cc in range(2):
        tot = PK[s, cc, 0].astype(F32)
        for r in (1, 2, 3):
            tot = tot + PK[s, cc, r].astype(F32)
        for k in range(3):
            BQ[0:1, (3 * cc + k) * 128 : (3 * cc + k + 1) * 128] = tot[k : k + 1, :]
    zag_far(A_WQ)
    got(size(384), pr.at[T_TOK])
    zag_core(A_WQ)

    def qkv(t, carry):
        cols = rows(t, 256)
        MIX[:, cols] = (dot_nn(X[...], WQ[:, cols]) + BQ[0:1, cols]).astype(BF)
        return carry

    lax.fori_loop(0, 3, qkv, 0)

    factor = 1.0 / math.sqrt(HD)

    def attend(n, carry):
        rr = rows(n, 256)
        ok = lax.broadcasted_iota(jnp.int32, (1, 256), 1) < lens[n]
        outs = []
        for i in range(4):
            q = MIX[rr, 192 * i : 192 * i + 64]
            k = MIX[rr, 192 * i + 64 : 192 * i + 128]
            v = MIX[rr, 192 * i + 128 : 192 * i + 192]
            sc = jnp.where(ok, dot_nt(q, k) * factor, -1e30)
            e = jnp.exp(sc - jnp.max(sc, axis=-1, keepdims=True))
            p = e * (1.0 / jnp.sum(e, axis=-1, keepdims=True))
            PROB[n, i] = p
            outs.append(dot_nn(p.astype(BF), v).astype(BF))
        CTX[rr, 0:128] = jnp.concatenate(outs[:2], axis=1)
        CTX[rr, 128:256] = jnp.concatenate(outs[2:], axis=1)
        return carry

    lax.fori_loop(0, 1, attend, 0)
    zag_relay(A_WI)

    zag_own(A_WB2)
    lax.fori_loop(1, 2, attend, 0)
    spread(
        T_CTX, [(j, CTX.at[rows(rank[j], 128)], CALL.at[rows(rank[j], 128), rows(s, 256)]) for j in (1, 2, 3)],
        CTX.at[pl.ds(0, 384)],
    )
    CALL[:, rows(s, 256)] = CTX[...]
    got(size(384), pr.at[T_WO])
    send(WO.at[:, c], WO.at[:, c], cs.at[A_WO], cr.at[A_WO], partner)
    got(WO.at[:, 1 - c], cr.at[A_WO])
    got(CTX.at[pl.ds(0, 384)], pr.at[T_CTX])

    zag_relay(A_WB)
    zag_own(A_WB3)
    def proj(t, carry):
        cols = rows(t, 256)
        w = WO[:, :, :, :, cols].reshape(1024, 256)
        XH1[:, cols] = X[rows(s, 128), cols].astype(F32) + (dot_nn(CALL[rows(s, 128), :], w) + VEC[3:4, cols])
        return carry

    lax.fori_loop(0, 4, proj, 0)

    def own_rows(h, q):
        return pl.ds(pl.multiple_of(h * 256 + s * 64 + q * 32, 32), 32)

    def halves(h):
        return pl.ds(256 * h, 256)

    def mine_of(h):
        return pl.ds(pl.multiple_of(h * 256 + s * 64, 64), 64)

    def rank_of(h, j):
        return pl.ds(pl.multiple_of(h * 256 + rank[j] * 64, 64), 64)

    def norm_one(h):
        def body(q, carry):
            rr = rows(2 * h + q, 32)
            hid = XH1[rr, :]
            ctr = hid - jnp.mean(hid, axis=-1, keepdims=True)
            rstd = lax.rsqrt(jnp.mean(ctr * ctr, axis=-1, keepdims=True) + NORM_EPS)
            xh = ctr * rstd
            nf = xh * VEC[4:5, :] + VEC[5:6, :]
            XH1[rr, :] = xh
            RS1[rr, :] = jnp.broadcast_to(rstd, (32, 128))
            NF[rr, :] = nf
            N[own_rows(h, q), :] = nf.astype(BF)
            return carry

        lax.fori_loop(0, 2, body, 0)

    for h in (0, 1):
        norm_one(h)
        spread(T_N + h, [(j, N.at[mine_of(h)], N.at[mine_of(h)]) for j in (1, 2, 3)], size(192))

    def spread_ctx(tag, blocks):
        pieces = [
            (j, CTX.at[rows(i, 128)], CALL.at[rows(i, 128), rows(s, 256)]) for j in (1, 2, 3) for i in blocks(j)
        ]
        spread(tag, pieces, size(32 * len(pieces)))

    zag_near(A_WI)
    zag_relay(A_WB2)
    zag_own(A_WB4)
    zag_far(A_WI)
    zag_core(A_WI)
    zag_relay(A_WB3)

    def ffn_in(h):
        rr = halves(h)

        def body(t, carry):
            cols = rows(t, 256)
            pre = dot_nn(N[rr, :], WI[:, cols]) + IB[9:10, cols]
            cdf = 0.5 * (1.0 + lax.erf(pre * math.sqrt(0.5)))
            ACT[rr, cols] = (pre * cdf).astype(BF)
            DG[rr, cols] = cdf + pre * jnp.exp(-0.5 * (pre * pre)) * (1.0 / math.sqrt(2.0 * math.pi))
            return carry

        lax.fori_loop(0, 4, body, 0)

    def spread_cols(tag, piece, hs=(0, 1)):
        for h in hs:
            for j in (1, 2, 3):
                src, dst = piece(h, j)
                rc(src, dst, ps.at[tag], pr.at[tag], peer(j)).start()

    def ffn_out(k):
        start, wide = PARTS[k]
        part_cols = pl.ds(start, wide)
        for h in (0, 1):
            rr = halves(h)

            def body(t, carry):
                cols = rows(start // 256 + t, 256)
                part = dot_nn(ACT[rr, :], WB[:, cols])
                SB[rr, cols] = part.astype(BF)
                ACC[:, cols] = part
                return carry

            lax.fori_loop(0, wide // 256, body, 0)
            spread_cols(
                T_RSF + k, lambda h, j: (SB.at[rank_of(h, j), part_cols], RB.at[h, j - 1, :, part_cols]), (h,)
            )
            OWN[pl.ds(64 * h, 64), part_cols] = ACC[rows(s, 64), part_cols]
        drains.append(lambda: sent(size(384 * wide // 1024), ps.at[T_RSF + k]))

    for h in (0, 1):
        got(size(192), pr.at[T_N + h])
        ffn_in(h)
        if h == 0:
            zag_relay(A_WB4)
            zag_near(A_WB)
            zag_far(A_WB)
    for k in range(4):
        if k >= 1:
            zag_near(A_WB + k)
            zag_far(A_WB + k)
        zag_core(A_WB + k)
        ffn_out(k)
    GV[...] = jnp.zeros_like(GV)

    def norm_two(h):
        def body(q, carry):
            rr = rows(2 * h + q, 32)
            part = rows(q, 32)
            hid = OWN[rr, :] + RB[h, 0, part, :].astype(F32) + RB[h, 1, part, :].astype(F32)
            hid = NF[rr, :] + (hid + RB[h, 2, part, :].astype(F32) + VEC[6:7, :])
            ctr = hid - jnp.mean(hid, axis=-1, keepdims=True)
            rstd = lax.rsqrt(jnp.mean(ctr * ctr, axis=-1, keepdims=True) + NORM_EPS)
            xh = ctr * rstd
            OUT[rr, :] = (xh * VEC[7:8, :] + VEC[8:9, :]).astype(BF)
            place = (s % 2) * 128 + (2 * h + q) * 32 + lax.broadcasted_iota(jnp.int32, (32, 1), 0)
            seed = jnp.where(place < lens[s // 2], cot[rr, :].astype(F32), 0.0)
            GV[7:8, :] += jnp.sum(seed * xh, axis=0, keepdims=True)
            GV[8:9, :] += jnp.sum(seed, axis=0, keepdims=True)
            u = seed * VEC[7:8, :]
            gs = rstd * (u - jnp.mean(u, axis=-1, keepdims=True) - xh * jnp.mean(u * xh, axis=-1, keepdims=True))
            GV[6:7, :] += jnp.sum(gs, axis=0, keepdims=True)
            GS[rr, :] = gs
            G[own_rows(h, q), :] = gs.astype(BF)
            for j in (1, 2, 3):
                ref = G.at[own_rows(h, q), pl.ds(*GPARTS[0])]
                rc(ref, ref, ps.at[T_G], pr.at[T_G], peer(j)).start()
            return carry

        lax.fori_loop(0, 2, body, 0)

    def g_piece(k):
        part = pl.ds(*GPARTS[k])
        return lambda h, j: (G.at[mine_of(h), part], G.at[mine_of(h), part])

    def g_size(k):
        return size(384 * GPARTS[k][1] // 1024)

    for k in range(4):
        got(size(384 * PARTS[k][1] // 1024), pr.at[T_RSF + k])
    for h in (0, 1):
        norm_two(h)
    for k in (1, 2):
        spread_cols(T_G + k, g_piece(k))
    for k in range(3):
        drains.append(lambda k=k: sent(g_size(k), ps.at[T_G + k]))
    spread_ctx(T_CA, lambda j: [s])
    put(OUT, out_o, 0)

    def act_first():
        def body(t, carry):
            cols = rows(t, 256)
            mI[:, :, cols] = dot_nt(G[:, 0:768], WB[cols, 0:768]).reshape(4, 128, 256)
            return carry

        lax.fori_loop(0, 4, body, 0)

    def bwd_act(h):
        rr = halves(h)

        def body(t, carry):
            cols = rows(t, 256)
            gp = mI[2 * h : 2 * h + 2, :, cols].reshape(256, 256)
            gp = (gp + dot_nt(G[rr, 768:1024], WB[cols, 768:1024])) * DG[rr, cols]
            GV[9:10, cols] += jnp.sum(gp, axis=0, keepdims=True)
            GPB[rr, cols] = gp.astype(BF)
            return carry

        lax.fori_loop(0, 4, body, 0)

    def bwd_in(h):
        rr = halves(h)

        def body(t, carry):
            cols = rows(t, 256)
            part = dot_nt(GPB[rr, :], WI[cols, :])
            SB2[rr, cols] = part.astype(BF)
            ACC[:, cols] = part
            return carry

        lax.fori_loop(0, 4, body, 0)
        spread(T_RSB + h, [(j, SB2.at[rank_of(h, j)], RB2.at[h, j - 1]) for j in (1, 2, 3)], size(192))
        OWN[pl.ds(64 * h, 64), :] = ACC[rows(s, 64), :]

    def turn(i):
        return (3 - z + (4 - z) * i) % 5

    def core_start(tag, t, csend, crecv):
        rc(csend.at[t], crecv.at[t], cs2.at[tag], cr2.at[tag, t], partner).start()

    def wgrad(tag, lhs, rhs, mine, csend, crecv, cols):
        def body(i, carry):
            t = turn(i)
            ACC[:, 0:cols] = dot_tn(lhs[:, rows(t, 256)], rhs[...])
            csend[t] = ACC[rows(1 - c, 128), 0:cols].astype(BF)
            mine[t] = ACC[rows(c, 128), 0:cols]
            core_start(tag, t, csend, crecv)
            return carry

        lax.fori_loop(0, 4, body, 0)
        drains.append(lambda: sent(csend, cs2.at[tag]))

    def wgrad_back(k):
        tag, (start, wide) = R_GB + k, GPARTS[k]
        cols = pl.ds(start, wide)

        def body(i, carry):
            t = turn(i)
            ACC[:, 0:wide] = dot_tn(ACT[:, rows(t, 256)], G[:, cols])
            csB[t, :, cols] = ACC[rows(1 - c, 128), 0:wide].astype(BF)
            mB[t, :, cols] = ACC[rows(c, 128), 0:wide]
            rc(csB.at[t, :, cols], crB.at[t, :, cols], cs2.at[tag], cr2.at[tag, t], partner).start()
            return carry

        lax.fori_loop(0, 4, body, 0)
        drains.append(lambda: sent(csB.at[:, :, cols], cs2.at[tag]))

    def zrs_send(tag, t, zsend, zrecv, relay, sub):
        @pl.when(jnp.logical_or(t == pair, t == across))
        def _():
            rc(zsend.at[(t, *sub)], zrecv.at[(z, *sub)], zs2.at[tag], zr2.at[tag, 0], plane(t)).start()

        @pl.when(jnp.logical_and(outer, t == far_end))
        def _():
            rc(zsend.at[(t, *sub)], relay.at[sub], zs2.at[tag], zr2.at[tag, 1], plane(inward)).start()

    def zrs_drain(tag, zsend, sub):
        drains.append(lambda: sent(zsend.at[(pl.ds(0, 3), *sub)], zs2.at[tag]))

    def core_sum(tag, mine, crecv, zsend, zrecv, relay, sub, start=True):
        def body(i, carry):
            t = turn(i)
            got(crecv.at[(t, *sub)], cr2.at[tag, t])
            v = mine[(t, *sub)] + crecv[(t, *sub)].astype(F32)
            mine[(t, *sub)] = v
            zsend[(t, *sub)] = v.astype(BF)
            if start:
                zrs_send(tag, t, zsend, zrecv, relay, sub)
            return carry

        lax.fori_loop(0, 4, body, 0)
        zrs_drain(tag, zsend, sub)

    def zrs_start(tag, zsend, zrecv, relay, sub):
        def body(i, carry):
            zrs_send(tag, turn(i), zsend, zrecv, relay, sub)
            return carry

        lax.fori_loop(0, 4, body, 0)

    def zrs_relay(tag, mine, zsend, zrecv, relay, sub):
        @pl.when(inner)
        def _():
            got(relay.at[sub], zr2.at[tag, 1])
            zsend[(far_end, *sub)] = (mine[(far_end, *sub)] + relay[sub].astype(F32)).astype(BF)
            rc(
                zsend.at[(far_end, *sub)], zrecv.at[(z, *sub)], zs2.at[tag], zr2.at[tag, 0], plane(far_end)
            ).start()

    def zrs_end(tag, mine, zrecv, res, sub):
        @pl.when(outer)
        def _():
            got(zrecv.at[(pl.ds(0, 2), *sub)], zr2.at[tag, 0])
            res[sub] = mine[(z, *sub)] + zrecv[(pair, *sub)].astype(F32) + zrecv[(across, *sub)].astype(F32)

        @pl.when(inner)
        def _():
            got(zrecv.at[(pl.ds(0, 3), *sub)], zr2.at[tag, 0])
            res[sub] = (
                mine[(z, *sub)] + zrecv[(pair, *sub)].astype(F32) + zrecv[(across, *sub)].astype(F32)
                + zrecv[(far_end, *sub)].astype(F32)
            )

    every = (pl.ds(0, 128),)
    back = [(pl.ds(0, 128), pl.ds(*part)) for part in GPARTS]

    def back_sum(k):
        core_sum(R_GB + k, mB, crB, zsB, zrB, rlB, back[k], k < 2)

    def back_relay(k):
        zrs_relay(R_GB + k, mB, zsB, zrB, rlB, back[k])

    for k in range(2):
        got(g_size(k), pr.at[T_G + k])
        wgrad_back(k)
        if k == 1:
            back_relay(0)
            pl.when(c == 1)(act_first)
        back_sum(k)
    pl.when(c == 0)(act_first)
    got(g_size(2), pr.at[T_G + 2])
    bwd_act(0)
    bwd_in(0)
    back_relay(1)
    bwd_act(1)
    wgrad(R_GI, N, GPB, mI, csI, crI, 1024)
    bwd_in(1)
    core_sum(R_GI, mI, crI, zsI, zrI, rlI, every)
    wgrad_back(2)

    def norm_one_bwd(h):
        def body(q, carry):
            rr = rows(2 * h + q, 32)
            part = rows(q, 32)
            gn = OWN[rr, :] + RB2[h, 0, part, :].astype(F32) + RB2[h, 1, part, :].astype(F32)
            gn = GS[rr, :] + (gn + RB2[h, 2, part, :].astype(F32))
            xh = XH1[rr, :]
            GV[4:5, :] += jnp.sum(gn * xh, axis=0, keepdims=True)
            GV[5:6, :] += jnp.sum(gn, axis=0, keepdims=True)
            u = gn * VEC[4:5, :]
            gf = RS1[rr, 0:1] * (
                u - jnp.mean(u, axis=-1, keepdims=True) - xh * jnp.mean(u * xh, axis=-1, keepdims=True)
            )
            GV[3:4, :] += jnp.sum(gf, axis=0, keepdims=True)
            GF[rr, :] = gf
            GFB[rr, :] = gf.astype(BF)
            return carry

        lax.fori_loop(0, 2, body, 0)

    got(size(192), pr.at[T_RSB])
    norm_one_bwd(0)
    back_sum(2)
    got(size(192), pr.at[T_RSB2])
    norm_one_bwd(1)

    def gctx(t):
        GCS[t] = dot_nt(GFB[...], WO[t].reshape(256, 1024)).astype(BF)

    me = rows(s, 128)
    for j in (1, 2, 3):
        gctx(rank[j])
        rc(GCS.at[rank[j]], GC.at[me], ps.at[T_GC], pr.at[T_GC], peer(j)).start()
    drains.append(lambda: sent(CTX.at[pl.ds(0, 384)], ps.at[T_GC]))
    gctx(s)
    GC[me, :] = GCS[s]
    GFC[me, :] = GFB[:, rows(s, 256)]
    zrs_relay(R_GI, mI, zsI, zrI, rlI, every)
    got(CTX.at[pl.ds(0, 384)], pr.at[T_GC])

    BQ[...] = jnp.zeros_like(BQ)

    def attend_bwd(n, carry):
        rr = rows(n, 256)
        for two in range(2):
            parts = []
            for i in (2 * two, 2 * two + 1):
                q = MIX[rr, 192 * i : 192 * i + 64]
                k = MIX[rr, 192 * i + 64 : 192 * i + 128]
                v = MIX[rr, 192 * i + 128 : 192 * i + 192]
                gc = GC[rr, 64 * i : 64 * i + 64]
                p = PROB[n, i]
                gp = dot_nt(gc, v)
                inside = jnp.sum(p * gp, axis=-1, keepdims=True)
                gsc = (p * (gp - inside) * factor).astype(BF)
                parts += [dot_nn(gsc, k), dot_tn(gsc, q), dot_tn(p.astype(BF), gc)]
            both = jnp.concatenate([x.astype(BF) for x in parts], axis=1)
            GM[rr, 384 * two : 384 * two + 384] = both
            BQ[0:1, 384 * two : 384 * two + 384] += jnp.sum(both.astype(F32), axis=0, keepdims=True)
        return carry

    lax.fori_loop(0, 1, attend_bwd, 0)
    spread(T_GF, [(j, GFB.at[:, rows(rank[j], 256)], GFC.at[me]) for j in (1, 2, 3)], CTX.at[pl.ds(0, 384)])
    spread_ctx(T_CB, lambda j: [rank[i] for i in (1, 2, 3) if i != j])
    lax.fori_loop(1, 2, attend_bwd, 0)
    for k in range(6):
        GV[k % 3 : k % 3 + 1, rows(2 * s + k // 3, 128)] = BQ[0:1, 128 * k : 128 * k + 128]
    for gg in range(8):
        GVC[gg % 2, gg // 2] = GV[:, 128 * gg : 128 * gg + 128]
    send(GVC.at[1 - c], RVC, cs2.at[R_SV], cr2.at[R_SV, 0], partner)
    wgrad(R_GQ, X, GM, mQ, csQ, crQ, 768)
    got(RVC, cr2.at[R_SV, 0])
    TVZ[...] = GVC[c] + RVC[...]
    for k in (1, 2, 3):
        t = (z + k) % 4
        rc(TVZ.at[t], RVZ.at[k - 1], zs2.at[R_SV], zr2.at[R_SV, 0], plane(t)).start()
    drains.append(lambda: sent(RVZ, zs2.at[R_SV]))
    core_sum(R_GQ, mQ, crQ, zsQ, zrQ, rlQ, every)
    def gtok(rr, j):
        def body(t, carry):
            cols = rows(t, 256)
            part = dot_nt(GM[rr, :], WQ[cols, :])
            if j == 0:
                OWN[:, cols] = part
            else:
                SB3[j - 1, :, cols] = part.astype(BF)
            return carry

        lax.fori_loop(0, 4, body, 0)

    for j in (1, 2, 3):
        gtok(rows(rank[j], 128), j)
        rc(SB3.at[j - 1], RB3.at[j - 1], ps.at[T_GT], pr.at[T_GT], peer(j)).start()
    drains.append(lambda: sent(size(384), ps.at[T_GT]))
    zrs_relay(R_GQ, mQ, zsQ, zrQ, rlQ, every)
    got(CTX.at[pl.ds(0, 384)], pr.at[T_GF])
    got(size(96), pr.at[T_CA])
    got(size(192), pr.at[T_CB])
    wgrad(R_GO, CALL, GFC, mO, csO, crO, 256)
    core_sum(R_GO, mO, crO, zsO, zrO, rlO, every)
    def last_part():
        zrs_start(R_GB3, zsB, zrB, rlB, back[2])

    pl.when(outer)(last_part)
    gtok(me, 0)
    for k in range(2):
        zrs_end(R_GB + k, mB, zrB, GBF, back[k])
    put(GBF.at[:, pl.ds(0, 768)], gb_o.at[:, pl.ds(0, 768)], 1)
    zrs_end(R_GI, mI, zrI, resI, every)
    for j in (1, 2, 3):
        siI[j - 1] = resI[rows(rank[j], 32), :].astype(BF)
    spread(T_GI, [(j, siI.at[j - 1], riI.at[j - 1]) for j in (1, 2, 3)], riI)
    for i in range(8):
        GIF[:, rows(4 * i + s, 128)] = resI[rows(s, 32), 128 * i : 128 * i + 128]
    got(RVZ, zr2.at[R_SV, 0])
    PV[...] = TVZ[z] + RVZ[0] + RVZ[1] + RVZ[2]
    spread(T_SV, [(j, PV, RVP.at[j - 1]) for j in (1, 2, 3)], RVP)
    zrs_relay(R_GO, mO, zsO, zrO, rlO, every)
    pl.when(inner)(last_part)
    got(size(384), pr.at[T_GT])

    def gtok_sum(t, carry):
        rr = rows(t, 32)
        h = OWN[rr, :] + RB3[0, rr, :].astype(F32) + RB3[1, rr, :].astype(F32) + RB3[2, rr, :].astype(F32)
        GTS[rr, :] = GF[rr, :] + h
        return carry

    lax.fori_loop(0, 4, gtok_sum, 0)
    put(GTS, gtok_o, 2)
    zrs_end(R_GQ, mQ, zrQ, resQ, every)
    for j in (1, 2, 3):
        siQ[j - 1] = resQ[rows(rank[j], 32), :].astype(BF)
    spread(T_GQ, [(j, siQ.at[j - 1], riQ.at[j - 1]) for j in (1, 2, 3)], riQ)
    back_relay(2)
    got(riI, pr.at[T_GI])
    for j in (1, 2, 3):
        for i in range(8):
            GIF[:, rows(4 * i + rank[j], 128)] = riI[j - 1, :, 128 * i : 128 * i + 128].astype(F32)
    put(GIF, gi_o, 3)
    zrs_end(R_GO, mO, zrO, resO, every)
    for j in (1, 2, 3):
        siO[j - 1] = resO[rows(rank[j], 32), :].astype(BF)
    spread(T_GO, [(j, siO.at[j - 1], riO.at[j - 1]) for j in (1, 2, 3)], riO)
    zrs_end(R_GB3, mB, zrB, GBF, back[2])
    put(GBF.at[:, pl.ds(768, 256)], gb_o.at[:, pl.ds(768, 256)], 7)
    got(RVP, pr.at[T_SV])
    tot = PV[...] + RVP[0] + RVP[1] + RVP[2]
    row = lax.broadcasted_iota(jnp.int32, (16, 128), 0)
    RVC[0] = jnp.where(row == 9, PV[...], tot)
    put(RVC.at[0], sv_o, 6)
    GQF[:, rows(s, 768)] = resQ[rows(s, 32), :]
    got(riQ, pr.at[T_GQ])
    for j in (1, 2, 3):
        GQF[:, rows(rank[j], 768)] = riQ[j - 1].astype(F32)
    put(GQF, gq_o, 5)
    GOF[:, rows(s, 256)] = resO[rows(s, 32), :]
    got(riO, pr.at[T_GO])
    for j in (1, 2, 3):
        GOF[:, rows(rank[j], 256)] = riO[j - 1].astype(F32)
    put(GOF, go_o, 4)
    for drain in drains:
        drain()


def hand_over(*refs):
    sources, targets, kept, (isem, osem) = refs[:7], refs[7:21], refs[21:36], refs[36:]
    s = lax.axis_index("seq")
    ins = [pltpu.make_async_copy(src, mid, isem.at[k]) for k, (src, mid) in enumerate(zip(sources, kept))]
    held = kept[:6] + kept[7:]
    outs = [pltpu.make_async_copy(mid, dst, osem.at[k]) for k, (mid, dst) in enumerate(zip(held, targets))]
    for k in (6, 0, 1, 2, 3, 4, 5):
        ins[k].start()
    qv, ob, g1, b1, ib, bb, g2, b2 = kept[7:]
    sums = kept[6]
    ins[6].wait()
    turned = pltpu.roll(sums[...], (128 - 32 * s) % 128, 1)
    for k, ref in ((3, ob), (4, g1), (5, b1), (6, bb), (7, g2), (8, b2)):
        ref[...] = turned[k : k + 1, 0:32]
    ib[...] = sums[9:10, :]
    line = jnp.where(s == 0, sums[0:1, :], jnp.where(s == 3, sums[2:3, :], sums[1:2, :]))
    qv[...] = jnp.where(s // 2 == 0, line[:, 0:64], line[:, 64:128])
    for k in range(6, 14):
        outs[k].start()
    for k in range(6):
        ins[k].wait()
        outs[k].start()
    for out in outs:
        out.wait()


def fused_shards(
    tokens, cotangent, slot_lengths, w_qkv, qv_bias, w_out, out_bias, ln1_gain, ln1_bias,
    w_in, in_bias, w_back, back_bias, ln2_gain, ln2_bias,
):
    vm = pltpu.VMEM
    dma = pltpu.SemaphoreType.DMA

    def item(n):
        return [
            vm((4, 128, n), F32), vm((4, 128, n), BF), vm((4, 128, n), BF),
            vm((4, 128, n), BF), vm((4, 128, n), BF), vm((128, n), BF),
        ]

    lengths = (64, 32, 32, 32, 128, 32, 32, 32)
    scratch = [vm((1, n), BF) for n in lengths]
    scratch += [
        vm((16, 128), BF), vm((16, 128), F32), vm((128, 1024), BF), vm((512, 1024), BF), vm((1024, 768), BF), vm((1024, 1024), BF), vm((1024, 1024), BF),
        vm((4, 2, 4, 32, 1024), BF), vm((4, 2, 4, 16, 128), BF), vm((16, 1024), F32), vm((16, 1024), F32),
        vm((8, 768), F32),
        vm((512, 768), BF), vm((2, 4, 256, 256), F32), vm((512, 256), BF), vm((512, 1024), BF),
        vm((128, 1024), F32), vm((128, 1024), F32), vm((128, 128), F32), vm((512, 1024), BF),
        vm((512, 1024), F32), vm((512, 1024), BF), vm((512, 1024), BF), vm((2, 3, 64, 1024), BF),
        vm((128, 1024), F32),
        vm((512, 1024), BF), vm((128, 1024), F32), vm((512, 1024), BF), vm((512, 1024), BF),
        vm((2, 3, 64, 1024), BF), vm((128, 1024), F32), vm((128, 1024), BF), vm((512, 256), BF), vm((4, 128, 256), BF),
        vm((512, 256), BF), vm((512, 768), BF), vm((3, 128, 1024), BF), vm((3, 128, 1024), BF),
        vm((256, 1024), F32),
    ]
    scratch += item(1024) + item(1024) + item(768) + item(256)
    scratch += [
        vm((3, 32, 1024), BF), vm((3, 32, 1024), BF), vm((3, 32, 768), BF), vm((3, 32, 768), BF),
        vm((3, 32, 256), BF), vm((3, 32, 256), BF),
        vm((128, 1024), F32), vm((128, 768), F32), vm((128, 256), F32),
        vm((16, 1024), F32), vm((2, 4, 16, 128), F32), vm((4, 16, 128), F32), vm((4, 16, 128), F32),
        vm((3, 16, 128), F32), vm((16, 128), F32), vm((3, 16, 128), F32),
        vm((128, 1024), BF), vm((128, 1024), F32), vm((32, 3072), F32), vm((32, 1024), F32),
        vm((32, 4096), F32), vm((128, 1024), F32),
        dma((8,)), dma((26,)), dma((26,)), dma((8,)), dma((8, 2)), dma((8,)), dma((8,)),
        dma((7,)), dma((7, 4)), dma((7,)), dma((7, 2)),
    ]
    shapes = [
        ((128, 1024), BF), ((128, 1024), F32), ((32, 3072), F32), ((32, 1024), F32),
        ((32, 4096), F32), ((128, 1024), F32), ((16, 128), F32),
    ]
    hbm = pl.BlockSpec(memory_space=pl.ANY)
    smem = pl.BlockSpec(memory_space=pltpu.SMEM)
    small = [v.reshape(1, -1) for v in (qv_bias, out_bias, ln1_gain, ln1_bias, in_bias, back_bias, ln2_gain, ln2_bias)]
    results = pl.pallas_call(
        layer_kernel,
        out_shape=[jax.ShapeDtypeStruct(a, b) for a, b in shapes],
        in_specs=[hbm] * 6 + [smem] + [hbm] * 8,
        out_specs=[hbm] * 7,
        scratch_shapes=scratch,
        compiler_params=pltpu.CompilerParams(
            collective_id=0, has_side_effects=True, vmem_limit_bytes=67_000_000
        ),
        name="encoder_layer",
    )(tokens, cotangent, w_qkv, w_out, w_in, w_back, slot_lengths, *small)
    final = pl.pallas_call(
        hand_over,
        out_shape=[jax.ShapeDtypeStruct(a, b) for a, b in shapes[:6]]
        + [jax.ShapeDtypeStruct((1, n), F32) for n in lengths],
        in_specs=[hbm] * 7,
        out_specs=[hbm] * 14,
        scratch_shapes=[vm(a, b) for a, b in shapes] + [vm((1, n), F32) for n in lengths] + [dma((7,)), dma((14,))],
        name="hand_over",
    )(*results)
    output, grad_tokens, grad_qkv, grad_wo, grad_wi, grad_wb = final[:6]
    qv, ob, g1, b1, ib, bb, g2, b2 = [v.reshape(-1) for v in final[6:]]
    return (output, grad_tokens, grad_qkv, qv, grad_wo, ob, g1, b1, grad_wi, ib, grad_wb, bb, g2, b2)


def solution(mesh):
    placed = (
        P(("grp", "seq"), None),
        P(("grp", "seq"), None),
        P("grp"),
        P(("grp", "seq"), None),
        P(("grp", "seq")),
        P(("grp", "seq"), None),
        P(("grp", "seq")),
        P(("grp", "seq")),
        P(("grp", "seq")),
        P(("grp", "seq"), None),
        P(("grp", "seq")),
        P(("grp", "seq"), None),
        P(("grp", "seq")),
        P(("grp", "seq")),
        P(("grp", "seq")),
    )
    fused = mesh.shape["grp"] == 2 * PLANES and mesh.shape["seq"] == RANKS
    return jax.shard_map(
        fused_shards if fused else shards,
        mesh=mesh,
        in_specs=placed,
        out_specs=(
            P(("grp", "seq"), None),
            P(("grp", "seq"), None),
            P(("grp", "seq"), None),
            P(("grp", "seq")),
            P(("grp", "seq"), None),
            P(("grp", "seq")),
            P(("grp", "seq")),
            P(("grp", "seq")),
            P(("grp", "seq"), None),
            P(("grp", "seq")),
            P(("grp", "seq"), None),
            P(("grp", "seq")),
            P(("grp", "seq")),
            P(("grp", "seq")),
        ),
        check_vma=False,
    )
```
